128 devices in a mesh: seq: 64 (over y, x_hi, z, core), dp: 2 (over x_lo).
Axes of the slice: x: 4 (x_hi: 2, x_lo: 2; x = x_hi * 2 + x_lo), y: 4, z: 4, core: 2. Of those that a mesh axis runs over, the one named last changes fastest.
Arguments:
- acceptors: bfloat16 [2, 8192, 2560], P('dp', 'seq'), may hold values from -2 to 2
- lookups: bfloat16 [2, 8192, 2560], P('dp', 'seq'), may hold values from -0.3125 to 0.3125
- payloads: bfloat16 [2, 8192, 2560], P('dp', 'seq'), may hold values from -6 to 6
- lagged_fading_source: bfloat16 [2, 8192, 2560], P('dp', 'seq'), may hold values from -6 to 6
- response_cotangent: bfloat16 [2, 8192, 2560], P('dp', 'seq'), may hold values from -2.5 to 2.5
- fading_lowering_array: bfloat16 [2560, 128], replicated, may hold values from -0.125 to 0.125
- fading_raising_array: bfloat16 [2560, 128], replicated, may hold values from -1.25 to 1.25
- feature_fading_speed: float32 [2560], replicated, may hold values from 5.812872e-06 to 0.125
- present_reward: float32 [2560], replicated, may hold values from 2.828427 to 22.627417
Outputs:
- mixed: bfloat16 [2, 8192, 2560], P('dp', 'seq')
- grad_receptance: bfloat16 [2, 8192, 2560], P('dp', 'seq')
- lookup_deriv: bfloat16 [2, 8192, 2560], P('dp', 'seq')
- payload_deriv: bfloat16 [2, 8192, 2560], P('dp', 'seq')
- grad_decay_input: bfloat16 [2, 8192, 2560], P('dp', 'seq')
- grad_lora_a: float32 [2560, 128], P('dp')
- grad_lora_b: float32 [2560, 128], P('dp')
- grad_time_decay: float32 [2560], P('dp')
- present_reward_deriv: float32 [2560], P('dp')
The draws below stay inside these ranges and needn't reach their ends.
All inputs are finite; a program needn't handle non-finite values.
Results may differ from the reference program's by a relative error of at most 0.006.
Values sent between devices are 32-bit elements.
A program may use at most 320 MiB of HBM per device.

```python
import math
import jax
import jax.numpy as jnp
from jax import lax

ATTENDER_TOTAL = 40
LANE_TOTAL = 64
DECAY_RANK = 128
BLOCK = 64
EMBED_SPAN = 2560
SEQLEN = 8192
SEQS = 2


def draw_feature_fading_speed(key, part):
    choose_key, slow_key, fast_key, corner_key = jax.random.split(jax.random.fold_in(key, 7), 4)
    slower = jnp.exp(jax.random.uniform(slow_key, (EMBED_SPAN,), jnp.float32, math.log(0.05), math.log(0.6))) / SEQLEN
    faster = 1.0 / jax.random.uniform(fast_key, (EMBED_SPAN,), jnp.float32, 8.0, 40.0)
    lasting = jax.random.uniform(choose_key, (EMBED_SPAN,), jnp.float32) < 0.5
    rates = jnp.where(lasting, slower, faster)
    return jnp.clip(rates, 0.05 / SEQLEN, 0.125).astype(jnp.float32)


def block_levels(own_key, shape, cuts, low, high):
    def one(dim, parts):
        heights = jax.random.uniform(jax.random.fold_in(jax.random.fold_in(own_key, 6), dim), (parts,), jnp.float32, low / len(cuts), high / len(cuts))
        return jnp.repeat(jnp.exp(heights), shape[dim] // parts).reshape((-1,) + (1,) * (len(shape) - dim - 1))

    factor_of = one(*cuts[0])
    for cut in cuts[1:]:
        factor_of = factor_of * one(*cut)
    return factor_of


def centred(own_key, dims, spread, limit, pieces=(), dtype=jnp.bfloat16):
    array = jax.random.normal(own_key, dims, jnp.float32) * spread
    if len(pieces) > 0:
        array = block_levels(own_key, dims, pieces, -0.22, 0.18) * array
    return jnp.clip(array, min=-limit, max=limit).astype(dtype)


def setup_inputs(seed: int = 0) -> dict:
    key_list = jax.random.split(jax.random.key(seed), 10)
    acceptors = centred(key_list[0], (SEQS, SEQLEN, EMBED_SPAN), (LANE_TOTAL ** -0.5), 2.0, ((0, 2), (1, 64)))
    lookups = centred(key_list[1], (SEQS, SEQLEN, EMBED_SPAN), (2.0 / SEQLEN ** 0.5), 0.3125, ((0, 2), (1, 64)))
    payloads = centred(key_list[2], (SEQS, SEQLEN, EMBED_SPAN), 1.0, 6.0, ((0, 2), (1, 64)))
    lagged_fading_source = centred(key_list[3], (SEQS, SEQLEN, EMBED_SPAN), 1.0, 6.0, ((0, 2), (1, 64)))
    response_cotangent = centred(key_list[4], (SEQS, SEQLEN, EMBED_SPAN), (16.0 / SEQLEN ** 0.5), 2.5, ((0, 2), (1, 64)))
    fading_lowering_array = centred(key_list[5], (EMBED_SPAN, DECAY_RANK), EMBED_SPAN ** -0.5, 0.125)
    fading_raising_array = centred(key_list[6], (EMBED_SPAN, DECAY_RANK), 0.08, 1.25)
    feature_fading_speed = draw_feature_fading_speed(jax.random.fold_in(key_list[9], 71), 0)
    present_reward = jnp.clip(jnp.exp(jax.random.uniform(key_list[8], (EMBED_SPAN,), jnp.float32, math.log(2.828427), math.log(22.627417))), 2.828427, 22.627417)
    return dict(acceptors=acceptors, lookups=lookups, payloads=payloads, lagged_fading_source=lagged_fading_source, response_cotangent=response_cotangent, fading_lowering_array=fading_lowering_array, fading_raising_array=fading_raising_array, feature_fading_speed=feature_fading_speed, present_reward=present_reward)


HIGH = lax.Precision.HIGHEST


def contract(pattern, left, right):
    return jnp.einsum(pattern, left, right, precision=HIGH, preferred_element_type=jnp.float32)


def decay_log_values(input_rows, fading_lowering_array, fading_raising_array, feature_fading_speed):
    apply_projection = jnp.dot(input_rows, fading_lowering_array, preferred_element_type=jnp.float32)
    smoothed_values = jnp.tanh(apply_projection)
    gate_portion = smoothed_values.astype(jnp.bfloat16)
    rank_projection = lax.dot_general(gate_portion, fading_raising_array, (((1,), (1,)), ((), ())), preferred_element_type=jnp.float32)
    return smoothed_values, gate_portion, -feature_fading_speed[None, :] * jnp.exp(rank_projection)


def compose(decays, own_states, backward):
    def advance(carry, member):
        run_decay, run_state = carry
        decay, own_state = member
        return (run_decay * decay, decay[..., None] * run_state + own_state), carry

    initial = (jnp.ones(decays.shape[1:], jnp.float32), jnp.zeros(own_states.shape[1:], jnp.float32))
    return lax.scan(advance, initial, (decays, own_states), reverse=backward)


def temporal_blend_sublevel(acceptor_lines, lookups, payloads, incoming_cotangent, fading_exponent, reward_by_attender, adjacent_shardlink):
    inclusive = jnp.cumsum(fading_exponent, axis=1)
    exclusive = inclusive - fading_exponent
    middle = inclusive[:, BLOCK // 2 - 1:BLOCK // 2]
    overall = inclusive[:, -1]
    entering = jnp.exp(exclusive)
    leaving = jnp.exp(overall[:, None] - inclusive)
    upward = jnp.exp(exclusive - middle)
    downward = jnp.exp(middle - inclusive)
    decays = jnp.exp(overall)
    reached = acceptor_lines * entering
    faded_keys = lookups * leaving
    own_states = contract("nchk,nchv->nhkv", faded_keys, payloads)
    pull_states = contract("nchk,nchv->nhkv", reached, incoming_cotangent)
    starts, block_ends = adjacent_shardlink(decays, own_states, pull_states)
    position = jnp.arange(BLOCK)
    beneath = position[:, None] > position[None, :]
    early_recept = acceptor_lines * upward
    late_keys = lookups * downward
    scores = jnp.where(beneath, contract("nthk,nshk->nhts", early_recept, late_keys), 0.0)
    present_contribution = jnp.sum(acceptor_lines * reward_by_attender * lookups, axis=-1)[..., None]
    blended_response = contract("nhts,nshv->nthv", scores, payloads) + present_contribution * payloads + contract("nthk,nhkv->nthv", reached, starts)
    grad_start = decays[..., None] * block_ends + pull_states
    products = jnp.where(beneath, contract("nthv,nshv->nhts", incoming_cotangent, payloads), 0.0)
    agreement_verify = jnp.sum(payloads * incoming_cotangent, axis=-1)[..., None]
    memory_acceptors = entering * contract("nhkv,nthv->nthk", starts, incoming_cotangent) + upward * contract("nhts,nshk->nthk", products, late_keys)
    memory_lookup_lines = leaving * contract("nhkv,nthv->nthk", block_ends, payloads) + downward * contract("nhst,nshk->nthk", products, early_recept)
    payload_deriv = contract("nthk,nhkv->nthv", faded_keys, block_ends) + contract("nhst,nshv->nthv", scores, incoming_cotangent) + present_contribution * incoming_cotangent
    acceptor_deriv = memory_acceptors + reward_by_attender * lookups * agreement_verify
    lookup_deriv = memory_lookup_lines + reward_by_attender * acceptor_lines * agreement_verify
    present_reward_deriv = jnp.sum(acceptor_lines * lookups * agreement_verify, axis=(0, 1))
    coupling = jnp.sum(grad_start * starts, axis=-1)
    change = lookups * memory_lookup_lines - acceptor_lines * memory_acceptors
    fading_deriv = coupling[:, None] + jnp.cumsum(change, axis=1) - change - acceptor_lines * memory_acceptors
    return blended_response, acceptor_deriv, lookup_deriv, payload_deriv, fading_deriv, present_reward_deriv


def sublevel_evaluation(reshaped_acceptors, reshaped_lookups, reshaped_payloads, reshaped_source, incoming_cotangent_reshaped, fading_lowering_array, fading_raising_array, feature_fading_speed, present_reward, adjacent_shardlink):
    smoothed_values, gate_portion, fading_exponent = decay_log_values(reshaped_source, fading_lowering_array, fading_raising_array, feature_fading_speed)
    tokens, feature_span = reshaped_acceptors.shape
    tiling_arrangement = (tokens // BLOCK, BLOCK, ATTENDER_TOTAL, LANE_TOTAL)
    collected_outcomes = temporal_blend_sublevel(reshaped_acceptors.astype(jnp.float32).reshape(tiling_arrangement),
                       reshaped_lookups.astype(jnp.float32).reshape(tiling_arrangement),
                       reshaped_payloads.astype(jnp.float32).reshape(tiling_arrangement),
                       incoming_cotangent_reshaped.astype(jnp.float32).reshape(tiling_arrangement),
                       fading_exponent.reshape(tiling_arrangement), present_reward.reshape(ATTENDER_TOTAL, LANE_TOTAL), adjacent_shardlink)
    blended_response, acceptor_deriv, lookup_deriv, payload_deriv, fading_deriv, present_reward_deriv = collected_outcomes
    slope = fading_deriv.reshape(tokens, feature_span) * fading_exponent
    slope_portion = slope.astype(jnp.bfloat16)
    gate_gradient = jnp.dot(slope_portion, fading_raising_array, preferred_element_type=jnp.float32)
    projection_gradient = (gate_gradient * (1.0 - smoothed_values * smoothed_values)).astype(jnp.bfloat16)
    input_gradient = lax.dot_general(projection_gradient, fading_lowering_array, (((1,), (1,)), ((), ())), preferred_element_type=jnp.float32).astype(jnp.bfloat16)
    lowering_array_deriv = lax.dot_general(reshaped_source, projection_gradient, (((0,), (0,)), ((), ())), preferred_element_type=jnp.float32)
    raising_array_deriv = lax.dot_general(slope_portion, gate_portion, (((0,), (0,)), ((), ())), preferred_element_type=jnp.float32)
    speed_deriv = jnp.sum(slope, axis=0)

    def flatten(member):
        return member.reshape(tokens, feature_span).astype(jnp.bfloat16)

    return (flatten(blended_response), flatten(acceptor_deriv), flatten(lookup_deriv), flatten(payload_deriv), input_gradient,
            (lowering_array_deriv, raising_array_deriv, speed_deriv, present_reward_deriv.reshape(feature_span)))


def sharded_ownlink(decays, own_states, pull_states):
    ahead_total, ahead = compose(decays, own_states, False)
    behind_total, behind = compose(decays, pull_states, True)
    return ahead[1], behind[1]


def reference(acceptors, lookups, payloads, lagged_fading_source, response_cotangent, fading_lowering_array, fading_raising_array, feature_fading_speed, present_reward):
    collected = []
    for symbol_stream in range(acceptors.shape[0]):
        collected.append(sublevel_evaluation(acceptors[symbol_stream], lookups[symbol_stream], payloads[symbol_stream], lagged_fading_source[symbol_stream],
                                    response_cotangent[symbol_stream], fading_lowering_array, fading_raising_array, feature_fading_speed, present_reward, sharded_ownlink))
    stacked = [jnp.stack([member[index] for member in collected]) for index in range(5)]
    summed = [jnp.sum(jnp.stack([member[5][index] for member in collected]), axis=0) for index in range(4)]
    return (stacked[0], stacked[1], stacked[2], stacked[3], stacked[4], summed[0], summed[1], summed[2], summed[3])
```

```python
import functools

import jax
import jax.numpy as jnp
from jax import lax
from jax.experimental import pallas as pl
from jax.experimental.pallas import tpu as pltpu
from jax.sharding import PartitionSpec as P

F32 = jnp.float32
BF16 = jnp.bfloat16
TOK = 128
HALF = 64
GROUPS = 4
PAIRS = 5
WIDTH = PAIRS * 128
CHIPS = 32
NN = (((1,), (0,)), ((), ()))
NT = (((1,), (1,)), ((), ()))
TN = (((0,), (0,)), ((), ()))


def dot(a, b, dims):
    return lax.dot_general(a, b, dims, preferred_element_type=F32)


def split(x, parts):
    pieces = []
    for _ in range(parts - 1):
        head = x.astype(BF16)
        pieces.append(head)
        x = x - head.astype(F32)
    pieces.append(x.astype(BF16))
    return pieces


def summed_by(matrix, x, parts):
    total = None
    for piece in split(x, parts):
        term = dot(matrix, piece, NN)
        total = term if total is None else total + term
    return total


def grids():
    row = lax.broadcasted_iota(jnp.int32, (TOK, TOK), 0)
    col = lax.broadcasted_iota(jnp.int32, (TOK, TOK), 1)
    same = (row < HALF) == (col < HALF)
    return row, col, same


def as_matrix(condition):
    return jnp.where(condition, 1.0, 0.0).astype(BF16)


def decay_sums(gate, raising, speed, lower):
    rank = dot(gate, raising, NT)
    log_decay = -speed * jnp.exp(rank)
    inclusive = summed_by(lower, log_decay, 3)
    return (
        log_decay,
        inclusive,
        inclusive - log_decay,
        inclusive[HALF - 1 : HALF],
        inclusive[TOK - 1 : TOK],
    )


def packed(product, left):
    return jnp.where(left[:HALF], product[:HALF], product[HALF:])


def spread(state, left):
    low = state.astype(BF16)
    zero = jnp.zeros_like(low)
    return jnp.concatenate(
        [jnp.where(left[:HALF], low, zero), jnp.where(left[:HALF], zero, low)], axis=0
    )


def first_kernel(
    x_ref, a_ref, r_ref, k_ref, v_ref, g_ref, b_ref, speed_ref,
    state_ref, decay_ref, smooth_ref, gate_ref,
):
    @pl.when(pl.program_id(0) == 0)
    def _():
        smooth = jnp.tanh(dot(x_ref[...], a_ref[...], NN))
        smooth_ref[...] = smooth
        gate_ref[...] = smooth.astype(BF16)

    row, col, same = grids()
    lower = as_matrix(same & (row >= col))
    left = col < HALF
    early = row < HALF
    gate = gate_ref[...]
    for pair in range(PAIRS):
        at = pl.ds(pair * 128, 128)
        _, inclusive, exclusive, total0, total1 = decay_sums(
            gate, b_ref[at, :], speed_ref[:, at], lower
        )
        to_end = jnp.exp(jnp.where(early, total0 + total1, total1) - inclusive)
        from_start = jnp.exp(jnp.where(early, exclusive, exclusive + total0))
        keys = (k_ref[:, at].astype(F32) * to_end).astype(BF16)
        reads = (r_ref[:, at].astype(F32) * from_start).astype(BF16)
        own = packed(dot(v_ref[:, at], keys, TN), left)
        pull = packed(dot(g_ref[:, at], reads, TN), left)
        rows = slice(pair * 8, pair * 8 + 8)
        state_ref[0, :, rows, :] = own.reshape(8, 8, 128)
        state_ref[1, :, rows, :] = pull.reshape(8, 8, 128)
        decay_ref[0, pair : pair + 1, :] = jnp.exp(total0 + total1)
    decay_ref[0, PAIRS:, :] = jnp.zeros((8 - PAIRS, 128), F32)


def first_stage(x, a, r, k, v, g, b, speed):
    tokens = pl.BlockSpec((TOK, WIDTH), lambda i: (0, i))
    whole = lambda shape: pl.BlockSpec(shape, lambda i: (0,) * len(shape))
    channels = x.shape[1]
    return pl.pallas_call(
        first_kernel,
        grid=(GROUPS,),
        in_specs=[
            whole((TOK, channels)),
            whole((channels, 128)),
            tokens,
            tokens,
            tokens,
            tokens,
            pl.BlockSpec((WIDTH, 128), lambda i: (i, 0)),
            pl.BlockSpec((1, WIDTH), lambda i: (0, i)),
        ],
        out_specs=[
            pl.BlockSpec((2, 8, 40, 128), lambda i: (0, i, 0, 0)),
            pl.BlockSpec((1, 8, 128), lambda i: (i, 0, 0)),
            whole((TOK, 128)),
            whole((TOK, 128)),
        ],
        out_shape=[
            jax.ShapeDtypeStruct((2, 32, 40, 128), F32),
            jax.ShapeDtypeStruct((GROUPS, 8, 128), F32),
            jax.ShapeDtypeStruct((TOK, 128), F32),
            jax.ShapeDtypeStruct((TOK, 128), BF16),
        ],
        name="first_stage",
    )(x, a, r, k, v, g, b, speed)


def second_kernel(
    x_ref, a_ref, r_ref, k_ref, v_ref, g_ref, b_ref, speed_ref, reward_ref,
    smooth_ref, gate_ref, state_ref,
    mixed_ref, dr_ref, dk_ref, dv_ref, dx_ref, sums_ref,
    slope_ref, acc_ref,
):
    group = pl.program_id(0)
    row, col, same = grids()
    lower = as_matrix(same & (row >= col))
    ones = as_matrix((row < HALF) == (col < HALF))
    left = col < HALF
    early = row < HALF
    wide_row = lax.broadcasted_iota(jnp.int32, (TOK, 2 * TOK), 0)
    wide_col = lax.broadcasted_iota(jnp.int32, (TOK, 2 * TOK), 1) % TOK
    wide_same = (wide_row < HALF) == (wide_col < HALF)
    beneath = wide_same & (wide_row > wide_col)
    above = wide_same & (wide_row < wide_col)
    around = jnp.where(
        same & ~early & (col < row), 1.0, jnp.where(same & early & (col >= row), -1.0, 0.0)
    ).astype(BF16)

    @pl.when(group == 0)
    def _():
        acc_ref[...] = jnp.zeros_like(acc_ref)
        sums_ref[:, :, 40:, :] = jnp.zeros((2, 64, 8, 128), F32)

    gate = gate_ref[...]

    def by_head(x):
        zero = jnp.zeros_like(x)
        return jnp.concatenate([jnp.where(left, x, zero), jnp.where(left, zero, x)], axis=0)

    for pair in range(PAIRS):
        at = pl.ds(pair * 128, 128)
        log_decay, inclusive, exclusive, total0, total1 = decay_sums(
            gate, b_ref[at, :], speed_ref[:, at], lower
        )
        middle = jnp.where(
            early, inclusive[HALF // 2 - 1 : HALF // 2], inclusive[HALF + HALF // 2 - 1 : HALF + HALF // 2]
        )
        entering = jnp.exp(exclusive)
        leaving = jnp.exp(jnp.where(early, total0, total1) - inclusive)
        upward = jnp.exp(exclusive - middle)
        downward = jnp.exp(middle - inclusive)
        r16, k16, v16, g16 = r_ref[:, at], k_ref[:, at], v_ref[:, at], g_ref[:, at]
        r, k, v, g = (t.astype(F32) for t in (r16, k16, v16, g16))
        reward = reward_ref[:, at]
        reached = (r * entering).astype(BF16)
        faded = (k * leaving).astype(BF16)
        up = (r * upward).astype(BF16)
        down = (k * downward).astype(BF16)
        v2, g2, up2, down2 = by_head(v16), by_head(g16), by_head(up), by_head(down)

        rows = slice(pair * 8, pair * 8 + 8)
        start0 = state_ref[0, :, rows, :].reshape(HALF, 128)
        end1 = state_ref[1, :, rows, :].reshape(HALF, 128)
        own0 = packed(dot(v16[:HALF], faded[:HALF], TN), left)
        pull1 = packed(dot(g16[HALF:], reached[HALF:], TN), left)
        start1 = jnp.exp(total0) * start0 + own0
        end0 = jnp.exp(total1) * end1 + pull1
        coupling = jnp.where(
            early,
            jnp.sum(end0.astype(BF16).astype(F32) * start1, axis=0, keepdims=True),
            jnp.sum(end0 * start1.astype(BF16).astype(F32), axis=0, keepdims=True),
        )
        s0, s1, e0, e1 = (spread(t, left) for t in (start0, start1, end0, end1))

        def both(lhs, first, last, dims):
            return jnp.concatenate(
                [dot(lhs[:HALF], first, dims), dot(lhs[HALF:], last, dims)], axis=0
            )

        zero = jnp.zeros((), F32)
        scores = jnp.where(beneath, dot(up, down2, NT), zero).astype(BF16)
        scores_t = jnp.where(above, dot(down, up2, NT), zero).astype(BF16)
        products = jnp.where(beneath, dot(g16, v2, NT), zero).astype(BF16)
        products_t = jnp.where(above, dot(v16, g2, NT), zero).astype(BF16)

        present = None
        for piece in split(r * reward * k, 2):
            term = dot(piece, ones, NN)
            present = term if present is None else present + term
        agreement = None
        for piece in split(v * g, 2):
            term = dot(piece, ones, NN)
            agreement = term if agreement is None else agreement + term

        mixed_ref[:, at] = (
            dot(scores, v2, NN) + present * v + both(reached, s0, s1, NT)
        ).astype(BF16)
        dv_ref[:, at] = (
            both(faded, e0, e1, NT) + dot(scores_t, g2, NN) + present * g
        ).astype(BF16)
        past = both(g16, s0, s1, NN)
        near_past = dot(products, down2, NN)
        later = both(v16, e0, e1, NN)
        near_later = dot(products_t, up2, NN)
        dr_ref[:, at] = (
            entering * past + upward * near_past + reward * k * agreement
        ).astype(BF16)
        dk_ref[:, at] = (
            leaving * later + downward * near_later + reward * r * agreement
        ).astype(BF16)
        read = reached.astype(F32) * past + up.astype(F32) * near_past
        change = faded.astype(F32) * later + down.astype(F32) * near_later - read
        slope = (coupling + summed_by(around, change, 2) - read) * log_decay
        slope16 = slope.astype(BF16)
        slope_ref[:, at] = slope16
        chunk = 32 * (group // 2) + PAIRS * (group % 2) + pair
        sums_ref[0, chunk, 40:41, :] = jnp.sum(slope, axis=0, keepdims=True)
        sums_ref[1, chunk, 40:41, :] = jnp.sum(r * k * agreement, axis=0, keepdims=True)

    slopes = slope_ref[...]
    acc_ref[...] += dot(slopes, b_ref[...], NN)
    sums_ref[1, pl.ds(group * 16, 16), :40, :] = dot(slopes, gate, TN).reshape(16, 40, 128)

    @pl.when(group == GROUPS - 1)
    def _():
        smooth = smooth_ref[...]
        project = (acc_ref[...] * (1.0 - smooth * smooth)).astype(BF16)
        for i in range(GROUPS):
            at = pl.ds(i * WIDTH, WIDTH)
            dx_ref[:, at] = dot(project, a_ref[at, :], NT).astype(BF16)
            sums_ref[0, i * 16 : i * 16 + 16, :40, :] = dot(x_ref[:, at], project, TN).reshape(
                16, 40, 128
            )


def second_stage(x, a, r, k, v, g, b, speed, reward, smooth, gate, states):
    tokens = pl.BlockSpec((TOK, WIDTH), lambda i: (0, i))
    whole = lambda shape: pl.BlockSpec(shape, lambda i: (0,) * len(shape))
    channels = x.shape[1]
    full = jax.ShapeDtypeStruct((TOK, channels), BF16)
    return pl.pallas_call(
        second_kernel,
        grid=(GROUPS,),
        in_specs=[
            whole((TOK, channels)),
            whole((channels, 128)),
            tokens,
            tokens,
            tokens,
            tokens,
            pl.BlockSpec((WIDTH, 128), lambda i: (i, 0)),
            pl.BlockSpec((1, WIDTH), lambda i: (0, i)),
            pl.BlockSpec((1, WIDTH), lambda i: (0, i)),
            whole((TOK, 128)),
            whole((TOK, 128)),
            pl.BlockSpec((2, 8, 40, 128), lambda i: (0, i, 0, 0)),
        ],
        out_specs=[
            tokens,
            tokens,
            tokens,
            tokens,
            whole((TOK, channels)),
            whole((2, 64, 48, 128)),
        ],
        out_shape=[full] * 5 + [jax.ShapeDtypeStruct((2, 64, 48, 128), F32)],
        scratch_shapes=[pltpu.VMEM((TOK, WIDTH), BF16), pltpu.VMEM((TOK, 128), F32)],
        name="second_stage",
    )(x, a, r, k, v, g, b, speed, reward, smooth, gate, states)


def place():
    seq = lax.axis_index("seq")
    return seq // 2, seq % 2


def scan_kernel(
    z_ref, d_ref, o_ref,
    x_ref, dx_ref, dc_ref, t_ref, r_ref, q_ref, p_ref, y_ref,
    swap_send, swap_recv, out_send, out_recv, back_send, back_recv, end_send, end_recv,
):
    chip, core = place()
    other = 1 - core
    partner = {"seq": chip * 2 + other}

    def peer(m):
        return {"seq": m * 2 + core}

    def turn(o):
        return lax.rem(chip + o, CHIPS)

    barrier = pltpu.get_barrier_semaphore()
    pl.semaphore_signal(barrier, inc=1, device_id=partner)

    @pl.loop(1, CHIPS)
    def _(o):
        pl.semaphore_signal(barrier, inc=1, device_id=peer(turn(o)))

    pl.semaphore_wait(barrier, CHIPS)

    swap = pltpu.make_async_remote_copy(
        z_ref.at[other], x_ref, swap_send.at[0], swap_recv.at[0], device_id=partner
    )
    swap_decay = pltpu.make_async_remote_copy(
        d_ref, dx_ref, swap_send.at[1], swap_recv.at[1], device_id=partner
    )
    swap_decay.start()
    swap.start()
    swap_decay.wait_recv()
    dc_ref[...] = d_ref[...] * dx_ref[...]
    swap.wait_recv()

    def out_copy(m, slot):
        return pltpu.make_async_remote_copy(
            t_ref.at[m], r_ref.at[slot], out_send.at[m], out_recv.at[slot], device_id=peer(m)
        )

    def back_copy(n, slot):
        return pltpu.make_async_remote_copy(
            q_ref.at[n], p_ref.at[slot], back_send.at[n], back_recv.at[slot], device_id=peer(n)
        )

    def end_copy(m):
        return pltpu.make_async_remote_copy(
            y_ref.at[m], o_ref.at[core, m], end_send.at[m], end_recv.at[m], device_id=partner
        )

    def end_wait(m):
        pltpu.make_async_remote_copy(
            y_ref.at[m], o_ref.at[other, m], end_send.at[m], end_recv.at[m], device_id=partner
        ).wait_recv()

    def chip_total(m, target):
        group = m // 8
        for j in range(PAIRS):
            rows = slice(8 * j, 8 * j + 8)
            target[rows, :] = dx_ref[group, j : j + 1, :] * z_ref[core, m, rows, :] + x_ref[m, rows, :]
        target[40:48, :] = dc_ref[group]

    chip_total(chip, r_ref.at[chip])

    @pl.loop(1, CHIPS)
    def _(o):
        m = turn(o)
        chip_total(m, t_ref.at[m])
        out_copy(m, chip).start()

    def step(i, carry):
        n = core * (CHIPS - 1) + (1 - 2 * core) * i

        @pl.when(n != chip)
        def _():
            out_copy(n, n).wait_recv()

        after = []
        for j in range(PAIRS):
            rows = slice(8 * j, 8 * j + 8)
            q_ref[n, rows, :] = carry[j]
            after.append(r_ref[n, 40 + j : 41 + j, :] * carry[j] + r_ref[n, rows, :])

        @pl.when(n != chip)
        def _():
            back_copy(n, chip).start()

        return tuple(after)

    lax.fori_loop(0, CHIPS, step, tuple(jnp.zeros((8, 128), F32) for _ in range(PAIRS)))

    def finish(m, source):
        group = m // 8
        o_ref[core, m] = source[...]
        for j in range(PAIRS):
            rows = slice(8 * j, 8 * j + 8)
            y_ref[m, rows, :] = d_ref[group, j : j + 1, :] * source[rows, :] + z_ref[core, m, rows, :]
        end_copy(m).start()

    finish(chip, q_ref.at[chip])

    @pl.loop(1, CHIPS)
    def _(o):
        m = turn(o)
        back_copy(m, m).wait_recv()
        finish(m, p_ref.at[m])

    end_wait(chip)
    swap.wait_send()
    swap_decay.wait_send()
    end_copy(chip).wait_send()

    @pl.loop(1, CHIPS)
    def _(o):
        m = turn(o)
        end_wait(m)
        out_copy(m, chip).wait_send()
        back_copy(m, chip).wait_send()
        end_copy(m).wait_send()


def scan_stage(states, decays):
    vmem = pl.BlockSpec(memory_space=pltpu.VMEM)
    state = pltpu.VMEM((32, 40, 128), F32)
    message = pltpu.VMEM((32, 48, 128), F32)
    decay = pltpu.VMEM((GROUPS, 8, 128), F32)
    sems = pltpu.SemaphoreType.DMA
    return pl.pallas_call(
        scan_kernel,
        in_specs=[vmem, vmem],
        out_specs=vmem,
        out_shape=jax.ShapeDtypeStruct((2, 32, 40, 128), F32),
        scratch_shapes=[state, decay, decay, message, message, state, state, state]
        + [sems((2,)), sems((2,))]
        + [sems((CHIPS,))] * 6,
        compiler_params=pltpu.CompilerParams(collective_id=0, has_side_effects=True),
        name="scan_stage",
    )(states, decays)


def reduce_stage(sums):
    whole = lax.psum(sums, ("seq", "dp"))
    return lax.dynamic_slice_in_dim(whole, lax.axis_index("dp") * 32, 32, 1)


def per_device(scan, reduce, r, k, v, x, g, lowering, raising, speed, reward):
    r, k, v, x, g = (t[0] for t in (r, k, v, x, g))
    speed, reward = speed[None], reward[None]
    states, decays, smooth, gate = first_stage(x, lowering, r, k, v, g, raising, speed)
    entering = scan(states, decays)
    mixed, dr, dk, dv, dx, sums = second_stage(
        x, lowering, r, k, v, g, raising, speed, reward, smooth, gate, entering
    )
    share = reduce(sums)
    return (
        mixed[None],
        dr[None],
        dk[None],
        dv[None],
        dx[None],
        share[0, :, :40].reshape(1280, 128),
        share[1, :, :40].reshape(1280, 128),
        share[0, :10, 40].reshape(1280),
        share[1, :10, 40].reshape(1280),
    )


def build(mesh, scan, reduce):
    tokens = P("dp", "seq", None)
    return jax.shard_map(
        functools.partial(per_device, scan, reduce),
        mesh=mesh,
        in_specs=(tokens,) * 5 + (P(),) * 4,
        out_specs=(tokens,) * 5 + (P("dp", None),) * 2 + (P("dp"),) * 2,
        check_vma=False,
    )


def solution(mesh):
    return build(mesh, scan_stage, reduce_stage)
```

```python
import functools

import jax
import jax.numpy as jnp
from jax import lax
from jax.experimental import pallas as pl
from jax.experimental.pallas import tpu as pltpu
from jax.sharding import PartitionSpec as P

F32 = jnp.float32
BF16 = jnp.bfloat16
TOK = 128
HALF = 64
GROUPS = 4
PAIRS = 5
WIDTH = PAIRS * 128
CHIPS = 32
CHUNKS = 2 * CHIPS
PARTS = 8
PART = CHUNKS // PARTS
NN = (((1,), (0,)), ((), ()))
NT = (((1,), (1,)), ((), ()))
TN = (((0,), (0,)), ((), ()))


def dot(a, b, dims):
    return lax.dot_general(a, b, dims, preferred_element_type=F32)


def split(x, parts):
    pieces = []
    for _ in range(parts - 1):
        head = x.astype(BF16)
        pieces.append(head)
        x = x - head.astype(F32)
    pieces.append(x.astype(BF16))
    return pieces


def summed_by(matrix, x, parts):
    total = None
    for piece in split(x, parts):
        term = dot(matrix, piece, NN)
        total = term if total is None else total + term
    return total


def grids():
    row = lax.broadcasted_iota(jnp.int32, (TOK, TOK), 0)
    col = lax.broadcasted_iota(jnp.int32, (TOK, TOK), 1)
    same = (row < HALF) == (col < HALF)
    return row, col, same


def as_matrix(condition):
    return jnp.where(condition, 1.0, 0.0).astype(BF16)


def decay_sums(gate, raising, speed, lower):
    rank = dot(gate, raising, NT)
    log_decay = -speed * jnp.exp(rank)
    inclusive = summed_by(lower, log_decay, 3)
    return (
        log_decay,
        inclusive,
        inclusive - log_decay,
        inclusive[HALF - 1 : HALF],
        inclusive[TOK - 1 : TOK],
    )


def packed(product, left):
    return jnp.where(left[:HALF], product[:HALF], product[HALF:])


def spread(state, left):
    low = state.astype(BF16)
    zero = jnp.zeros_like(low)
    return jnp.concatenate(
        [jnp.where(left[:HALF], low, zero), jnp.where(left[:HALF], zero, low)], axis=0
    )


def first_kernel(
    x_ref, a_ref, r_ref, k_ref, v_ref, g_ref, b_ref, speed_ref,
    state_ref, decay_ref, smooth_ref, gate_ref,
):
    @pl.when(pl.program_id(0) == 0)
    def _():
        smooth = jnp.tanh(dot(x_ref[...], a_ref[...], NN))
        smooth_ref[...] = smooth
        gate_ref[...] = smooth.astype(BF16)

    row, col, same = grids()
    lower = as_matrix(same & (row >= col))
    left = col < HALF
    early = row < HALF
    gate = gate_ref[...]
    for pair in range(PAIRS):
        at = pl.ds(pair * 128, 128)
        _, inclusive, exclusive, total0, total1 = decay_sums(
            gate, b_ref[at, :], speed_ref[:, at], lower
        )
        to_end = jnp.exp(jnp.where(early, total0 + total1, total1) - inclusive)
        from_start = jnp.exp(jnp.where(early, exclusive, exclusive + total0))
        keys = (k_ref[:, at].astype(F32) * to_end).astype(BF16)
        reads = (r_ref[:, at].astype(F32) * from_start).astype(BF16)
        own = packed(dot(v_ref[:, at], keys, TN), left)
        pull = packed(dot(g_ref[:, at], reads, TN), left)
        rows = slice(pair * 8, pair * 8 + 8)
        state_ref[0, :, rows, :] = own.reshape(8, 8, 128)
        state_ref[1, :, rows, :] = pull.reshape(8, 8, 128)
        decay_ref[0, pair : pair + 1, :] = jnp.exp(total0 + total1)
    decay_ref[0, PAIRS:, :] = jnp.zeros((8 - PAIRS, 128), F32)


def first_stage(x, a, r, k, v, g, b, speed):
    tokens = pl.BlockSpec((TOK, WIDTH), lambda i: (0, i))
    whole = lambda shape: pl.BlockSpec(shape, lambda i: (0,) * len(shape))
    channels = x.shape[1]
    return pl.pallas_call(
        first_kernel,
        grid=(GROUPS,),
        in_specs=[
            whole((TOK, channels)),
            whole((channels, 128)),
            tokens,
            tokens,
            tokens,
            tokens,
            pl.BlockSpec((WIDTH, 128), lambda i: (i, 0)),
            pl.BlockSpec((1, WIDTH), lambda i: (0, i)),
        ],
        out_specs=[
            pl.BlockSpec((2, 8, 40, 128), lambda i: (0, i, 0, 0)),
            pl.BlockSpec((1, 8, 128), lambda i: (i, 0, 0)),
            whole((TOK, 128)),
            whole((TOK, 128)),
        ],
        out_shape=[
            jax.ShapeDtypeStruct((2, 32, 40, 128), F32),
            jax.ShapeDtypeStruct((GROUPS, 8, 128), F32),
            jax.ShapeDtypeStruct((TOK, 128), F32),
            jax.ShapeDtypeStruct((TOK, 128), BF16),
        ],
        name="first_stage",
    )(x, a, r, k, v, g, b, speed)


def second_kernel(
    x_ref, a_ref, r_ref, k_ref, v_ref, g_ref, b_ref, speed_ref, reward_ref,
    smooth_ref, gate_ref, state_ref,
    mixed_ref, dr_ref, dk_ref, dv_ref, dx_ref, sums_ref,
    slope_ref, acc_ref,
):
    group = pl.program_id(0)
    row, col, same = grids()
    lower = as_matrix(same & (row >= col))
    ones = as_matrix((row < HALF) == (col < HALF))
    left = col < HALF
    early = row < HALF
    wide_row = lax.broadcasted_iota(jnp.int32, (TOK, 2 * TOK), 0)
    wide_col = lax.broadcasted_iota(jnp.int32, (TOK, 2 * TOK), 1) % TOK
    wide_same = (wide_row < HALF) == (wide_col < HALF)
    beneath = wide_same & (wide_row > wide_col)
    above = wide_same & (wide_row < wide_col)
    around = jnp.where(
        same & ~early & (col < row), 1.0, jnp.where(same & early & (col >= row), -1.0, 0.0)
    ).astype(BF16)

    @pl.when(group == 0)
    def _():
        acc_ref[...] = jnp.zeros_like(acc_ref)
        sums_ref[:, :, 40:, :] = jnp.zeros((2, 64, 8, 128), F32)

    gate = gate_ref[...]

    def by_head(x):
        zero = jnp.zeros_like(x)
        return jnp.concatenate([jnp.where(left, x, zero), jnp.where(left, zero, x)], axis=0)

    for pair in range(PAIRS):
        at = pl.ds(pair * 128, 128)
        log_decay, inclusive, exclusive, total0, total1 = decay_sums(
            gate, b_ref[at, :], speed_ref[:, at], lower
        )
        middle = jnp.where(
            early, inclusive[HALF // 2 - 1 : HALF // 2], inclusive[HALF + HALF // 2 - 1 : HALF + HALF // 2]
        )
        entering = jnp.exp(exclusive)
        leaving = jnp.exp(jnp.where(early, total0, total1) - inclusive)
        upward = jnp.exp(exclusive - middle)
        downward = jnp.exp(middle - inclusive)
        r16, k16, v16, g16 = r_ref[:, at], k_ref[:, at], v_ref[:, at], g_ref[:, at]
        r, k, v, g = (t.astype(F32) for t in (r16, k16, v16, g16))
        reward = reward_ref[:, at]
        reached = (r * entering).astype(BF16)
        faded = (k * leaving).astype(BF16)
        up = (r * upward).astype(BF16)
        down = (k * downward).astype(BF16)
        v2, g2, up2, down2 = by_head(v16), by_head(g16), by_head(up), by_head(down)

        rows = slice(pair * 8, pair * 8 + 8)
        start0 = state_ref[0, :, rows, :].reshape(HALF, 128)
        end1 = state_ref[1, :, rows, :].reshape(HALF, 128)
        own0 = packed(dot(v16[:HALF], faded[:HALF], TN), left)
        pull1 = packed(dot(g16[HALF:], reached[HALF:], TN), left)
        start1 = jnp.exp(total0) * start0 + own0
        end0 = jnp.exp(total1) * end1 + pull1
        coupling = jnp.where(
            early,
            jnp.sum(end0.astype(BF16).astype(F32) * start1, axis=0, keepdims=True),
            jnp.sum(end0 * start1.astype(BF16).astype(F32), axis=0, keepdims=True),
        )
        s0, s1, e0, e1 = (spread(t, left) for t in (start0, start1, end0, end1))

        def both(lhs, first, last, dims):
            return jnp.concatenate(
                [dot(lhs[:HALF], first, dims), dot(lhs[HALF:], last, dims)], axis=0
            )

        zero = jnp.zeros((), F32)
        scores = jnp.where(beneath, dot(up, down2, NT), zero).astype(BF16)
        scores_t = jnp.where(above, dot(down, up2, NT), zero).astype(BF16)
        products = jnp.where(beneath, dot(g16, v2, NT), zero).astype(BF16)
        products_t = jnp.where(above, dot(v16, g2, NT), zero).astype(BF16)

        present = None
        for piece in split(r * reward * k, 2):
            term = dot(piece, ones, NN)
            present = term if present is None else present + term
        agreement = None
        for piece in split(v * g, 2):
            term = dot(piece, ones, NN)
            agreement = term if agreement is None else agreement + term

        mixed_ref[:, at] = (
            dot(scores, v2, NN) + present * v + both(reached, s0, s1, NT)
        ).astype(BF16)
        dv_ref[:, at] = (
            both(faded, e0, e1, NT) + dot(scores_t, g2, NN) + present * g
        ).astype(BF16)
        past = both(g16, s0, s1, NN)
        near_past = dot(products, down2, NN)
        later = both(v16, e0, e1, NN)
        near_later = dot(products_t, up2, NN)
        dr_ref[:, at] = (
            entering * past + upward * near_past + reward * k * agreement
        ).astype(BF16)
        dk_ref[:, at] = (
            leaving * later + downward * near_later + reward * r * agreement
        ).astype(BF16)
        read = reached.astype(F32) * past + up.astype(F32) * near_past
        change = faded.astype(F32) * later + down.astype(F32) * near_later - read
        slope = (coupling + summed_by(around, change, 2) - read) * log_decay
        slope16 = slope.astype(BF16)
        slope_ref[:, at] = slope16
        chunk = 32 * (group // 2) + PAIRS * (group % 2) + pair
        sums_ref[0, chunk, 40:41, :] = jnp.sum(slope, axis=0, keepdims=True)
        sums_ref[1, chunk, 40:41, :] = jnp.sum(r * k * agreement, axis=0, keepdims=True)

    slopes = slope_ref[...]
    acc_ref[...] += dot(slopes, b_ref[...], NN)
    sums_ref[1, pl.ds(group * 16, 16), :40, :] = dot(slopes, gate, TN).reshape(16, 40, 128)

    @pl.when(group == GROUPS - 1)
    def _():
        smooth = smooth_ref[...]
        project = (acc_ref[...] * (1.0 - smooth * smooth)).astype(BF16)
        for i in range(GROUPS):
            at = pl.ds(i * WIDTH, WIDTH)
            dx_ref[:, at] = dot(project, a_ref[at, :], NT).astype(BF16)
            sums_ref[0, i * 16 : i * 16 + 16, :40, :] = dot(x_ref[:, at], project, TN).reshape(
                16, 40, 128
            )


def second_stage(x, a, r, k, v, g, b, speed, reward, smooth, gate, states):
    tokens = pl.BlockSpec((TOK, WIDTH), lambda i: (0, i))
    whole = lambda shape: pl.BlockSpec(shape, lambda i: (0,) * len(shape))
    channels = x.shape[1]
    full = jax.ShapeDtypeStruct((TOK, channels), BF16)
    return pl.pallas_call(
        second_kernel,
        grid=(GROUPS,),
        in_specs=[
            whole((TOK, channels)),
            whole((channels, 128)),
            tokens,
            tokens,
            tokens,
            tokens,
            pl.BlockSpec((WIDTH, 128), lambda i: (i, 0)),
            pl.BlockSpec((1, WIDTH), lambda i: (0, i)),
            pl.BlockSpec((1, WIDTH), lambda i: (0, i)),
            whole((TOK, 128)),
            whole((TOK, 128)),
            pl.BlockSpec((2, 8, 40, 128), lambda i: (0, i, 0, 0)),
        ],
        out_specs=[
            tokens,
            tokens,
            tokens,
            tokens,
            whole((TOK, channels)),
            whole((2, 64, 48, 128)),
        ],
        out_shape=[full] * 5 + [jax.ShapeDtypeStruct((2, 64, 48, 128), F32)],
        scratch_shapes=[pltpu.VMEM((TOK, WIDTH), BF16), pltpu.VMEM((TOK, 128), F32)],
        name="second_stage",
    )(x, a, r, k, v, g, b, speed, reward, smooth, gate, states)


def place():
    seq = lax.axis_index("seq")
    return seq // 2, seq % 2


def scan_kernel(
    z_ref, d_ref, o_ref,
    x_ref, dx_ref, dc_ref, t_ref, r_ref, q_ref, p_ref, y_ref,
    swap_send, swap_recv, out_send, out_recv, back_send, back_recv, end_send, end_recv,
):
    chip, core = place()
    other = 1 - core
    partner = {"seq": chip * 2 + other}

    def peer(m):
        return {"seq": m * 2 + core}

    def turn(o):
        return lax.rem(chip + o, CHIPS)

    barrier = pltpu.get_barrier_semaphore()
    pl.semaphore_signal(barrier, inc=1, device_id=partner)

    @pl.loop(1, CHIPS)
    def _(o):
        pl.semaphore_signal(barrier, inc=1, device_id=peer(turn(o)))

    pl.semaphore_wait(barrier, CHIPS)

    swap = pltpu.make_async_remote_copy(
        z_ref.at[other], x_ref, swap_send.at[0], swap_recv.at[0], device_id=partner
    )
    swap_decay = pltpu.make_async_remote_copy(
        d_ref, dx_ref, swap_send.at[1], swap_recv.at[1], device_id=partner
    )
    swap_decay.start()
    swap.start()
    swap_decay.wait_recv()
    dc_ref[...] = d_ref[...] * dx_ref[...]
    swap.wait_recv()

    def out_copy(m, slot):
        return pltpu.make_async_remote_copy(
            t_ref.at[m], r_ref.at[slot], out_send.at[m], out_recv.at[slot], device_id=peer(m)
        )

    def back_copy(n, slot):
        return pltpu.make_async_remote_copy(
            q_ref.at[n], p_ref.at[slot], back_send.at[n], back_recv.at[slot], device_id=peer(n)
        )

    def end_copy(m):
        return pltpu.make_async_remote_copy(
            y_ref.at[m], o_ref.at[core, m], end_send.at[m], end_recv.at[m], device_id=partner
        )

    def end_wait(m):
        pltpu.make_async_remote_copy(
            y_ref.at[m], o_ref.at[other, m], end_send.at[m], end_recv.at[m], device_id=partner
        ).wait_recv()

    def chip_total(m, target):
        group = m // 8
        for j in range(PAIRS):
            rows = slice(8 * j, 8 * j + 8)
            target[rows, :] = dx_ref[group, j : j + 1, :] * z_ref[core, m, rows, :] + x_ref[m, rows, :]
        target[40:48, :] = dc_ref[group]

    chip_total(chip, r_ref.at[chip])

    @pl.loop(1, CHIPS)
    def _(o):
        m = turn(o)
        chip_total(m, t_ref.at[m])
        out_copy(m, chip).start()

    def step(i, carry):
        n = core * (CHIPS - 1) + (1 - 2 * core) * i

        @pl.when(n != chip)
        def _():
            out_copy(n, n).wait_recv()

        after = []
        for j in range(PAIRS):
            rows = slice(8 * j, 8 * j + 8)
            q_ref[n, rows, :] = carry[j]
            after.append(r_ref[n, 40 + j : 41 + j, :] * carry[j] + r_ref[n, rows, :])

        @pl.when(n != chip)
        def _():
            back_copy(n, chip).start()

        return tuple(after)

    lax.fori_loop(0, CHIPS, step, tuple(jnp.zeros((8, 128), F32) for _ in range(PAIRS)))

    def finish(m, source):
        group = m // 8
        o_ref[core, m] = source[...]
        for j in range(PAIRS):
            rows = slice(8 * j, 8 * j + 8)
            y_ref[m, rows, :] = d_ref[group, j : j + 1, :] * source[rows, :] + z_ref[core, m, rows, :]
        end_copy(m).start()

    finish(chip, q_ref.at[chip])

    @pl.loop(1, CHIPS)
    def _(o):
        m = turn(o)
        back_copy(m, m).wait_recv()
        finish(m, p_ref.at[m])

    end_wait(chip)
    swap.wait_send()
    swap_decay.wait_send()
    end_copy(chip).wait_send()

    @pl.loop(1, CHIPS)
    def _(o):
        m = turn(o)
        end_wait(m)
        out_copy(m, chip).wait_send()
        back_copy(m, chip).wait_send()
        end_copy(m).wait_send()


def scan_stage(states, decays):
    vmem = pl.BlockSpec(memory_space=pltpu.VMEM)
    state = pltpu.VMEM((32, 40, 128), F32)
    message = pltpu.VMEM((32, 48, 128), F32)
    decay = pltpu.VMEM((GROUPS, 8, 128), F32)
    sems = pltpu.SemaphoreType.DMA
    return pl.pallas_call(
        scan_kernel,
        in_specs=[vmem, vmem],
        out_specs=vmem,
        out_shape=jax.ShapeDtypeStruct((2, 32, 40, 128), F32),
        scratch_shapes=[state, decay, decay, message, message, state, state, state]
        + [sems((2,)), sems((2,))]
        + [sems((CHIPS,))] * 6,
        compiler_params=pltpu.CompilerParams(collective_id=0, has_side_effects=True),
        name="scan_stage",
    )(states, decays)


def reduce_kernel(
    w_ref, o_ref,
    x_ref, t_ref, r_ref, s_ref,
    swap_send, swap_recv, out_send, out_recv, back_send, back_recv, end_send, end_recv,
):
    chip, core = place()
    half = lax.axis_index("dp")
    other = 1 - core
    mine = half * CHIPS + chip
    partner = {"seq": chip * 2 + other}

    def peer(c):
        return {"seq": lax.rem(c, CHIPS) * 2 + core, "dp": c // CHIPS}

    def turn(o):
        return lax.rem(mine + o, CHUNKS)

    def near(o):
        return lax.rem(chip + o, CHIPS)

    barrier = pltpu.get_barrier_semaphore()
    pl.semaphore_signal(barrier, inc=1, device_id=partner)

    @pl.loop(1, CHUNKS)
    def _(o):
        pl.semaphore_signal(barrier, inc=1, device_id=peer(turn(o)))

    pl.semaphore_wait(barrier, CHUNKS)

    def swap_copy(part):
        at = pl.ds(part * PART, PART)
        return pltpu.make_async_remote_copy(
            w_ref.at[other, at], x_ref.at[at], swap_send.at[part], swap_recv.at[part], device_id=partner
        )

    def out_copy(c, slot):
        return pltpu.make_async_remote_copy(
            t_ref.at[c], r_ref.at[slot], out_send.at[c], out_recv.at[slot], device_id=peer(c)
        )

    def back_copy(n):
        return pltpu.make_async_remote_copy(
            s_ref, o_ref.at[core, chip], back_send.at[n], back_recv.at[chip],
            device_id={"seq": n * 2 + core},
        )

    def back_wait(n):
        pltpu.make_async_remote_copy(
            s_ref, o_ref.at[core, n], back_send.at[n], back_recv.at[n],
            device_id={"seq": n * 2 + core},
        ).wait_recv()

    def end_copy(n):
        return pltpu.make_async_remote_copy(
            o_ref.at[core, n], o_ref.at[core, n], end_send.at[n], end_recv.at[n], device_id=partner
        )

    def end_wait(n):
        pltpu.make_async_remote_copy(
            o_ref.at[other, n], o_ref.at[other, n], end_send.at[n], end_recv.at[n], device_id=partner
        ).wait_recv()

    for part in range(PARTS):
        swap_copy(part).start()
    for part in range(PARTS):
        swap_copy(part).wait_recv()

        @pl.loop(part * PART, part * PART + PART)
        def _(c):
            t_ref[c] = w_ref[core, c] + x_ref[c]

            @pl.when(c != mine)
            def _():
                out_copy(c, mine).start()

    def add(o, total):
        c = turn(o)
        out_copy(c, c).wait_recv()
        return total + r_ref[c]

    s_ref[...] = lax.fori_loop(1, CHUNKS, add, t_ref[mine])

    @pl.loop(1, CHIPS)
    def _(o):
        back_copy(near(o)).start()

    o_ref[core, chip] = s_ref[...]
    end_copy(chip).start()

    @pl.loop(1, CHIPS)
    def _(o):
        n = near(o)
        back_wait(n)
        end_copy(n).start()

    for part in range(PARTS):
        swap_copy(part).wait_send()

    @pl.loop(1, CHUNKS)
    def _(o):
        out_copy(turn(o), mine).wait_send()

    @pl.loop(0, CHIPS)
    def _(o):
        n = near(o)
        end_wait(n)
        end_copy(n).wait_send()

    @pl.loop(1, CHIPS)
    def _(o):
        back_copy(near(o)).wait_send()


def reduce_stage(sums):
    vmem = pl.BlockSpec(memory_space=pltpu.VMEM)
    rows = sums.shape[2]
    chunks = pltpu.VMEM((CHUNKS, rows, 128), F32)
    sems = pltpu.SemaphoreType.DMA
    return pl.pallas_call(
        reduce_kernel,
        in_specs=[vmem],
        out_specs=vmem,
        out_shape=jax.ShapeDtypeStruct((2, CHIPS, rows, 128), F32),
        scratch_shapes=[chunks, chunks, chunks, pltpu.VMEM((rows, 128), F32)]
        + [sems((PARTS,))] * 2
        + [sems((CHUNKS,))] * 2
        + [sems((CHIPS,))] * 4,
        compiler_params=pltpu.CompilerParams(collective_id=1, has_side_effects=True),
        name="reduce_stage",
    )(sums)


def per_device(scan, reduce, r, k, v, x, g, lowering, raising, speed, reward):
    r, k, v, x, g = (t[0] for t in (r, k, v, x, g))
    speed, reward = speed[None], reward[None]
    states, decays, smooth, gate = first_stage(x, lowering, r, k, v, g, raising, speed)
    entering = scan(states, decays)
    mixed, dr, dk, dv, dx, sums = second_stage(
        x, lowering, r, k, v, g, raising, speed, reward, smooth, gate, entering
    )
    share = reduce(sums)
    return (
        mixed[None],
        dr[None],
        dk[None],
        dv[None],
        dx[None],
        share[0, :, :40].reshape(1280, 128),
        share[1, :, :40].reshape(1280, 128),
        share[0, :10, 40].reshape(1280),
        share[1, :10, 40].reshape(1280),
    )


def build(mesh, scan, reduce):
    tokens = P("dp", "seq", None)
    return jax.shard_map(
        functools.partial(per_device, scan, reduce),
        mesh=mesh,
        in_specs=(tokens,) * 5 + (P(),) * 4,
        out_specs=(tokens,) * 5 + (P("dp", None),) * 2 + (P("dp"),) * 2,
        check_vma=False,
    )


def solution(mesh):
    return build(mesh, scan_stage, reduce_stage)
```

```python
import jax
import jax.numpy as jnp
from jax import lax
from jax.experimental import pallas as pl
from jax.experimental.pallas import tpu as pltpu
from jax.sharding import PartitionSpec as P

F32 = jnp.float32
BF16 = jnp.bfloat16
TOK = 128
HALF = 64
GROUPS = 4
PAIRS = 5
WIDTH = PAIRS * 128
CHIPS = 32
CHUNKS = 2 * CHIPS
BATCH = CHUNKS // GROUPS
NN = (((1,), (0,)), ((), ()))
NT = (((1,), (1,)), ((), ()))
TN = (((0,), (0,)), ((), ()))


def dot(a, b, dims):
    return lax.dot_general(a, b, dims, preferred_element_type=F32)


def split(x, parts):
    pieces = []
    for _ in range(parts - 1):
        head = x.astype(BF16)
        pieces.append(head)
        x = x - head.astype(F32)
    pieces.append(x.astype(BF16))
    return pieces


def summed_by(matrix, x, parts):
    total = None
    for piece in split(x, parts):
        term = dot(matrix, piece, NN)
        total = term if total is None else total + term
    return total


def grids():
    row = lax.broadcasted_iota(jnp.int32, (TOK, TOK), 0)
    col = lax.broadcasted_iota(jnp.int32, (TOK, TOK), 1)
    same = (row < HALF) == (col < HALF)
    return row, col, same


def as_matrix(condition):
    return jnp.where(condition, 1.0, 0.0).astype(BF16)


def decay_sums(gate, raising, speed, lower):
    rank = dot(gate, raising, NT)
    log_decay = -speed * jnp.exp(rank)
    inclusive = summed_by(lower, log_decay, 3)
    return (
        log_decay,
        inclusive,
        inclusive - log_decay,
        inclusive[HALF - 1 : HALF],
        inclusive[TOK - 1 : TOK],
    )


def both(lhs, first, last, dims):
    return jnp.concatenate([dot(lhs[:HALF], first, dims), dot(lhs[HALF:], last, dims)], axis=0)


def packed(product, left):
    return jnp.where(left[:HALF], product[:HALF], product[HALF:])


def spread(state, left):
    zero = jnp.zeros_like(state)
    return jnp.concatenate(
        [jnp.where(left[:HALF], state, zero), jnp.where(left[:HALF], zero, state)], axis=0
    )


def whole_kernel(
    x_hbm, a_hbm, r_hbm, k_hbm, v_hbm, g_hbm, b_hbm, speed_ref, reward_ref,
    mixed_ref, dr_ref, dk_ref, dv_ref, dx_ref, red_ref,
    x_ref, a_ref, r_ref, k_ref, v_ref, g_ref, b_ref, fetch_sem,
    s0_ref, s1_ref, e0_ref, e1_ref,
    smooth_ref, gate_ref, log_ref, sum_ref, enter_ref, leave_ref, reached_ref, faded_ref,
    own_ref, pull_ref, ends_ref,
    mixed_near, dv_near, dr_near, dk_near, read_near, change_near, slope_ref, acc_ref,
    z_ref, d_ref, zx_ref, dx_decay, dc_ref, t_ref, rec_ref, q_ref, p_ref, y_ref, st_ref,
    wa_ref, wb_ref, wx_ref, wt_ref, wr_ref, ws_ref,
    swap_send, swap_recv, out_send, out_recv, back_send, back_recv, end_send, end_recv,
    give_send, give_recv, cast_send, cast_recv, share_send, share_recv, last_send, last_recv,
):
    seq = lax.axis_index("seq")
    chip, core = seq // 2, seq % 2
    other = 1 - core
    mine = lax.axis_index("dp") * CHIPS + chip
    partner = {"seq": chip * 2 + other}

    def peer(m):
        return {"seq": m * 2 + core}

    def owner(c):
        return {"seq": lax.rem(c, CHIPS) * 2 + core, "dp": c // CHIPS}

    def turn(o):
        return lax.rem(chip + o, CHIPS)

    def wide_turn(o):
        return lax.rem(mine + o, CHUNKS)

    fetches = [
        pltpu.make_async_copy(source, target, fetch_sem.at[i])
        for i, (source, target) in enumerate(
            (
                (x_hbm, x_ref),
                (a_hbm, a_ref),
                (b_hbm, b_ref),
                (k_hbm, k_ref),
                (r_hbm, r_ref),
                (v_hbm, v_ref),
                (g_hbm, g_ref),
            )
        )
    ]
    for fetch in fetches:
        fetch.start()

    barrier = pltpu.get_barrier_semaphore()
    pl.semaphore_signal(barrier, inc=1, device_id=partner)

    @pl.loop(1, CHUNKS)
    def _(o):
        pl.semaphore_signal(barrier, inc=1, device_id=owner(wide_turn(o)))

    row, col, same = grids()
    lower = as_matrix(same & (row >= col))
    ones = as_matrix((row < HALF) == (col < HALF))
    left = col < HALF
    early = row < HALF
    around = jnp.where(
        same & ~early & (col < row), 1.0, jnp.where(same & early & (col >= row), -1.0, 0.0)
    ).astype(BF16)

    fetches[0].wait()
    fetches[1].wait()
    smooth = jnp.tanh(dot(x_ref[...], a_ref[...], NN))
    smooth_ref[...] = smooth
    gate_ref[...] = smooth.astype(BF16)
    acc_ref[...] = jnp.zeros_like(acc_ref)
    wa_ref[:, 40:, :] = jnp.zeros((CHUNKS, 8, 128), F32)
    wb_ref[:, 40:, :] = jnp.zeros((CHUNKS, 8, 128), F32)

    def lanes(group, pair):
        return pl.ds(pl.multiple_of(group * WIDTH + pair * 128, 128), 128)

    def vector(ref, group, pair):
        return ref[lanes(group, pair)].reshape(1, 128)

    def by_head(x):
        zero = jnp.zeros_like(x)
        return jnp.concatenate([jnp.where(left, x, zero), jnp.where(left, zero, x)], axis=0)

    def outputs_of(group):
        for pair in range(PAIRS):
            at = lanes(group, pair)
            s0, s1, e0, e1 = (
                spread(ref[:, at], left) for ref in (s0_ref, s1_ref, e0_ref, e1_ref)
            )
            mixed_ref[:, at] = (
                mixed_near[:, at] + both(reached_ref[:, at], s0, s1, NT)
            ).astype(BF16)
            dv_ref[:, at] = (dv_near[:, at] + both(faded_ref[:, at], e0, e1, NT)).astype(BF16)

    def states_of(group):
        gate = gate_ref[...]
        for pair in range(PAIRS):
            at = lanes(group, pair)
            log_decay, inclusive, exclusive, total0, total1 = decay_sums(
                gate, b_ref[at, :], vector(speed_ref, group, pair), lower
            )
            entering = jnp.exp(exclusive)
            leaving = jnp.exp(jnp.where(early, total0, total1) - inclusive)
            reached = (r_ref[:, at].astype(F32) * entering).astype(BF16)
            faded = (k_ref[:, at].astype(F32) * leaving).astype(BF16)
            log_ref[:, at] = log_decay
            sum_ref[:, at] = inclusive
            enter_ref[:, at] = entering
            leave_ref[:, at] = leaving
            reached_ref[:, at] = reached
            faded_ref[:, at] = faded
            v16, g16 = v_ref[:, at], g_ref[:, at]
            own0 = packed(dot(v16[:HALF], faded[:HALF], TN), left)
            own1 = packed(dot(v16[HALF:], faded[HALF:], TN), left)
            pull0 = packed(dot(g16[:HALF], reached[:HALF], TN), left)
            pull1 = packed(dot(g16[HALF:], reached[HALF:], TN), left)
            end0, end1 = jnp.exp(total0), jnp.exp(total1)
            own_ref[:, at] = own0
            pull_ref[:, at] = pull1
            ends_ref[0:1, at] = end0
            ends_ref[1:2, at] = end1
            rows = slice(pair * 8, pair * 8 + 8)
            chunks = pl.ds(group * 8, 8)
            z_ref[0, chunks, rows, :] = (end1 * own0 + own1).reshape(8, 8, 128)
            z_ref[1, chunks, rows, :] = (end0 * pull1 + pull0).reshape(8, 8, 128)
            d_ref[group, pair : pair + 1, :] = jnp.exp(total0 + total1)
        d_ref[group, PAIRS:, :] = jnp.zeros((8 - PAIRS, 128), F32)

    def near_terms(group):
        wide_row = lax.broadcasted_iota(jnp.int32, (TOK, 2 * TOK), 0)
        wide_col = lax.broadcasted_iota(jnp.int32, (TOK, 2 * TOK), 1) % TOK
        wide_same = (wide_row < HALF) == (wide_col < HALF)
        beneath = wide_same & (wide_row > wide_col)
        above = wide_same & (wide_row < wide_col)
        zero = jnp.zeros((), F32)
        for pair in range(PAIRS):
            at = lanes(group, pair)
            inclusive = sum_ref[:, at]
            middle = jnp.where(
                early,
                inclusive[HALF // 2 - 1 : HALF // 2],
                inclusive[HALF + HALF // 2 - 1 : HALF + HALF // 2],
            )
            upward = jnp.exp(inclusive - log_ref[:, at] - middle)
            downward = jnp.exp(middle - inclusive)
            v16, g16 = v_ref[:, at], g_ref[:, at]
            r, k, v, g = (t[:, at].astype(F32) for t in (r_ref, k_ref, v_ref, g_ref))
            reward = vector(reward_ref, group, pair)
            up = (r * upward).astype(BF16)
            down = (k * downward).astype(BF16)
            v2, g2, up2, down2 = by_head(v16), by_head(g16), by_head(up), by_head(down)
            scores = jnp.where(beneath, dot(up, down2, NT), zero).astype(BF16)
            scores_t = jnp.where(above, dot(down, up2, NT), zero).astype(BF16)
            products = jnp.where(beneath, dot(g16, v2, NT), zero).astype(BF16)
            products_t = jnp.where(above, dot(v16, g2, NT), zero).astype(BF16)
            present = summed_over(r * reward * k, ones)
            agreement = summed_over(v * g, ones)
            mixed_near[:, at] = dot(scores, v2, NN) + present * v
            dv_near[:, at] = dot(scores_t, g2, NN) + present * g
            near_past = dot(products, down2, NN)
            near_later = dot(products_t, up2, NN)
            dr_near[:, at] = upward * near_past + reward * k * agreement
            dk_near[:, at] = downward * near_later + reward * r * agreement
            read = up.astype(F32) * near_past
            read_near[:, at] = read
            change_near[:, at] = down.astype(F32) * near_later - read
            chunk = CHIPS * (group // 2) + PAIRS * (group % 2) + pair
            wb_ref[chunk, 40:41, :] = jnp.sum(r * k * agreement, axis=0, keepdims=True)

    def far_terms(group):
        gate = gate_ref[...]
        for pair in range(PAIRS):
            at = lanes(group, pair)
            rows = slice(pair * 8, pair * 8 + 8)
            chunks = pl.ds(group * 8, 8)
            start0 = st_ref[0, chunks, rows, :].reshape(HALF, 128)
            end1 = st_ref[1, chunks, rows, :].reshape(HALF, 128)
            start1 = ends_ref[0:1, at] * start0 + own_ref[:, at]
            end0 = ends_ref[1:2, at] * end1 + pull_ref[:, at]
            lows = [t.astype(BF16) for t in (start0, start1, end0, end1)]
            for low_ref, low in zip((s0_ref, s1_ref, e0_ref, e1_ref), lows):
                low_ref[:, at] = low
            s0, s1, e0, e1 = (spread(t, left) for t in lows)
            coupling = jnp.where(
                early,
                jnp.sum(lows[2].astype(F32) * start1, axis=0, keepdims=True),
                jnp.sum(end0 * lows[1].astype(F32), axis=0, keepdims=True),
            )
            reached, faded = reached_ref[:, at], faded_ref[:, at]
            past = both(g_ref[:, at], s0, s1, NN)
            later = both(v_ref[:, at], e0, e1, NN)
            dr_ref[:, at] = (dr_near[:, at] + enter_ref[:, at] * past).astype(BF16)
            dk_ref[:, at] = (dk_near[:, at] + leave_ref[:, at] * later).astype(BF16)
            far_read = reached.astype(F32) * past
            read = read_near[:, at] + far_read
            change = change_near[:, at] + (faded.astype(F32) * later - far_read)
            slope = (coupling + summed_by(around, change, 2) - read) * log_ref[:, at]
            slope_ref[:, at] = slope.astype(BF16)
            chunk = CHIPS * (group // 2) + PAIRS * (group % 2) + pair
            wa_ref[chunk, 40:41, :] = jnp.sum(slope, axis=0, keepdims=True)
        wide = pl.ds(pl.multiple_of(group * WIDTH, 128), WIDTH)
        slopes = slope_ref[:, wide]
        acc_ref[...] += dot(slopes, b_ref[wide, :], NN)
        wb_ref[pl.ds(group * BATCH, BATCH), :40, :] = dot(slopes, gate, TN).reshape(BATCH, 40, 128)

    def swap(group):
        chunks = pl.ds(group * 8, 8)
        return pltpu.make_async_remote_copy(
            z_ref.at[other, chunks], zx_ref.at[chunks],
            swap_send.at[group], swap_recv.at[group], device_id=partner,
        )

    def swap_decay(group):
        return pltpu.make_async_remote_copy(
            d_ref.at[group], dx_decay.at[group],
            swap_send.at[GROUPS + group], swap_recv.at[GROUPS + group], device_id=partner,
        )

    for fetch in fetches[2:]:
        fetch.wait()

    @pl.loop(0, GROUPS)
    def _(group):
        states_of(group)

        @pl.when(group == 0)
        def _():
            pl.semaphore_wait(barrier, CHUNKS)

        swap_decay(group).start()
        swap(group).start()

    @pl.loop(0, GROUPS)
    def _(group):
        swap_decay(group).wait_recv()
        dc_ref[group] = d_ref[group] * dx_decay[group]
        swap(group).wait_recv()

    def out_copy(m, slot):
        return pltpu.make_async_remote_copy(
            t_ref.at[m], rec_ref.at[slot], out_send.at[m], out_recv.at[slot], device_id=peer(m)
        )

    def back_copy(n, slot):
        return pltpu.make_async_remote_copy(
            q_ref.at[n], p_ref.at[slot], back_send.at[n], back_recv.at[slot], device_id=peer(n)
        )

    def end_copy(m):
        return pltpu.make_async_remote_copy(
            y_ref.at[m], st_ref.at[core, m], end_send.at[m], end_recv.at[m], device_id=partner
        )

    def end_wait(m):
        pltpu.make_async_remote_copy(
            y_ref.at[m], st_ref.at[other, m], end_send.at[m], end_recv.at[m], device_id=partner
        ).wait_recv()

    def chip_total(m, target):
        group = m // 8
        for j in range(PAIRS):
            rows = slice(8 * j, 8 * j + 8)
            target[rows, :] = (
                dx_decay[group, j : j + 1, :] * z_ref[core, m, rows, :] + zx_ref[m, rows, :]
            )
        target[40:48, :] = dc_ref[group]

    def pick(j):
        return (2 + 3 * j + 3 * (j // 2) + 2 * (j // 3)) % 4

    def farthest(i):
        y = lax.rem(chip // 8 + pick((i // 4) % 4), 4)
        x = lax.rem((chip // 4) % 2 + 1 - i // 16, 2)
        z = lax.rem(chip % 4 + pick(i % 4), 4)
        return (y * 2 + x) * 4 + z

    @pl.loop(0, CHIPS - 1)
    def _(i):
        m = farthest(i)
        chip_total(m, t_ref.at[m])
        out_copy(m, chip).start()

    chip_total(chip, rec_ref.at[chip])

    @pl.loop(0, GROUPS - 1)
    def _(group):
        near_terms(group)

    def step(i, carry):
        n = core * (CHIPS - 1) + (1 - 2 * core) * i

        @pl.when(n != chip)
        def _():
            out_copy(n, n).wait_recv()

        after = []
        for j in range(PAIRS):
            rows = slice(8 * j, 8 * j + 8)
            q_ref[n, rows, :] = carry[j]
            after.append(rec_ref[n, 40 + j : 41 + j, :] * carry[j] + rec_ref[n, rows, :])

        @pl.when(n != chip)
        def _():
            back_copy(n, chip).start()

        return tuple(after)

    lax.fori_loop(0, CHIPS, step, tuple(jnp.zeros((8, 128), F32) for _ in range(PAIRS)))

    near_terms(GROUPS - 1)

    def finish(m, source):
        group = m // 8
        st_ref[core, m] = source[...]
        for j in range(PAIRS):
            rows = slice(8 * j, 8 * j + 8)
            y_ref[m, rows, :] = (
                d_ref[group, j : j + 1, :] * source[rows, :] + z_ref[core, m, rows, :]
            )
        end_copy(m).start()

    finish(chip, q_ref.at[chip])

    @pl.loop(1, CHIPS)
    def _(o):
        m = turn(o)
        back_copy(m, m).wait_recv()
        finish(m, p_ref.at[m])

    def give(w_ref, part):
        at = pl.ds(part * BATCH, BATCH)
        return pltpu.make_async_remote_copy(
            w_ref.at[at], wx_ref.at[at], give_send.at[part], give_recv.at[part], device_id=partner
        )

    def cast(c, slot):
        return pltpu.make_async_remote_copy(
            wt_ref.at[c], wr_ref.at[slot], cast_send.at[c], cast_recv.at[slot], device_id=owner(c)
        )

    def ship(w_ref, part):
        give(w_ref, part).wait_recv()

        @pl.loop(0, BATCH)
        def _(i):
            c = part * BATCH + lax.rem(mine + 1 + i, BATCH)
            wt_ref[c] = w_ref[c] + wx_ref[c]

            @pl.when(c != mine)
            def _():
                cast(c, mine).start()

    def rotated(i):
        return lax.rem(mine // BATCH + 1 + i, GROUPS)

    @pl.loop(0, GROUPS)
    def _(i):
        group = rotated(i)

        @pl.loop(group * 8, group * 8 + 8)
        def _(m):
            end_wait(m)

        far_terms(group)

        @pl.when(core == 0)
        def _():
            give(wb_ref, group).start()

        @pl.when((core == 1) & (i > 0))
        def _():
            ship(wb_ref, rotated(i - 1))

    smooth = smooth_ref[...]
    project = (acc_ref[...] * (1.0 - smooth * smooth)).astype(BF16)

    @pl.loop(0, GROUPS)
    def _(i):
        group = rotated(i)
        wide = pl.ds(pl.multiple_of(group * WIDTH, 128), WIDTH)
        wa_ref[pl.ds(group * BATCH, BATCH), :40, :] = dot(x_ref[:, wide], project, TN).reshape(
            BATCH, 40, 128
        )

        @pl.when(core == 1)
        def _():
            give(wa_ref, group).start()

    @pl.when(core == 1)
    def _():
        ship(wb_ref, rotated(GROUPS - 1))

    @pl.when(core == 0)
    def _():
        @pl.loop(0, GROUPS)
        def _(i):
            ship(wa_ref, rotated(i))

    @pl.loop(0, GROUPS)
    def _(group):
        wide = pl.ds(pl.multiple_of(group * WIDTH, 128), WIDTH)
        dx_ref[:, wide] = dot(project, a_ref[wide, :], NT).astype(BF16)
        outputs_of(group)

    def share(n):
        return pltpu.make_async_remote_copy(
            ws_ref, red_ref.at[core, chip], share_send.at[n], share_recv.at[chip], device_id=peer(n)
        )

    def share_wait(n):
        pltpu.make_async_remote_copy(
            ws_ref, red_ref.at[core, n], share_send.at[n], share_recv.at[n], device_id=peer(n)
        ).wait_recv()

    def last(n):
        return pltpu.make_async_remote_copy(
            red_ref.at[core, n], red_ref.at[core, n], last_send.at[n], last_recv.at[n],
            device_id=partner,
        )

    def last_wait(n):
        pltpu.make_async_remote_copy(
            red_ref.at[other, n], red_ref.at[other, n], last_send.at[n], last_recv.at[n],
            device_id=partner,
        ).wait_recv()

    def add(o, total):
        c = wide_turn(o)
        cast(c, c).wait_recv()
        return total + wr_ref[c]

    ws_ref[...] = lax.fori_loop(1, CHUNKS, add, wt_ref[mine])

    @pl.loop(0, CHIPS - 1)
    def _(i):
        share(farthest(i)).start()

    red_ref[core, chip] = ws_ref[...]
    last(chip).start()

    @pl.loop(1, CHIPS)
    def _(o):
        n = turn(o)
        share_wait(n)
        last(n).start()

    end_copy(chip).wait_send()

    @pl.loop(1, CHIPS)
    def _(o):
        m = turn(o)
        out_copy(m, chip).wait_send()
        back_copy(m, chip).wait_send()
        end_copy(m).wait_send()
        share(m).wait_send()

    @pl.loop(0, GROUPS)
    def _(group):
        swap(group).wait_send()
        swap_decay(group).wait_send()
        give(wb_ref, group).wait_send()

    @pl.loop(1, CHUNKS)
    def _(o):
        cast(wide_turn(o), mine).wait_send()

    @pl.loop(0, CHIPS)
    def _(o):
        n = turn(o)
        last_wait(n)
        last(n).wait_send()


def summed_over(x, ones):
    total = None
    for piece in split(x, 2):
        term = dot(piece, ones, NN)
        total = term if total is None else total + term
    return total


def whole_stage(x, a, r, k, v, g, b, speed, reward):
    vmem = pl.BlockSpec(memory_space=pltpu.VMEM)
    channels = x.shape[1]
    full = jax.ShapeDtypeStruct((TOK, channels), BF16)
    wide = pltpu.VMEM((TOK, channels), F32)
    short = pltpu.VMEM((TOK, channels), BF16)
    half = pltpu.VMEM((HALF, channels), F32)
    low = pltpu.VMEM((HALF, channels), BF16)
    matrix = pltpu.VMEM((channels, 128), BF16)
    square = pltpu.VMEM((TOK, 128), F32)
    state = pltpu.VMEM((32, 40, 128), F32)
    states = pltpu.VMEM((2, 32, 40, 128), F32)
    message = pltpu.VMEM((32, 48, 128), F32)
    decay = pltpu.VMEM((GROUPS, 8, 128), F32)
    sums = pltpu.VMEM((CHUNKS, 48, 128), F32)
    sems = pltpu.SemaphoreType.DMA
    return pl.pallas_call(
        whole_kernel,
        in_specs=[pl.BlockSpec(memory_space=pltpu.HBM)] * 7 + [vmem] * 2,
        out_specs=[vmem] * 6,
        out_shape=[full] * 5 + [jax.ShapeDtypeStruct((2, CHIPS, 48, 128), F32)],
        scratch_shapes=[short, matrix, short, short, short, short, matrix, sems((7,))]
        + [low] * 4
        + [square, pltpu.VMEM((TOK, 128), BF16)]
        + [wide] * 4
        + [short] * 2
        + [half, half, pltpu.VMEM((8, channels), F32)]
        + [wide] * 6
        + [short, square]
        + [states, decay, state, decay, decay, message, message, state, state, state, states]
        + [sums] * 5
        + [pltpu.VMEM((48, 128), F32)]
        + [sems((2 * GROUPS,))] * 2
        + [sems((CHIPS,))] * 6
        + [sems((GROUPS,))] * 2
        + [sems((CHUNKS,))] * 2
        + [sems((CHIPS,))] * 4,
        compiler_params=pltpu.CompilerParams(
            collective_id=0, has_side_effects=True, vmem_limit_bytes=50 * 1024 * 1024
        ),
        name="whole_stage",
    )(x, a, r, k, v, g, b, speed, reward)


def emit_kernel(*refs):
    sources, red_ref = refs[:5], refs[5]
    targets, sem = refs[6:13], refs[15]
    time_ref, bonus_ref = refs[13:15]
    parts = list(sources) + [red_ref.at[0, :, pl.ds(0, 40)], red_ref.at[1, :, pl.ds(0, 40)]]
    copies = [
        pltpu.make_async_copy(part, target, sem.at[i])
        for i, (part, target) in enumerate(zip(parts, targets))
    ]
    for copy in copies:
        copy.start()
    for i in range(10):
        time_ref[pl.ds(128 * i, 128)] = red_ref[0, i, 40:41, :].reshape(128)
        bonus_ref[pl.ds(128 * i, 128)] = red_ref[1, i, 40:41, :].reshape(128)
    for copy in copies:
        copy.wait()


def emit_stage(mixed, dr, dk, dv, dx, red):
    vmem = pl.BlockSpec(memory_space=pltpu.VMEM)
    hbm = pl.BlockSpec(memory_space=pltpu.HBM)
    full = jax.ShapeDtypeStruct(mixed.shape, BF16)
    return pl.pallas_call(
        emit_kernel,
        in_specs=[vmem] * 6,
        out_specs=[hbm] * 7 + [vmem] * 2,
        out_shape=[full] * 5
        + [jax.ShapeDtypeStruct((CHIPS, 40, 128), F32)] * 2
        + [jax.ShapeDtypeStruct((1280,), F32)] * 2,
        scratch_shapes=[pltpu.SemaphoreType.DMA((7,))],
        compiler_params=pltpu.CompilerParams(vmem_limit_bytes=8 * 1024 * 1024),
        name="emit_stage",
    )(mixed, dr, dk, dv, dx, red)


def per_device(r, k, v, x, g, lowering, raising, speed, reward):
    r, k, v, x, g = (t[0] for t in (r, k, v, x, g))
    outs = emit_stage(*whole_stage(x, lowering, r, k, v, g, raising, speed, reward))
    lora = tuple(t.reshape(1280, 128) for t in outs[5:7])
    return tuple(t[None] for t in outs[:5]) + lora + tuple(outs[7:])


def solution(mesh):
    tokens = P("dp", "seq", None)
    return jax.shard_map(
        per_device,
        mesh=mesh,
        in_specs=(tokens,) * 5 + (P(),) * 4,
        out_specs=(tokens,) * 5 + (P("dp", None),) * 2 + (P("dp"),) * 2,
        check_vma=False,
    )
```

```python
import jax
import jax.numpy as jnp
from jax import lax
from jax.experimental import pallas as pl
from jax.experimental.pallas import tpu as pltpu
from jax.sharding import PartitionSpec as P

F32 = jnp.float32
BF16 = jnp.bfloat16
TOK = 128
HALF = 64
GROUPS = 4
PAIRS = 5
WIDTH = PAIRS * 128
CHIPS = 32
CHUNKS = 2 * CHIPS
BATCH = CHUNKS // GROUPS
NN = (((1,), (0,)), ((), ()))
NT = (((1,), (1,)), ((), ()))
TN = (((0,), (0,)), ((), ()))


def dot(a, b, dims):
    return lax.dot_general(a, b, dims, preferred_element_type=F32)


def split(x, parts):
    pieces = []
    for _ in range(parts - 1):
        head = x.astype(BF16)
        pieces.append(head)
        x = x - head.astype(F32)
    pieces.append(x.astype(BF16))
    return pieces


def summed_by(matrix, x, parts):
    total = None
    for piece in split(x, parts):
        term = dot(matrix, piece, NN)
        total = term if total is None else total + term
    return total


def grids():
    row = lax.broadcasted_iota(jnp.int32, (TOK, TOK), 0)
    col = lax.broadcasted_iota(jnp.int32, (TOK, TOK), 1)
    same = (row < HALF) == (col < HALF)
    return row, col, same


def as_matrix(condition):
    return jnp.where(condition, 1.0, 0.0).astype(BF16)


def decay_sums(gate, raising, speed, lower):
    rank = dot(gate, raising, NT)
    log_decay = -speed * jnp.exp(rank)
    inclusive = summed_by(lower, log_decay, 3)
    return (
        log_decay,
        inclusive,
        inclusive - log_decay,
        inclusive[HALF - 1 : HALF],
        inclusive[TOK - 1 : TOK],
    )


def both(lhs, first, last, dims):
    return jnp.concatenate([dot(lhs[:HALF], first, dims), dot(lhs[HALF:], last, dims)], axis=0)


def packed(product, left):
    return jnp.where(left[:HALF], product[:HALF], product[HALF:])


def spread(state, left):
    zero = jnp.zeros_like(state)
    return jnp.concatenate(
        [jnp.where(left[:HALF], state, zero), jnp.where(left[:HALF], zero, state)], axis=0
    )


def whole_kernel(
    x_hbm, a_hbm, r_hbm, k_hbm, v_hbm, g_hbm, b_hbm, speed_hbm, reward_hbm,
    mixed_ref, dr_ref, dk_ref, dv_ref, dx_ref, red_ref,
    x_ref, a_ref, r_ref, k_ref, v_ref, g_ref, b_ref, speed_ref, reward_ref, fetch_sem,
    s0_ref, s1_ref, e0_ref, e1_ref,
    smooth_ref, gate_ref, log_ref, sum_ref, enter_ref, leave_ref, reached_ref, faded_ref,
    own_ref, pull_ref, ends_ref,
    mixed_near, dv_near, dr_near, dk_near, read_near, change_near, slope_ref, acc_ref,
    z_ref, d_ref, zx_ref, dx_decay, dc_ref, t_ref, rec_ref, q_ref, p_ref, y_ref, st_ref,
    wa_ref, wb_ref, wx_ref, wt_ref, wr_ref, ws_ref,
    swap_send, swap_recv, out_send, out_recv, back_send, back_recv, end_send, end_recv,
    give_send, give_recv, cast_send, cast_recv, share_send, share_recv, last_send, last_recv,
):
    seq = lax.axis_index("seq")
    chip, core = seq // 2, seq % 2
    other = 1 - core
    mine = lax.axis_index("dp") * CHIPS + chip
    partner = {"seq": chip * 2 + other}

    def peer(m):
        return {"seq": m * 2 + core}

    def owner(c):
        return {"seq": lax.rem(c, CHIPS) * 2 + core, "dp": c // CHIPS}

    def turn(o):
        return lax.rem(chip + o, CHIPS)

    def wide_turn(o):
        return lax.rem(mine + o, CHUNKS)

    fetches = [
        pltpu.make_async_copy(source, target, fetch_sem.at[i])
        for i, (source, target) in enumerate(
            (
                (x_hbm, x_ref),
                (a_hbm, a_ref),
                (b_hbm, b_ref),
                (speed_hbm, speed_ref),
                (k_hbm, k_ref),
                (r_hbm, r_ref),
                (v_hbm, v_ref),
                (g_hbm, g_ref),
                (reward_hbm, reward_ref),
            )
        )
    ]
    for fetch in fetches:
        fetch.start()

    barrier = pltpu.get_barrier_semaphore()
    pl.semaphore_signal(barrier, inc=1, device_id=partner)

    @pl.loop(1, CHUNKS)
    def _(o):
        pl.semaphore_signal(barrier, inc=1, device_id=owner(wide_turn(o)))

    row, col, same = grids()
    lower = as_matrix(same & (row >= col))
    ones = as_matrix((row < HALF) == (col < HALF))
    left = col < HALF
    early = row < HALF
    around = jnp.where(
        same & ~early & (col < row), 1.0, jnp.where(same & early & (col >= row), -1.0, 0.0)
    ).astype(BF16)

    fetches[0].wait()
    fetches[1].wait()
    smooth = jnp.tanh(dot(x_ref[...], a_ref[...], NN))
    smooth_ref[...] = smooth
    gate_ref[...] = smooth.astype(BF16)
    acc_ref[...] = jnp.zeros_like(acc_ref)
    wa_ref[:, 40:, :] = jnp.zeros((CHUNKS, 8, 128), F32)
    wb_ref[:, 40:, :] = jnp.zeros((CHUNKS, 8, 128), F32)

    def lanes(group, pair):
        return pl.ds(pl.multiple_of(group * WIDTH + pair * 128, 128), 128)

    def vector(ref, group, pair):
        return ref[lanes(group, pair)].reshape(1, 128)

    def by_head(x):
        zero = jnp.zeros_like(x)
        return jnp.concatenate([jnp.where(left, x, zero), jnp.where(left, zero, x)], axis=0)

    def outputs_of(group):
        for pair in range(PAIRS):
            at = lanes(group, pair)
            s0, s1, e0, e1 = (
                spread(ref[:, at], left) for ref in (s0_ref, s1_ref, e0_ref, e1_ref)
            )
            mixed_ref[:, at] = (
                mixed_near[:, at] + both(reached_ref[:, at], s0, s1, NT)
            ).astype(BF16)
            dv_ref[:, at] = (dv_near[:, at] + both(faded_ref[:, at], e0, e1, NT)).astype(BF16)

    def states_of(group):
        gate = gate_ref[...]
        for pair in range(PAIRS):
            at = lanes(group, pair)
            log_decay, inclusive, exclusive, total0, total1 = decay_sums(
                gate, b_ref[at, :], vector(speed_ref, group, pair), lower
            )
            entering = jnp.exp(exclusive)
            leaving = jnp.exp(jnp.where(early, total0, total1) - inclusive)
            reached = (r_ref[:, at].astype(F32) * entering).astype(BF16)
            faded = (k_ref[:, at].astype(F32) * leaving).astype(BF16)
            log_ref[:, at] = log_decay
            sum_ref[:, at] = inclusive
            enter_ref[:, at] = entering
            leave_ref[:, at] = leaving
            reached_ref[:, at] = reached
            faded_ref[:, at] = faded
            v16, g16 = v_ref[:, at], g_ref[:, at]
            own0 = packed(dot(v16[:HALF], faded[:HALF], TN), left)
            own1 = packed(dot(v16[HALF:], faded[HALF:], TN), left)
            pull0 = packed(dot(g16[:HALF], reached[:HALF], TN), left)
            pull1 = packed(dot(g16[HALF:], reached[HALF:], TN), left)
            end0, end1 = jnp.exp(total0), jnp.exp(total1)
            own_ref[:, at] = own0
            pull_ref[:, at] = pull1
            ends_ref[0:1, at] = end0
            ends_ref[1:2, at] = end1
            rows = slice(pair * 8, pair * 8 + 8)
            chunks = pl.ds(group * 8, 8)
            z_ref[0, chunks, rows, :] = (end1 * own0 + own1).reshape(8, 8, 128)
            z_ref[1, chunks, rows, :] = (end0 * pull1 + pull0).reshape(8, 8, 128)
            d_ref[group, pair : pair + 1, :] = jnp.exp(total0 + total1)
        d_ref[group, PAIRS:, :] = jnp.zeros((8 - PAIRS, 128), F32)

    def near_terms(group):
        wide_row = lax.broadcasted_iota(jnp.int32, (TOK, 2 * TOK), 0)
        wide_col = lax.broadcasted_iota(jnp.int32, (TOK, 2 * TOK), 1) % TOK
        wide_same = (wide_row < HALF) == (wide_col < HALF)
        beneath = wide_same & (wide_row > wide_col)
        above = wide_same & (wide_row < wide_col)
        zero = jnp.zeros((), F32)
        for pair in range(PAIRS):
            at = lanes(group, pair)
            inclusive = sum_ref[:, at]
            middle = jnp.where(
                early,
                inclusive[HALF // 2 - 1 : HALF // 2],
                inclusive[HALF + HALF // 2 - 1 : HALF + HALF // 2],
            )
            upward = jnp.exp(inclusive - log_ref[:, at] - middle)
            downward = jnp.exp(middle - inclusive)
            v16, g16 = v_ref[:, at], g_ref[:, at]
            r, k, v, g = (t[:, at].astype(F32) for t in (r_ref, k_ref, v_ref, g_ref))
            reward = vector(reward_ref, group, pair)
            up = (r * upward).astype(BF16)
            down = (k * downward).astype(BF16)
            v2, g2, up2, down2 = by_head(v16), by_head(g16), by_head(up), by_head(down)
            scores = jnp.where(beneath, dot(up, down2, NT), zero).astype(BF16)
            scores_t = jnp.where(above, dot(down, up2, NT), zero).astype(BF16)
            products = jnp.where(beneath, dot(g16, v2, NT), zero).astype(BF16)
            products_t = jnp.where(above, dot(v16, g2, NT), zero).astype(BF16)
            present = summed_over(r * reward * k, ones)
            agreement = summed_over(v * g, ones)
            mixed_near[:, at] = dot(scores, v2, NN) + present * v
            dv_near[:, at] = dot(scores_t, g2, NN) + present * g
            near_past = dot(products, down2, NN)
            near_later = dot(products_t, up2, NN)
            dr_near[:, at] = upward * near_past + reward * k * agreement
            dk_near[:, at] = downward * near_later + reward * r * agreement
            read = up.astype(F32) * near_past
            read_near[:, at] = read
            change_near[:, at] = down.astype(F32) * near_later - read
            chunk = CHIPS * (group // 2) + PAIRS * (group % 2) + pair
            wb_ref[chunk, 40:41, :] = jnp.sum(r * k * agreement, axis=0, keepdims=True)

    def far_terms(group):
        gate = gate_ref[...]
        for pair in range(PAIRS):
            at = lanes(group, pair)
            rows = slice(pair * 8, pair * 8 + 8)
            chunks = pl.ds(group * 8, 8)
            start0 = st_ref[0, chunks, rows, :].reshape(HALF, 128)
            end1 = st_ref[1, chunks, rows, :].reshape(HALF, 128)
            start1 = ends_ref[0:1, at] * start0 + own_ref[:, at]
            end0 = ends_ref[1:2, at] * end1 + pull_ref[:, at]
            lows = [t.astype(BF16) for t in (start0, start1, end0, end1)]
            for low_ref, low in zip((s0_ref, s1_ref, e0_ref, e1_ref), lows):
                low_ref[:, at] = low
            s0, s1, e0, e1 = (spread(t, left) for t in lows)
            coupling = jnp.where(
                early,
                jnp.sum(lows[2].astype(F32) * start1, axis=0, keepdims=True),
                jnp.sum(end0 * lows[1].astype(F32), axis=0, keepdims=True),
            )
            reached, faded = reached_ref[:, at], faded_ref[:, at]
            past = both(g_ref[:, at], s0, s1, NN)
            later = both(v_ref[:, at], e0, e1, NN)
            dr_ref[:, at] = (dr_near[:, at] + enter_ref[:, at] * past).astype(BF16)
            dk_ref[:, at] = (dk_near[:, at] + leave_ref[:, at] * later).astype(BF16)
            far_read = reached.astype(F32) * past
            read = read_near[:, at] + far_read
            change = change_near[:, at] + (faded.astype(F32) * later - far_read)
            slope = (coupling + summed_by(around, change, 2) - read) * log_ref[:, at]
            slope_ref[:, at] = slope.astype(BF16)
            chunk = CHIPS * (group // 2) + PAIRS * (group % 2) + pair
            wa_ref[chunk, 40:41, :] = jnp.sum(slope, axis=0, keepdims=True)
        wide = pl.ds(pl.multiple_of(group * WIDTH, 128), WIDTH)
        slopes = slope_ref[:, wide]
        acc_ref[...] += dot(slopes, b_ref[wide, :], NN)
        wb_ref[pl.ds(group * BATCH, BATCH), :40, :] = dot(slopes, gate, TN).reshape(BATCH, 40, 128)

    def swap(group):
        chunks = pl.ds(group * 8, 8)
        return pltpu.make_async_remote_copy(
            z_ref.at[other, chunks], zx_ref.at[chunks],
            swap_send.at[group], swap_recv.at[group], device_id=partner,
        )

    def swap_decay(group):
        return pltpu.make_async_remote_copy(
            d_ref.at[group], dx_decay.at[group],
            swap_send.at[GROUPS + group], swap_recv.at[GROUPS + group], device_id=partner,
        )

    for fetch in fetches[2:]:
        fetch.wait()

    @pl.loop(0, GROUPS)
    def _(group):
        states_of(group)

        @pl.when(group == 0)
        def _():
            pl.semaphore_wait(barrier, CHUNKS)

        swap_decay(group).start()
        swap(group).start()

    @pl.loop(0, GROUPS)
    def _(group):
        swap_decay(group).wait_recv()
        dc_ref[group] = d_ref[group] * dx_decay[group]
        swap(group).wait_recv()

    def out_copy(m, slot):
        return pltpu.make_async_remote_copy(
            t_ref.at[m], rec_ref.at[slot], out_send.at[m], out_recv.at[slot], device_id=peer(m)
        )

    def back_copy(n, slot):
        return pltpu.make_async_remote_copy(
            q_ref.at[n], p_ref.at[slot], back_send.at[n], back_recv.at[slot], device_id=peer(n)
        )

    def end_copy(m):
        return pltpu.make_async_remote_copy(
            y_ref.at[m], st_ref.at[core, m], end_send.at[m], end_recv.at[m], device_id=partner
        )

    def end_wait(m):
        pltpu.make_async_remote_copy(
            y_ref.at[m], st_ref.at[other, m], end_send.at[m], end_recv.at[m], device_id=partner
        ).wait_recv()

    def chip_total(m, target):
        group = m // 8
        for j in range(PAIRS):
            rows = slice(8 * j, 8 * j + 8)
            target[rows, :] = (
                dx_decay[group, j : j + 1, :] * z_ref[core, m, rows, :] + zx_ref[m, rows, :]
            )
        target[40:48, :] = dc_ref[group]

    def pick(j):
        return (2 + 3 * j + 3 * (j // 2) + 2 * (j // 3)) % 4

    def farthest(i):
        y = lax.rem(chip // 8 + pick((i // 4) % 4), 4)
        x = lax.rem((chip // 4) % 2 + 1 - i // 16, 2)
        z = lax.rem(chip % 4 + pick(i % 4), 4)
        return (y * 2 + x) * 4 + z

    @pl.loop(0, CHIPS - 1)
    def _(i):
        m = farthest(i)
        chip_total(m, t_ref.at[m])
        out_copy(m, chip).start()

    chip_total(chip, rec_ref.at[chip])

    @pl.loop(0, GROUPS - 1)
    def _(group):
        near_terms(group)

    def step(i, carry):
        n = core * (CHIPS - 1) + (1 - 2 * core) * i

        @pl.when(n != chip)
        def _():
            out_copy(n, n).wait_recv()

        after = []
        for j in range(PAIRS):
            rows = slice(8 * j, 8 * j + 8)
            q_ref[n, rows, :] = carry[j]
            after.append(rec_ref[n, 40 + j : 41 + j, :] * carry[j] + rec_ref[n, rows, :])

        @pl.when(n != chip)
        def _():
            back_copy(n, chip).start()

        return tuple(after)

    lax.fori_loop(0, CHIPS, step, tuple(jnp.zeros((8, 128), F32) for _ in range(PAIRS)))

    near_terms(GROUPS - 1)

    def finish(m, source):
        group = m // 8
        st_ref[core, m] = source[...]
        for j in range(PAIRS):
            rows = slice(8 * j, 8 * j + 8)
            y_ref[m, rows, :] = (
                d_ref[group, j : j + 1, :] * source[rows, :] + z_ref[core, m, rows, :]
            )
        end_copy(m).start()

    finish(chip, q_ref.at[chip])

    @pl.loop(1, CHIPS)
    def _(o):
        m = turn(o)
        back_copy(m, m).wait_recv()
        finish(m, p_ref.at[m])

    def give(w_ref, part):
        at = pl.ds(part * BATCH, BATCH)
        return pltpu.make_async_remote_copy(
            w_ref.at[at], wx_ref.at[at], give_send.at[part], give_recv.at[part], device_id=partner
        )

    def cast(c, slot):
        return pltpu.make_async_remote_copy(
            wt_ref.at[c], wr_ref.at[slot], cast_send.at[c], cast_recv.at[slot], device_id=owner(c)
        )

    def ship(w_ref, part):
        give(w_ref, part).wait_recv()

        @pl.loop(0, BATCH)
        def _(i):
            c = part * BATCH + lax.rem(mine + 1 + i, BATCH)
            wt_ref[c] = w_ref[c] + wx_ref[c]

            @pl.when(c != mine)
            def _():
                cast(c, mine).start()

    def rotated(i):
        return lax.rem(mine // BATCH + 1 + i, GROUPS)

    @pl.loop(0, GROUPS)
    def _(i):
        group = rotated(i)

        @pl.loop(group * 8, group * 8 + 8)
        def _(m):
            end_wait(m)

        far_terms(group)

        @pl.when(core == 0)
        def _():
            give(wb_ref, group).start()

        @pl.when((core == 1) & (i > 0))
        def _():
            ship(wb_ref, rotated(i - 1))

    smooth = smooth_ref[...]
    project = (acc_ref[...] * (1.0 - smooth * smooth)).astype(BF16)

    @pl.loop(0, GROUPS)
    def _(i):
        group = rotated(i)
        wide = pl.ds(pl.multiple_of(group * WIDTH, 128), WIDTH)
        wa_ref[pl.ds(group * BATCH, BATCH), :40, :] = dot(x_ref[:, wide], project, TN).reshape(
            BATCH, 40, 128
        )

        @pl.when(core == 1)
        def _():
            give(wa_ref, group).start()

    @pl.when(core == 1)
    def _():
        ship(wb_ref, rotated(GROUPS - 1))

    @pl.when(core == 0)
    def _():
        @pl.loop(0, GROUPS)
        def _(i):
            ship(wa_ref, rotated(i))

    @pl.loop(0, GROUPS)
    def _(group):
        wide = pl.ds(pl.multiple_of(group * WIDTH, 128), WIDTH)
        dx_ref[:, wide] = dot(project, a_ref[wide, :], NT).astype(BF16)
        outputs_of(group)

    def share(n):
        return pltpu.make_async_remote_copy(
            ws_ref, red_ref.at[core, chip], share_send.at[n], share_recv.at[chip], device_id=peer(n)
        )

    def share_wait(n):
        pltpu.make_async_remote_copy(
            ws_ref, red_ref.at[core, n], share_send.at[n], share_recv.at[n], device_id=peer(n)
        ).wait_recv()

    def last(n):
        return pltpu.make_async_remote_copy(
            red_ref.at[core, n], red_ref.at[core, n], last_send.at[n], last_recv.at[n],
            device_id=partner,
        )

    def last_wait(n):
        pltpu.make_async_remote_copy(
            red_ref.at[other, n], red_ref.at[other, n], last_send.at[n], last_recv.at[n],
            device_id=partner,
        ).wait_recv()

    def add(o, total):
        c = wide_turn(o)
        cast(c, c).wait_recv()
        return total + wr_ref[c]

    ws_ref[...] = lax.fori_loop(1, CHUNKS, add, wt_ref[mine])

    @pl.loop(0, CHIPS - 1)
    def _(i):
        share(farthest(i)).start()

    red_ref[core, chip] = ws_ref[...]
    last(chip).start()

    @pl.loop(1, CHIPS)
    def _(o):
        n = turn(o)
        share_wait(n)
        last(n).start()

    end_copy(chip).wait_send()

    @pl.loop(1, CHIPS)
    def _(o):
        m = turn(o)
        out_copy(m, chip).wait_send()
        back_copy(m, chip).wait_send()
        end_copy(m).wait_send()
        share(m).wait_send()

    @pl.loop(0, GROUPS)
    def _(group):
        swap(group).wait_send()
        swap_decay(group).wait_send()
        give(wb_ref, group).wait_send()

    @pl.loop(1, CHUNKS)
    def _(o):
        cast(wide_turn(o), mine).wait_send()

    @pl.loop(0, CHIPS)
    def _(o):
        n = turn(o)
        last_wait(n)
        last(n).wait_send()


def summed_over(x, ones):
    total = None
    for piece in split(x, 2):
        term = dot(piece, ones, NN)
        total = term if total is None else total + term
    return total


def whole_stage(x, a, r, k, v, g, b, speed, reward):
    vmem = pl.BlockSpec(memory_space=pltpu.VMEM)
    channels = x.shape[1]
    full = jax.ShapeDtypeStruct((TOK, channels), BF16)
    wide = pltpu.VMEM((TOK, channels), F32)
    short = pltpu.VMEM((TOK, channels), BF16)
    half = pltpu.VMEM((HALF, channels), F32)
    low = pltpu.VMEM((HALF, channels), BF16)
    matrix = pltpu.VMEM((channels, 128), BF16)
    vector = pltpu.VMEM((channels,), F32)
    square = pltpu.VMEM((TOK, 128), F32)
    state = pltpu.VMEM((32, 40, 128), F32)
    states = pltpu.VMEM((2, 32, 40, 128), F32)
    message = pltpu.VMEM((32, 48, 128), F32)
    decay = pltpu.VMEM((GROUPS, 8, 128), F32)
    sums = pltpu.VMEM((CHUNKS, 48, 128), F32)
    sems = pltpu.SemaphoreType.DMA
    speed, reward = (pltpu.with_memory_space_constraint(t, pltpu.HBM) for t in (speed, reward))
    x, a, r, k, v, g, b = (
        pltpu.with_memory_space_constraint(t, pltpu.HBM) for t in (x, a, r, k, v, g, b)
    )
    return pl.pallas_call(
        whole_kernel,
        in_specs=[pl.BlockSpec(memory_space=pltpu.HBM)] * 9,
        out_specs=[vmem] * 6,
        out_shape=[full] * 5 + [jax.ShapeDtypeStruct((2, CHIPS, 48, 128), F32)],
        scratch_shapes=[short, matrix, short, short, short, short, matrix, vector, vector, sems((9,))]
        + [low] * 4
        + [square, pltpu.VMEM((TOK, 128), BF16)]
        + [wide] * 4
        + [short] * 2
        + [half, half, pltpu.VMEM((8, channels), F32)]
        + [wide] * 6
        + [short, square]
        + [states, decay, state, decay, decay, message, message, state, state, state, states]
        + [sums] * 5
        + [pltpu.VMEM((48, 128), F32)]
        + [sems((2 * GROUPS,))] * 2
        + [sems((CHIPS,))] * 6
        + [sems((GROUPS,))] * 2
        + [sems((CHUNKS,))] * 2
        + [sems((CHIPS,))] * 4,
        compiler_params=pltpu.CompilerParams(
            collective_id=0, has_side_effects=True, vmem_limit_bytes=50 * 1024 * 1024
        ),
        name="whole_stage",
    )(x, a, r, k, v, g, b, speed, reward)


def emit_kernel(*refs):
    sources, red_hbm = refs[:5], refs[5]
    targets, weights = refs[6:11], refs[11:13]
    time_ref, bonus_ref, red_ref, red_sem, sem = refs[13:]
    fetches = [
        pltpu.make_async_copy(red_hbm.at[i], red_ref.at[i], red_sem.at[i]) for i in range(2)
    ]
    copies = [
        pltpu.make_async_copy(source, target, sem.at[i])
        for i, (source, target) in enumerate(zip(sources, targets))
    ]
    for copy in fetches + copies:
        copy.start()
    for i, (fetch, target) in enumerate(zip(fetches, weights)):
        fetch.wait()
        copies.append(
            pltpu.make_async_copy(red_ref.at[i, :, pl.ds(0, 40)], target, sem.at[5 + i])
        )
        copies[-1].start()
    for i in range(10):
        time_ref[pl.ds(128 * i, 128)] = red_ref[0, i, 40:41, :].reshape(128)
        bonus_ref[pl.ds(128 * i, 128)] = red_ref[1, i, 40:41, :].reshape(128)
    for copy in copies:
        copy.wait()


def emit_stage(mixed, dr, dk, dv, dx, red):
    vmem = pl.BlockSpec(memory_space=pltpu.VMEM)
    hbm = pl.BlockSpec(memory_space=pltpu.HBM)
    full = jax.ShapeDtypeStruct(mixed.shape, BF16)
    red = pltpu.with_memory_space_constraint(red, pltpu.HBM)
    return pl.pallas_call(
        emit_kernel,
        in_specs=[vmem] * 5 + [hbm],
        out_specs=[hbm] * 7 + [vmem] * 2,
        out_shape=[full] * 5
        + [jax.ShapeDtypeStruct((CHIPS, 40, 128), F32)] * 2
        + [jax.ShapeDtypeStruct((1280,), F32)] * 2,
        scratch_shapes=[
            pltpu.VMEM(red.shape, F32),
            pltpu.SemaphoreType.DMA((2,)),
            pltpu.SemaphoreType.DMA((7,)),
        ],
        compiler_params=pltpu.CompilerParams(vmem_limit_bytes=8 * 1024 * 1024),
        name="emit_stage",
    )(mixed, dr, dk, dv, dx, red)


def per_device(r, k, v, x, g, lowering, raising, speed, reward):
    r, k, v, x, g = (t[0] for t in (r, k, v, x, g))
    outs = emit_stage(*whole_stage(x, lowering, r, k, v, g, raising, speed, reward))
    lora = tuple(t.reshape(1280, 128) for t in outs[5:7])
    return tuple(t[None] for t in outs[:5]) + lora + tuple(outs[7:])


def solution(mesh):
    tokens = P("dp", "seq", None)
    return jax.shard_map(
        per_device,
        mesh=mesh,
        in_specs=(tokens,) * 5 + (P(),) * 4,
        out_specs=(tokens,) * 5 + (P("dp", None),) * 2 + (P("dp"),) * 2,
        check_vma=False,
    )
```

```python
import jax
import jax.numpy as jnp
from jax import lax
from jax.experimental import pallas as pl
from jax.experimental.pallas import tpu as pltpu
from jax.sharding import PartitionSpec as P

F32 = jnp.float32
BF16 = jnp.bfloat16
TOK = 128
HALF = 64
GROUPS = 4
PAIRS = 5
WIDTH = PAIRS * 128
CHIPS = 32
CHUNKS = 2 * CHIPS
BATCH = CHUNKS // GROUPS
NN = (((1,), (0,)), ((), ()))
NT = (((1,), (1,)), ((), ()))
TN = (((0,), (0,)), ((), ()))


def dot(a, b, dims):
    return lax.dot_general(a, b, dims, preferred_element_type=F32)


def split(x, parts):
    pieces = []
    for _ in range(parts - 1):
        head = x.astype(BF16)
        pieces.append(head)
        x = x - head.astype(F32)
    pieces.append(x.astype(BF16))
    return pieces


def summed_by(matrix, x, parts):
    total = None
    for piece in split(x, parts):
        term = dot(matrix, piece, NN)
        total = term if total is None else total + term
    return total


def grids():
    row = lax.broadcasted_iota(jnp.int32, (TOK, TOK), 0)
    col = lax.broadcasted_iota(jnp.int32, (TOK, TOK), 1)
    same = (row < HALF) == (col < HALF)
    return row, col, same


def as_matrix(condition):
    return jnp.where(condition, 1.0, 0.0).astype(BF16)


def decay_sums(gate, raising, speed, lower):
    rank = dot(gate, raising, NT)
    log_decay = -speed * jnp.exp(rank)
    inclusive = summed_by(lower, log_decay, 3)
    return (
        log_decay,
        inclusive,
        inclusive - log_decay,
        inclusive[HALF - 1 : HALF],
        inclusive[TOK - 1 : TOK],
    )


def both(lhs, first, last, dims):
    return jnp.concatenate([dot(lhs[:HALF], first, dims), dot(lhs[HALF:], last, dims)], axis=0)


def twofold(pieces, high, low):
    return dot(pieces[0], high, NN) + dot(pieces[1], high, NN) + dot(pieces[0], low, NN)


def packed(product, left):
    return jnp.where(left[:HALF], product[:HALF], product[HALF:])


def spread(state, left):
    zero = jnp.zeros_like(state)
    return jnp.concatenate(
        [jnp.where(left[:HALF], state, zero), jnp.where(left[:HALF], zero, state)], axis=0
    )


def whole_kernel(
    x_hbm, a_hbm, r_hbm, k_hbm, v_hbm, g_hbm, b_hbm, speed_hbm, reward_hbm,
    mixed_ref, dr_ref, dk_ref, dv_ref, dx_ref, red_ref,
    x_ref, a_ref, r_ref, k_ref, v_ref, g_ref, b_ref, speed_ref, reward_ref, fetch_sem,
    s0_ref, s1_ref, e0_ref, e1_ref,
    smooth_ref, gate_ref, log_ref, sum_ref, enter_ref, leave_ref, reached_ref, faded_ref,
    own_ref, pull_ref, ends_ref,
    mixed_near, dv_near, dr_near, dk_near, read_near, change_near, acc_ref,
    z_ref, d_ref, zx_ref, dx_decay, dc_ref, t_ref, rec_ref, q_ref, p_ref, y_ref, st_ref,
    wa_ref, wb_ref, wx_ref, wt_ref, wr_ref, ws_ref,
    swap_send, decay_send, out_send, back_send, end_send, give_send, cast_send, share_send,
    last_send, last_recv, swap_recv, back_recv, end_recv, give_recv, cast_recv,
):
    seq = lax.axis_index("seq")
    chip, core = seq // 2, seq % 2
    other = 1 - core
    half = lax.axis_index("dp") * CHIPS
    mine = half + chip
    partner = {"seq": chip * 2 + other}

    def peer(m):
        return {"seq": m * 2 + core}

    def owner(c):
        return {"seq": lax.rem(c, CHIPS) * 2 + core, "dp": c // CHIPS}

    def turn(o):
        return lax.rem(chip + o, CHIPS)

    def wide_turn(o):
        return lax.rem(mine + o, CHUNKS)

    fetches = [
        pltpu.make_async_copy(source, target, fetch_sem.at[i])
        for i, (source, target) in enumerate(
            (
                (x_hbm, x_ref),
                (a_hbm, a_ref),
                (b_hbm, b_ref),
                (speed_hbm, speed_ref),
                (k_hbm, k_ref),
                (r_hbm, r_ref),
                (v_hbm, v_ref),
                (g_hbm, g_ref),
                (reward_hbm, reward_ref),
            )
        )
    ]
    for fetch in fetches:
        fetch.start()

    barrier = pltpu.get_barrier_semaphore()
    pl.semaphore_signal(barrier, inc=1, device_id=partner)

    @pl.loop(1, CHUNKS)
    def _(o):
        pl.semaphore_signal(barrier, inc=1, device_id=owner(wide_turn(o)))

    row, col, same = grids()
    lower = as_matrix(same & (row >= col))
    ones = as_matrix((row < HALF) == (col < HALF))
    left = col < HALF
    early = row < HALF
    around = jnp.where(
        same & ~early & (col < row), 1.0, jnp.where(same & early & (col >= row), -1.0, 0.0)
    ).astype(BF16)

    fetches[0].wait()
    fetches[1].wait()
    smooth = jnp.tanh(dot(x_ref[...], a_ref[...], NN))
    smooth_ref[...] = smooth
    gate_ref[...] = smooth.astype(BF16)
    acc_ref[...] = jnp.zeros_like(acc_ref)
    wa_ref[:, 40:, :] = jnp.zeros((CHUNKS, 8, 128), F32)
    wb_ref[:, 40:, :] = jnp.zeros((CHUNKS, 8, 128), F32)

    def lanes(group, pair):
        return pl.ds(pl.multiple_of(group * WIDTH + pair * 128, 128), 128)

    def vector(ref, group, pair):
        return ref[lanes(group, pair)].reshape(1, 128)

    def by_head(x):
        zero = jnp.zeros_like(x)
        return jnp.concatenate([jnp.where(left, x, zero), jnp.where(left, zero, x)], axis=0)

    def outputs_of(group):
        for pair in range(PAIRS):
            at = lanes(group, pair)
            s0, s1, e0, e1 = (
                spread(ref[:, at], left) for ref in (s0_ref, s1_ref, e0_ref, e1_ref)
            )
            mixed_ref[:, at] = (
                mixed_near[:, at] + both(reached_ref[:, at], s0, s1, NT)
            ).astype(BF16)
            dv_ref[:, at] = (dv_near[:, at] + both(faded_ref[:, at], e0, e1, NT)).astype(BF16)

    def group_lanes(group):
        return pl.ds(pl.multiple_of(group * WIDTH, 128), WIDTH)

    def pair_lanes(pair):
        return slice(pair * 128, pair * 128 + 128)

    def states_of(group):
        wide = group_lanes(group)
        early_wide = lax.broadcasted_iota(jnp.int32, (TOK, WIDTH), 0) < HALF
        log_decay, inclusive, exclusive, total0, total1 = decay_sums(
            gate_ref[...], b_ref[wide, :], speed_ref[wide].reshape(1, WIDTH), lower
        )
        log_ref[:, wide] = log_decay
        sum_ref[:, wide] = inclusive
        entering = jnp.exp(exclusive)
        leaving = jnp.exp(jnp.where(early_wide, total0, total1) - inclusive)
        enter_ref[:, wide] = entering
        leave_ref[:, wide] = leaving
        reached = (r_ref[:, wide].astype(F32) * entering).astype(BF16)
        faded = (k_ref[:, wide].astype(F32) * leaving).astype(BF16)
        reached_ref[:, wide] = reached
        faded_ref[:, wide] = faded
        end0, end1 = jnp.exp(total0), jnp.exp(total1)
        ends_ref[0:1, wide] = end0
        ends_ref[1:2, wide] = end1
        decay = jnp.exp(total0 + total1)
        chunks = pl.ds(group * 8, 8)
        for pair in range(PAIRS):
            at = pair_lanes(pair)
            here = lanes(group, pair)
            v16, g16 = v_ref[:, here], g_ref[:, here]
            own0 = packed(dot(v16[:HALF], faded[:HALF, at], TN), left)
            own1 = packed(dot(v16[HALF:], faded[HALF:, at], TN), left)
            pull0 = packed(dot(g16[:HALF], reached[:HALF, at], TN), left)
            pull1 = packed(dot(g16[HALF:], reached[HALF:, at], TN), left)
            own_ref[:, here] = own0
            pull_ref[:, here] = pull1
            rows = slice(pair * 8, pair * 8 + 8)
            z_ref[0, chunks, rows, :] = (end1[:, at] * own0 + own1).reshape(8, 8, 128)
            z_ref[1, chunks, rows, :] = (end0[:, at] * pull1 + pull0).reshape(8, 8, 128)
            d_ref[group, pair : pair + 1, :] = decay[:, at]
        d_ref[group, PAIRS:, :] = jnp.zeros((8 - PAIRS, 128), F32)

    def near_terms(group):
        wide_row = lax.broadcasted_iota(jnp.int32, (TOK, 2 * TOK), 0)
        wide_col = lax.broadcasted_iota(jnp.int32, (TOK, 2 * TOK), 1) % TOK
        wide_same = (wide_row < HALF) == (wide_col < HALF)
        beneath = wide_same & (wide_row > wide_col)
        above = wide_same & (wide_row < wide_col)
        zero = jnp.zeros((), F32)
        for pair in range(PAIRS):
            at = lanes(group, pair)
            inclusive = sum_ref[:, at]
            middle = jnp.where(
                early,
                inclusive[HALF // 2 - 1 : HALF // 2],
                inclusive[HALF + HALF // 2 - 1 : HALF + HALF // 2],
            )
            upward = jnp.exp(inclusive - log_ref[:, at] - middle)
            downward = jnp.exp(middle - inclusive)
            v16, g16 = v_ref[:, at], g_ref[:, at]
            r, k, v, g = (t[:, at].astype(F32) for t in (r_ref, k_ref, v_ref, g_ref))
            reward = vector(reward_ref, group, pair)
            up, up_low = split(r * upward, 2)
            down, down_low = split(k * downward, 2)
            v2, g2, up2, down2 = by_head(v16), by_head(g16), by_head(up), by_head(down)
            scores = jnp.where(beneath, dot(up, down2, NT), zero).astype(BF16)
            scores_t = jnp.where(above, dot(down, up2, NT), zero).astype(BF16)
            products = split(jnp.where(beneath, dot(g16, v2, NT), zero), 2)
            products_t = split(jnp.where(above, dot(v16, g2, NT), zero), 2)
            present = summed_over(r * reward * k, ones)
            agreement = summed_over(v * g, ones)
            mixed_near[:, at] = dot(scores, v2, NN) + present * v
            dv_near[:, at] = dot(scores_t, g2, NN) + present * g
            near_past = twofold(products, down2, by_head(down_low))
            near_later = twofold(products_t, up2, by_head(up_low))
            dr_near[:, at] = upward * near_past + reward * k * agreement
            dk_near[:, at] = downward * near_later + reward * r * agreement
            read = (up.astype(F32) + up_low.astype(F32)) * near_past
            read_near[:, at] = read
            change_near[:, at] = (
                down.astype(F32) + down_low.astype(F32)
            ) * near_later - read
            chunk = CHIPS * (group // 2) + PAIRS * (group % 2) + pair
            wb_ref[chunk, 40:41, :] = jnp.sum(r * k * agreement, axis=0, keepdims=True)

    def far_terms(group):
        wide = group_lanes(group)
        chunks = pl.ds(group * 8, 8)
        starts, ends = [], []
        for pair in range(PAIRS):
            rows = slice(pair * 8, pair * 8 + 8)
            starts.append(st_ref[0, chunks, rows, :].reshape(HALF, 128))
            ends.append(st_ref[1, chunks, rows, :].reshape(HALF, 128))
        start0, end1 = jnp.concatenate(starts, axis=1), jnp.concatenate(ends, axis=1)
        start1 = ends_ref[0:1, wide] * start0 + own_ref[:, wide]
        end0 = ends_ref[1:2, wide] * end1 + pull_ref[:, wide]
        lows = [t.astype(BF16) for t in (start0, start1, end0, end1)]
        for low_ref, low in zip((s0_ref, s1_ref, e0_ref, e1_ref), lows):
            low_ref[:, wide] = low
        pasts, laters = [], []
        for pair in range(PAIRS):
            at = pair_lanes(pair)
            here = lanes(group, pair)
            s0, s1, e0, e1 = (spread(t[:, at], left) for t in lows)
            pasts.append(both(g_ref[:, here], s0, s1, NN))
            laters.append(both(v_ref[:, here], e0, e1, NN))
        past, later = jnp.concatenate(pasts, axis=1), jnp.concatenate(laters, axis=1)
        far_read = reached_ref[:, wide].astype(F32) * past
        change = change_near[:, wide] + (faded_ref[:, wide].astype(F32) * later - far_read)
        total = summed_by(around, change, 2)
        dr_ref[:, wide] = (dr_near[:, wide] + enter_ref[:, wide] * past).astype(BF16)
        dk_ref[:, wide] = (dk_near[:, wide] + leave_ref[:, wide] * later).astype(BF16)
        coupling = jnp.where(
            lax.broadcasted_iota(jnp.int32, (TOK, WIDTH), 0) < HALF,
            jnp.sum(lows[2].astype(F32) * start1, axis=0, keepdims=True),
            jnp.sum(end0 * lows[1].astype(F32), axis=0, keepdims=True),
        )
        slope = (coupling + total - (read_near[:, wide] + far_read)) * log_ref[:, wide]
        slopes = slope.astype(BF16)
        acc_ref[...] += dot(slopes, b_ref[wide, :], NN)
        wb_ref[pl.ds(group * BATCH, BATCH), :40, :] = dot(slopes, gate_ref[...], TN).reshape(
            BATCH, 40, 128
        )
        slope_sum = jnp.sum(slope, axis=0, keepdims=True)
        chunk = CHIPS * (group // 2) + PAIRS * (group % 2)
        for pair in range(PAIRS):
            wa_ref[chunk + pair, 40:41, :] = slope_sum[:, pair_lanes(pair)]

    def swap(group):
        chunks = pl.ds(group * 8, 8)
        return pltpu.make_async_remote_copy(
            z_ref.at[other, chunks], zx_ref.at[chunks],
            swap_send, swap_recv.at[group], device_id=partner,
        )

    def swap_decay(group):
        return pltpu.make_async_remote_copy(
            d_ref.at[group], dx_decay.at[group],
            decay_send, swap_recv.at[GROUPS + group], device_id=partner,
        )

    for fetch in fetches[2:]:
        fetch.wait()

    @pl.loop(0, GROUPS)
    def _(group):
        states_of(group)

        @pl.when(group == 0)
        def _():
            pl.semaphore_wait(barrier, CHUNKS)

        swap_decay(group).start()
        swap(group).start()

    @pl.loop(0, GROUPS)
    def _(group):
        swap_decay(group).wait_recv()
        dc_ref[group] = d_ref[group] * dx_decay[group]
        swap(group).wait_recv()

    def out_copy(m, slot):
        return pltpu.make_async_remote_copy(
            t_ref.at[m], rec_ref.at[slot], out_send, cast_recv.at[half + slot], device_id=peer(m)
        )

    def back_copy(n, slot):
        return pltpu.make_async_remote_copy(
            q_ref.at[n], p_ref.at[slot], back_send, back_recv.at[slot], device_id=peer(n)
        )

    def end_copy(m):
        return pltpu.make_async_remote_copy(
            y_ref.at[m], st_ref.at[core, m], end_send, end_recv.at[m // 8], device_id=partner
        )

    def end_wait(group):
        chunks = pl.ds(group * 8, 8)
        pltpu.make_async_remote_copy(
            y_ref.at[chunks], st_ref.at[other, chunks], end_send, end_recv.at[group],
            device_id=partner,
        ).wait_recv()

    def chip_total(m, target):
        group = m // 8
        for j in range(PAIRS):
            rows = slice(8 * j, 8 * j + 8)
            target[rows, :] = (
                dx_decay[group, j : j + 1, :] * z_ref[core, m, rows, :] + zx_ref[m, rows, :]
            )
        target[40:48, :] = dc_ref[group]

    def pick(j):
        return (2 + 3 * j + 3 * (j // 2) + 2 * (j // 3)) % 4

    def farthest(i):
        y = lax.rem(chip // 8 + pick((i // 4) % 4), 4)
        x = lax.rem((chip // 4) % 2 + 1 - i // 16, 2)
        z = lax.rem(chip % 4 + pick(i % 4), 4)
        return (y * 2 + x) * 4 + z

    @pl.loop(0, CHIPS - 1)
    def _(i):
        m = farthest(i)
        chip_total(m, t_ref.at[m])
        out_copy(m, chip).start()

    chip_total(chip, rec_ref.at[chip])

    @pl.loop(0, GROUPS - 1)
    def _(group):
        near_terms(group)

    def step(i, carry):
        n = core * (CHIPS - 1) + (1 - 2 * core) * i

        @pl.when(n != chip)
        def _():
            out_copy(n, n).wait_recv()

        after = []
        for j in range(PAIRS):
            rows = slice(8 * j, 8 * j + 8)
            q_ref[n, rows, :] = carry[j]
            after.append(rec_ref[n, 40 + j : 41 + j, :] * carry[j] + rec_ref[n, rows, :])

        @pl.when(n != chip)
        def _():
            back_copy(n, chip).start()

        return tuple(after)

    lax.fori_loop(0, CHIPS, step, tuple(jnp.zeros((8, 128), F32) for _ in range(PAIRS)))

    near_terms(GROUPS - 1)

    def finish(m, source):
        group = m // 8
        st_ref[core, m] = source[...]
        for j in range(PAIRS):
            rows = slice(8 * j, 8 * j + 8)
            y_ref[m, rows, :] = (
                d_ref[group, j : j + 1, :] * source[rows, :] + z_ref[core, m, rows, :]
            )
        end_copy(m).start()

    finish(chip, q_ref.at[chip])

    @pl.loop(1, CHIPS)
    def _(o):
        m = turn(o)
        back_copy(m, m).wait_recv()
        finish(m, p_ref.at[m])

    def give(w_ref, part):
        at = pl.ds(part * BATCH, BATCH)
        return pltpu.make_async_remote_copy(
            w_ref.at[at], wx_ref.at[at], give_send, give_recv.at[part], device_id=partner
        )

    def cast(c, slot):
        return pltpu.make_async_remote_copy(
            wt_ref.at[c], wr_ref.at[slot], cast_send, cast_recv.at[slot], device_id=owner(c)
        )

    def ship(w_ref, part):
        give(w_ref, part).wait_recv()

        @pl.loop(0, BATCH)
        def _(i):
            c = part * BATCH + lax.rem(mine + 1 + i, BATCH)
            wt_ref[c] = w_ref[c] + wx_ref[c]

            @pl.when(c != mine)
            def _():
                cast(c, mine).start()

    def rotated(i):
        return lax.rem(mine // BATCH + 1 + i, GROUPS)

    @pl.loop(0, GROUPS)
    def _(i):
        group = rotated(i)

        end_wait(group)
        far_terms(group)

        @pl.when(core == 0)
        def _():
            give(wb_ref, group).start()

        @pl.when((core == 1) & (i > 0))
        def _():
            ship(wb_ref, rotated(i - 1))

    smooth = smooth_ref[...]
    project = (acc_ref[...] * (1.0 - smooth * smooth)).astype(BF16)

    @pl.loop(0, GROUPS)
    def _(i):
        group = rotated(i)
        wide = pl.ds(pl.multiple_of(group * WIDTH, 128), WIDTH)
        wa_ref[pl.ds(group * BATCH, BATCH), :40, :] = dot(x_ref[:, wide], project, TN).reshape(
            BATCH, 40, 128
        )

        @pl.when(core == 1)
        def _():
            give(wa_ref, group).start()

    @pl.when(core == 1)
    def _():
        ship(wb_ref, rotated(GROUPS - 1))

    @pl.when(core == 0)
    def _():
        @pl.loop(0, GROUPS)
        def _(i):
            ship(wa_ref, rotated(i))

    @pl.loop(0, GROUPS)
    def _(group):
        wide = pl.ds(pl.multiple_of(group * WIDTH, 128), WIDTH)
        dx_ref[:, wide] = dot(project, a_ref[wide, :], NT).astype(BF16)
        outputs_of(group)

    def share(n):
        return pltpu.make_async_remote_copy(
            ws_ref, red_ref.at[core, chip], share_send, back_recv.at[chip], device_id=peer(n)
        )

    def share_wait(n):
        pltpu.make_async_remote_copy(
            ws_ref, red_ref.at[core, n], share_send, back_recv.at[n], device_id=peer(n)
        ).wait_recv()

    def last(n):
        return pltpu.make_async_remote_copy(
            red_ref.at[core, n], red_ref.at[core, n], last_send, last_recv, device_id=partner
        )

    def add(o, total):
        c = wide_turn(o)
        cast(c, c).wait_recv()
        return total + wr_ref[c]

    ws_ref[...] = lax.fori_loop(1, CHUNKS, add, wt_ref[mine])

    @pl.loop(0, CHIPS - 1)
    def _(i):
        share(farthest(i)).start()

    red_ref[core, chip] = ws_ref[...]
    last(chip).start()

    @pl.loop(1, CHIPS)
    def _(o):
        n = turn(o)
        share_wait(n)
        last(n).start()

    def sent(ref, sem):
        pltpu.make_async_remote_copy(ref, ref, sem, last_recv, device_id=partner).wait_send()

    sent(z_ref.at[other], swap_send)
    sent(d_ref, decay_send)
    sent(t_ref.at[pl.ds(0, CHIPS - 1)], out_send)
    sent(q_ref.at[pl.ds(0, CHIPS - 1)], back_send)
    sent(y_ref, end_send)
    sent(wb_ref, give_send)
    sent(wt_ref.at[pl.ds(0, CHUNKS - 1)], cast_send)
    sent(red_ref.at[core, pl.ds(0, CHIPS - 1)], share_send)
    sent(red_ref.at[core], last_send)
    pltpu.make_async_remote_copy(
        red_ref.at[other], red_ref.at[other], last_send, last_recv, device_id=partner
    ).wait_recv()


def summed_over(x, ones):
    total = None
    for piece in split(x, 2):
        term = dot(piece, ones, NN)
        total = term if total is None else total + term
    return total


def whole_stage(x, a, r, k, v, g, b, speed, reward):
    vmem = pl.BlockSpec(memory_space=pltpu.VMEM)
    channels = x.shape[1]
    full = jax.ShapeDtypeStruct((TOK, channels), BF16)
    wide = pltpu.VMEM((TOK, channels), F32)
    short = pltpu.VMEM((TOK, channels), BF16)
    half = pltpu.VMEM((HALF, channels), F32)
    low = pltpu.VMEM((HALF, channels), BF16)
    matrix = pltpu.VMEM((channels, 128), BF16)
    vector = pltpu.VMEM((channels,), F32)
    square = pltpu.VMEM((TOK, 128), F32)
    state = pltpu.VMEM((32, 40, 128), F32)
    states = pltpu.VMEM((2, 32, 40, 128), F32)
    message = pltpu.VMEM((32, 48, 128), F32)
    decay = pltpu.VMEM((GROUPS, 8, 128), F32)
    sums = pltpu.VMEM((CHUNKS, 48, 128), F32)
    sems = pltpu.SemaphoreType.DMA
    speed, reward = (pltpu.with_memory_space_constraint(t, pltpu.HBM) for t in (speed, reward))
    x, a, r, k, v, g, b = (
        pltpu.with_memory_space_constraint(t, pltpu.HBM) for t in (x, a, r, k, v, g, b)
    )
    return pl.pallas_call(
        whole_kernel,
        in_specs=[pl.BlockSpec(memory_space=pltpu.HBM)] * 9,
        out_specs=[vmem] * 6,
        out_shape=[full] * 5 + [jax.ShapeDtypeStruct((2, CHIPS, 48, 128), F32)],
        scratch_shapes=[short, matrix, short, short, short, short, matrix, vector, vector, sems((9,))]
        + [low] * 4
        + [square, pltpu.VMEM((TOK, 128), BF16)]
        + [wide] * 4
        + [short] * 2
        + [half, half, pltpu.VMEM((8, channels), F32)]
        + [wide] * 6
        + [square]
        + [states, decay, state, decay, decay, message, message, state, state, state, states]
        + [sums] * 5
        + [pltpu.VMEM((48, 128), F32)]
        + [sems(())] * 10
        + [sems((2 * GROUPS,)), sems((CHIPS,)), sems((GROUPS,)), sems((GROUPS,)), sems((CHUNKS,))],
        compiler_params=pltpu.CompilerParams(
            collective_id=0, has_side_effects=True, vmem_limit_bytes=50 * 1024 * 1024
        ),
        name="whole_stage",
    )(x, a, r, k, v, g, b, speed, reward)


def emit_kernel(*refs):
    sources, red_hbm = refs[:5], refs[5]
    targets, weights = refs[6:11], refs[11:13]
    time_ref, bonus_ref, red_ref, red_sem, sem = refs[13:]
    fetches = [
        pltpu.make_async_copy(red_hbm.at[i], red_ref.at[i], red_sem.at[i]) for i in range(2)
    ]
    copies = [
        pltpu.make_async_copy(source, target, sem.at[i])
        for i, (source, target) in enumerate(zip(sources, targets))
    ]
    for copy in fetches + copies:
        copy.start()
    for i, (fetch, target) in enumerate(zip(fetches, weights)):
        fetch.wait()
        copies.append(
            pltpu.make_async_copy(red_ref.at[i, :, pl.ds(0, 40)], target, sem.at[5 + i])
        )
        copies[-1].start()
    for i in range(10):
        time_ref[pl.ds(128 * i, 128)] = red_ref[0, i, 40:41, :].reshape(128)
        bonus_ref[pl.ds(128 * i, 128)] = red_ref[1, i, 40:41, :].reshape(128)
    for copy in copies:
        copy.wait()


def emit_stage(mixed, dr, dk, dv, dx, red):
    vmem = pl.BlockSpec(memory_space=pltpu.VMEM)
    hbm = pl.BlockSpec(memory_space=pltpu.HBM)
    full = jax.ShapeDtypeStruct(mixed.shape, BF16)
    red = pltpu.with_memory_space_constraint(red, pltpu.HBM)
    return pl.pallas_call(
        emit_kernel,
        in_specs=[vmem] * 5 + [hbm],
        out_specs=[hbm] * 7 + [vmem] * 2,
        out_shape=[full] * 5
        + [jax.ShapeDtypeStruct((CHIPS, 40, 128), F32)] * 2
        + [jax.ShapeDtypeStruct((1280,), F32)] * 2,
        scratch_shapes=[
            pltpu.VMEM(red.shape, F32),
            pltpu.SemaphoreType.DMA((2,)),
            pltpu.SemaphoreType.DMA((7,)),
        ],
        compiler_params=pltpu.CompilerParams(vmem_limit_bytes=8 * 1024 * 1024),
        name="emit_stage",
    )(mixed, dr, dk, dv, dx, red)


def per_device(r, k, v, x, g, lowering, raising, speed, reward):
    r, k, v, x, g = (t[0] for t in (r, k, v, x, g))
    outs = emit_stage(*whole_stage(x, lowering, r, k, v, g, raising, speed, reward))
    lora = tuple(t.reshape(1280, 128) for t in outs[5:7])
    return tuple(t[None] for t in outs[:5]) + lora + tuple(outs[7:])


def solution(mesh):
    tokens = P("dp", "seq", None)
    return jax.shard_map(
        per_device,
        mesh=mesh,
        in_specs=(tokens,) * 5 + (P(),) * 4,
        out_specs=(tokens,) * 5 + (P("dp", None),) * 2 + (P("dp"),) * 2,
        check_vma=False,
    )
```

```python
import jax
import jax.numpy as jnp
from jax import lax
from jax.experimental import pallas as pl
from jax.experimental.pallas import tpu as pltpu
from jax.sharding import PartitionSpec as P

F32 = jnp.float32
BF16 = jnp.bfloat16
TOK = 128
HALF = 64
GROUPS = 4
PAIRS = 5
WIDTH = PAIRS * 128
CHIPS = 32
CHUNKS = 2 * CHIPS
BATCH = CHUNKS // GROUPS
HOPS = (0, 1, 2, 1)
OFFSETS = sorted(
    ((y, x, z) for y in range(4) for x in range(2) for z in range(4) if y + x + z > 0),
    key=lambda step: -(HOPS[step[0]] + 2 * step[1] + HOPS[step[2]]),
)
NN = (((1,), (0,)), ((), ()))
NT = (((1,), (1,)), ((), ()))
TN = (((0,), (0,)), ((), ()))


def dot(a, b, dims):
    return lax.dot_general(a, b, dims, preferred_element_type=F32)


def split(x, parts):
    pieces = []
    for _ in range(parts - 1):
        head = x.astype(BF16)
        pieces.append(head)
        x = x - head.astype(F32)
    pieces.append(x.astype(BF16))
    return pieces


def summed_by(matrix, x, parts):
    total = None
    for piece in split(x, parts):
        term = dot(matrix, piece, NN)
        total = term if total is None else total + term
    return total


def grids():
    row = lax.broadcasted_iota(jnp.int32, (TOK, TOK), 0)
    col = lax.broadcasted_iota(jnp.int32, (TOK, TOK), 1)
    same = (row < HALF) == (col < HALF)
    return row, col, same


def as_matrix(condition):
    return jnp.where(condition, 1.0, 0.0).astype(BF16)


def decay_sums(gate, raising, speed, lower):
    rank = dot(gate, raising, NT)
    log_decay = -speed * jnp.exp(rank)
    inclusive = summed_by(lower, log_decay, 3)
    return (
        log_decay,
        inclusive,
        inclusive - log_decay,
        inclusive[HALF - 1 : HALF],
        inclusive[TOK - 1 : TOK],
    )


def both(lhs, first, last, dims):
    return jnp.concatenate([dot(lhs[:HALF], first, dims), dot(lhs[HALF:], last, dims)], axis=0)


def twofold(pieces, high, low):
    return dot(pieces[0], high, NN) + dot(pieces[1], high, NN) + dot(pieces[0], low, NN)


def packed(product, left):
    return jnp.where(left[:HALF], product[:HALF], product[HALF:])


def spread(state, left):
    zero = jnp.zeros_like(state)
    return jnp.concatenate(
        [jnp.where(left[:HALF], state, zero), jnp.where(left[:HALF], zero, state)], axis=0
    )


def whole_kernel(
    x_hbm, a_hbm, r_hbm, k_hbm, v_hbm, g_hbm, b_hbm, speed_hbm, reward_hbm,
    mixed_ref, dr_ref, dk_ref, dv_ref, dx_ref, red_ref,
    x_ref, a_ref, r_ref, k_ref, v_ref, g_ref, b_ref, speed_ref, reward_ref, fetch_sem,
    s0_ref, s1_ref, e0_ref, e1_ref,
    smooth_ref, gate_ref, log_ref, sum_ref, enter_ref, leave_ref, reached_ref, faded_ref,
    own_ref, pull_ref, ends_ref,
    mixed_near, dv_near, dr_near, dk_near, read_near, change_near, acc_ref,
    z_ref, d_ref, zx_ref, dx_decay, dc_ref, t_ref, rec_ref, q_ref, p_ref, y_ref, st_ref,
    wa_ref, wb_ref, wx_ref, wt_ref, wr_ref, ws_ref,
    swap_send, decay_send, out_send, back_send, end_send, give_send, cast_send, share_send,
    last_send, last_recv, swap_recv, back_recv, end_recv, give_recv, cast_recv,
):
    seq = lax.axis_index("seq")
    chip, core = seq // 2, seq % 2
    other = 1 - core
    half = lax.axis_index("dp") * CHIPS
    mine = half + chip
    partner = {"seq": chip * 2 + other}

    def peer(m):
        return {"seq": m * 2 + core}

    def owner(c):
        return {"seq": lax.rem(c, CHIPS) * 2 + core, "dp": c // CHIPS}

    def turn(o):
        return lax.rem(chip + o, CHIPS)

    def wide_turn(o):
        return lax.rem(mine + o, CHUNKS)

    fetches = [
        pltpu.make_async_copy(source, target, fetch_sem.at[i])
        for i, (source, target) in enumerate(
            (
                (x_hbm, x_ref),
                (a_hbm, a_ref),
                (b_hbm, b_ref),
                (speed_hbm, speed_ref),
                (k_hbm, k_ref),
                (r_hbm, r_ref),
                (v_hbm, v_ref),
                (g_hbm, g_ref),
                (reward_hbm, reward_ref),
            )
        )
    ]
    for fetch in fetches:
        fetch.start()

    barrier = pltpu.get_barrier_semaphore()
    pl.semaphore_signal(barrier, inc=1, device_id=partner)

    depths = [lax.rem(chip // 8 + d, 4) for d in range(4)]
    sides = [lax.rem(chip // 4 + d, 2) for d in range(2)]
    levels = [lax.rem(chip + d, 4) for d in range(4)]
    far_first = [(depths[y], (depths[y] * 2 + sides[x]) * 4 + levels[z]) for y, x, z in OFFSETS]

    for replica in (1 - lax.axis_index("dp"), lax.axis_index("dp")):
        for _, m in far_first:
            pl.semaphore_signal(
                barrier, inc=1, device_id={"seq": m * 2 + core, "dp": replica}
            )
    pl.semaphore_signal(
        barrier, inc=1, device_id={"dp": 1 - lax.axis_index("dp")}
    )

    row, col, same = grids()
    lower = as_matrix(same & (row >= col))
    ones = as_matrix((row < HALF) == (col < HALF))
    left = col < HALF
    early = row < HALF
    around = jnp.where(
        same & ~early & (col < row), 1.0, jnp.where(same & early & (col >= row), -1.0, 0.0)
    ).astype(BF16)

    fetches[0].wait()
    fetches[1].wait()
    smooth = jnp.tanh(dot(x_ref[...], a_ref[...], NN))
    smooth_ref[...] = smooth
    gate_ref[...] = smooth.astype(BF16)
    acc_ref[...] = jnp.zeros_like(acc_ref)
    wa_ref[:, 40:, :] = jnp.zeros((CHUNKS, 8, 128), F32)
    wb_ref[:, 40:, :] = jnp.zeros((CHUNKS, 8, 128), F32)

    def lanes(group, pair):
        return pl.ds(pl.multiple_of(group * WIDTH + pair * 128, 128), 128)

    def vector(ref, group, pair):
        return ref[lanes(group, pair)].reshape(1, 128)

    def by_head(x):
        zero = jnp.zeros_like(x)
        return jnp.concatenate([jnp.where(left, x, zero), jnp.where(left, zero, x)], axis=0)

    def outputs_of(group):
        for pair in range(PAIRS):
            at = lanes(group, pair)
            s0, s1, e0, e1 = (
                spread(ref[:, at], left) for ref in (s0_ref, s1_ref, e0_ref, e1_ref)
            )
            mixed_ref[:, at] = (
                mixed_near[:, at] + both(reached_ref[:, at], s0, s1, NT)
            ).astype(BF16)
            dv_ref[:, at] = (dv_near[:, at] + both(faded_ref[:, at], e0, e1, NT)).astype(BF16)

    def group_lanes(group):
        return pl.ds(pl.multiple_of(group * WIDTH, 128), WIDTH)

    def pair_lanes(pair):
        return slice(pair * 128, pair * 128 + 128)

    def states_of(group):
        wide = group_lanes(group)
        early_wide = lax.broadcasted_iota(jnp.int32, (TOK, WIDTH), 0) < HALF
        log_decay, inclusive, exclusive, total0, total1 = decay_sums(
            gate_ref[...], b_ref[wide, :], speed_ref[wide].reshape(1, WIDTH), lower
        )
        log_ref[:, wide] = log_decay
        sum_ref[:, wide] = inclusive
        entering = jnp.exp(exclusive)
        leaving = jnp.exp(jnp.where(early_wide, total0, total1) - inclusive)
        enter_ref[:, wide] = entering
        leave_ref[:, wide] = leaving
        reached = (r_ref[:, wide].astype(F32) * entering).astype(BF16)
        faded = (k_ref[:, wide].astype(F32) * leaving).astype(BF16)
        reached_ref[:, wide] = reached
        faded_ref[:, wide] = faded
        end0, end1 = jnp.exp(total0), jnp.exp(total1)
        ends_ref[0:1, wide] = end0
        ends_ref[1:2, wide] = end1
        decay = jnp.exp(total0 + total1)
        chunks = pl.ds(group * 8, 8)
        for pair in range(PAIRS):
            at = pair_lanes(pair)
            here = lanes(group, pair)
            v16, g16 = v_ref[:, here], g_ref[:, here]
            own0 = packed(dot(v16[:HALF], faded[:HALF, at], TN), left)
            own1 = packed(dot(v16[HALF:], faded[HALF:, at], TN), left)
            pull0 = packed(dot(g16[:HALF], reached[:HALF, at], TN), left)
            pull1 = packed(dot(g16[HALF:], reached[HALF:, at], TN), left)
            own_ref[:, here] = own0
            pull_ref[:, here] = pull1
            rows = slice(pair * 8, pair * 8 + 8)
            z_ref[0, chunks, rows, :] = (end1[:, at] * own0 + own1).reshape(8, 8, 128)
            z_ref[1, chunks, rows, :] = (end0[:, at] * pull1 + pull0).reshape(8, 8, 128)
            d_ref[group, pair : pair + 1, :] = decay[:, at]
        d_ref[group, PAIRS:, :] = jnp.zeros((8 - PAIRS, 128), F32)

    def near_terms(group):
        wide_row = lax.broadcasted_iota(jnp.int32, (TOK, 2 * TOK), 0)
        wide_col = lax.broadcasted_iota(jnp.int32, (TOK, 2 * TOK), 1) % TOK
        wide_same = (wide_row < HALF) == (wide_col < HALF)
        beneath = wide_same & (wide_row > wide_col)
        above = wide_same & (wide_row < wide_col)
        zero = jnp.zeros((), F32)
        for pair in range(PAIRS):
            at = lanes(group, pair)
            inclusive = sum_ref[:, at]
            middle = jnp.where(
                early,
                inclusive[HALF // 2 - 1 : HALF // 2],
                inclusive[HALF + HALF // 2 - 1 : HALF + HALF // 2],
            )
            upward = jnp.exp(inclusive - log_ref[:, at] - middle)
            downward = jnp.exp(middle - inclusive)
            v16, g16 = v_ref[:, at], g_ref[:, at]
            r, k, v, g = (t[:, at].astype(F32) for t in (r_ref, k_ref, v_ref, g_ref))
            reward = vector(reward_ref, group, pair)
            up, up_low = split(r * upward, 2)
            down, down_low = split(k * downward, 2)
            v2, g2, up2, down2 = by_head(v16), by_head(g16), by_head(up), by_head(down)
            scores = jnp.where(beneath, dot(up, down2, NT), zero).astype(BF16)
            scores_t = jnp.where(above, dot(down, up2, NT), zero).astype(BF16)
            products = split(jnp.where(beneath, dot(g16, v2, NT), zero), 2)
            products_t = split(jnp.where(above, dot(v16, g2, NT), zero), 2)
            present = summed_over(r * reward * k, ones)
            agreement = summed_over(v * g, ones)
            mixed_near[:, at] = dot(scores, v2, NN) + present * v
            dv_near[:, at] = dot(scores_t, g2, NN) + present * g
            near_past = twofold(products, down2, by_head(down_low))
            near_later = twofold(products_t, up2, by_head(up_low))
            dr_near[:, at] = upward * near_past + reward * k * agreement
            dk_near[:, at] = downward * near_later + reward * r * agreement
            read = (up.astype(F32) + up_low.astype(F32)) * near_past
            read_near[:, at] = read
            change_near[:, at] = (
                down.astype(F32) + down_low.astype(F32)
            ) * near_later - read
            chunk = CHIPS * (group // 2) + PAIRS * (group % 2) + pair
            wb_ref[chunk, 40:41, :] = jnp.sum(r * k * agreement, axis=0, keepdims=True)

    def far_terms(group):
        wide = group_lanes(group)
        chunks = pl.ds(group * 8, 8)
        starts, ends = [], []
        for pair in range(PAIRS):
            rows = slice(pair * 8, pair * 8 + 8)
            starts.append(st_ref[0, chunks, rows, :].reshape(HALF, 128))
            ends.append(st_ref[1, chunks, rows, :].reshape(HALF, 128))
        start0, end1 = jnp.concatenate(starts, axis=1), jnp.concatenate(ends, axis=1)
        start1 = ends_ref[0:1, wide] * start0 + own_ref[:, wide]
        end0 = ends_ref[1:2, wide] * end1 + pull_ref[:, wide]
        lows = [t.astype(BF16) for t in (start0, start1, end0, end1)]
        for low_ref, low in zip((s0_ref, s1_ref, e0_ref, e1_ref), lows):
            low_ref[:, wide] = low
        pasts, laters = [], []
        for pair in range(PAIRS):
            at = pair_lanes(pair)
            here = lanes(group, pair)
            s0, s1, e0, e1 = (spread(t[:, at], left) for t in lows)
            pasts.append(both(g_ref[:, here], s0, s1, NN))
            laters.append(both(v_ref[:, here], e0, e1, NN))
        past, later = jnp.concatenate(pasts, axis=1), jnp.concatenate(laters, axis=1)
        far_read = reached_ref[:, wide].astype(F32) * past
        change = change_near[:, wide] + (faded_ref[:, wide].astype(F32) * later - far_read)
        total = summed_by(around, change, 2)
        dr_ref[:, wide] = (dr_near[:, wide] + enter_ref[:, wide] * past).astype(BF16)
        dk_ref[:, wide] = (dk_near[:, wide] + leave_ref[:, wide] * later).astype(BF16)
        coupling = jnp.where(
            lax.broadcasted_iota(jnp.int32, (TOK, WIDTH), 0) < HALF,
            jnp.sum(lows[2].astype(F32) * start1, axis=0, keepdims=True),
            jnp.sum(end0 * lows[1].astype(F32), axis=0, keepdims=True),
        )
        slope = (coupling + total - (read_near[:, wide] + far_read)) * log_ref[:, wide]
        slopes = slope.astype(BF16)
        acc_ref[...] += dot(slopes, b_ref[wide, :], NN)
        wb_ref[pl.ds(group * BATCH, BATCH), :40, :] = dot(slopes, gate_ref[...], TN).reshape(
            BATCH, 40, 128
        )
        slope_sum = jnp.sum(slope, axis=0, keepdims=True)
        chunk = CHIPS * (group // 2) + PAIRS * (group % 2)
        for pair in range(PAIRS):
            wa_ref[chunk + pair, 40:41, :] = slope_sum[:, pair_lanes(pair)]

    def swap(group):
        chunks = pl.ds(group * 8, 8)
        return pltpu.make_async_remote_copy(
            z_ref.at[other, chunks], zx_ref.at[chunks],
            swap_send, swap_recv.at[group], device_id=partner,
        )

    def swap_decay(group):
        return pltpu.make_async_remote_copy(
            d_ref.at[group], dx_decay.at[group],
            decay_send, swap_recv.at[GROUPS + group], device_id=partner,
        )

    for fetch in fetches[2:]:
        fetch.wait()

    @pl.loop(0, GROUPS)
    def _(group):
        states_of(group)

        @pl.when(group == 0)
        def _():
            pl.semaphore_wait(barrier, CHUNKS)

        swap_decay(group).start()
        swap(group).start()

    @pl.loop(0, GROUPS)
    def _(group):
        swap_decay(group).wait_recv()
        dc_ref[group] = d_ref[group] * dx_decay[group]
        swap(group).wait_recv()

    def out_copy(m, slot):
        return pltpu.make_async_remote_copy(
            t_ref.at[m], rec_ref.at[slot], out_send, cast_recv.at[half + slot], device_id=peer(m)
        )

    def back_copy(n, slot):
        return pltpu.make_async_remote_copy(
            q_ref.at[n], p_ref.at[slot], back_send, back_recv.at[slot], device_id=peer(n)
        )

    def end_copy(m):
        return pltpu.make_async_remote_copy(
            y_ref.at[m], st_ref.at[core, m], end_send, end_recv.at[m // 8], device_id=partner
        )

    def end_wait(group):
        chunks = pl.ds(group * 8, 8)
        pltpu.make_async_remote_copy(
            y_ref.at[chunks], st_ref.at[other, chunks], end_send, end_recv.at[group],
            device_id=partner,
        ).wait_recv()

    def chip_total(m, group, target):
        for j in range(PAIRS):
            rows = slice(8 * j, 8 * j + 8)
            target[rows, :] = (
                dx_decay[group, j : j + 1, :] * z_ref[core, m, rows, :] + zx_ref[m, rows, :]
            )
        target[40:48, :] = dc_ref[group]

    for depth, m in far_first:
        chip_total(m, depth, t_ref.at[m])
        out_copy(m, chip).start()

    chip_total(chip, depths[0], rec_ref.at[chip])

    @pl.loop(0, GROUPS - 1)
    def _(group):
        near_terms(group)

    def step(i, carry):
        n = core * (CHIPS - 1) + (1 - 2 * core) * i

        @pl.when(n != chip)
        def _():
            out_copy(n, n).wait_recv()

        after = []
        for j in range(PAIRS):
            rows = slice(8 * j, 8 * j + 8)
            q_ref[n, rows, :] = carry[j]
            after.append(rec_ref[n, 40 + j : 41 + j, :] * carry[j] + rec_ref[n, rows, :])

        @pl.when(n != chip)
        def _():
            back_copy(n, chip).start()

        return tuple(after)

    lax.fori_loop(0, CHIPS, step, tuple(jnp.zeros((8, 128), F32) for _ in range(PAIRS)))

    near_terms(GROUPS - 1)

    def finish(m, source):
        group = m // 8
        st_ref[core, m] = source[...]
        for j in range(PAIRS):
            rows = slice(8 * j, 8 * j + 8)
            y_ref[m, rows, :] = (
                d_ref[group, j : j + 1, :] * source[rows, :] + z_ref[core, m, rows, :]
            )
        end_copy(m).start()

    finish(chip, q_ref.at[chip])

    @pl.loop(1, CHIPS)
    def _(o):
        m = turn(o)
        back_copy(m, m).wait_recv()
        finish(m, p_ref.at[m])

    def give(w_ref, part):
        at = pl.ds(part * BATCH, BATCH)
        return pltpu.make_async_remote_copy(
            w_ref.at[at], wx_ref.at[at], give_send, give_recv.at[part], device_id=partner
        )

    def cast(c, slot):
        return pltpu.make_async_remote_copy(
            wt_ref.at[c], wr_ref.at[slot], cast_send, cast_recv.at[slot], device_id=owner(c)
        )

    def ship(w_ref, part):
        give(w_ref, part).wait_recv()

        @pl.loop(0, BATCH)
        def _(i):
            c = part * BATCH + lax.rem(mine + 1 + i, BATCH)
            wt_ref[c] = w_ref[c] + wx_ref[c]

            @pl.when(c != mine)
            def _():
                cast(c, mine).start()

    def rotated(i):
        return lax.rem(mine // BATCH + 1 + i, GROUPS)

    @pl.loop(0, GROUPS)
    def _(i):
        group = rotated(i)

        end_wait(group)
        far_terms(group)

        @pl.when(core == 0)
        def _():
            give(wb_ref, group).start()

        @pl.when((core == 1) & (i > 0))
        def _():
            ship(wb_ref, rotated(i - 1))

    smooth = smooth_ref[...]
    project = (acc_ref[...] * (1.0 - smooth * smooth)).astype(BF16)

    @pl.loop(0, GROUPS)
    def _(i):
        group = rotated(i)
        wide = pl.ds(pl.multiple_of(group * WIDTH, 128), WIDTH)
        wa_ref[pl.ds(group * BATCH, BATCH), :40, :] = dot(x_ref[:, wide], project, TN).reshape(
            BATCH, 40, 128
        )

        @pl.when(core == 1)
        def _():
            give(wa_ref, group).start()

    @pl.when(core == 1)
    def _():
        ship(wb_ref, rotated(GROUPS - 1))

    @pl.when(core == 0)
    def _():
        @pl.loop(0, GROUPS)
        def _(i):
            ship(wa_ref, rotated(i))

    @pl.loop(0, GROUPS)
    def _(group):
        wide = pl.ds(pl.multiple_of(group * WIDTH, 128), WIDTH)
        dx_ref[:, wide] = dot(project, a_ref[wide, :], NT).astype(BF16)
        outputs_of(group)

    def share(n):
        return pltpu.make_async_remote_copy(
            ws_ref, red_ref.at[core, chip], share_send, back_recv.at[chip], device_id=peer(n)
        )

    def share_wait(n):
        pltpu.make_async_remote_copy(
            ws_ref, red_ref.at[core, n], share_send, back_recv.at[n], device_id=peer(n)
        ).wait_recv()

    def last(n):
        return pltpu.make_async_remote_copy(
            red_ref.at[core, n], red_ref.at[core, n], last_send, last_recv, device_id=partner
        )

    def add(o, total):
        c = wide_turn(o)
        cast(c, c).wait_recv()
        return total + wr_ref[c]

    ws_ref[...] = lax.fori_loop(1, CHUNKS, add, wt_ref[mine])

    for _, m in far_first:
        share(m).start()

    red_ref[core, chip] = ws_ref[...]
    last(chip).start()

    @pl.loop(1, CHIPS)
    def _(o):
        n = turn(o)
        share_wait(n)
        last(n).start()

    def sent(ref, sem):
        pltpu.make_async_remote_copy(ref, ref, sem, last_recv, device_id=partner).wait_send()

    sent(z_ref.at[other], swap_send)
    sent(d_ref, decay_send)
    sent(t_ref.at[pl.ds(0, CHIPS - 1)], out_send)
    sent(q_ref.at[pl.ds(0, CHIPS - 1)], back_send)
    sent(y_ref, end_send)
    sent(wb_ref, give_send)
    sent(wt_ref.at[pl.ds(0, CHUNKS - 1)], cast_send)
    sent(red_ref.at[core, pl.ds(0, CHIPS - 1)], share_send)
    sent(red_ref.at[core], last_send)
    pltpu.make_async_remote_copy(
        red_ref.at[other], red_ref.at[other], last_send, last_recv, device_id=partner
    ).wait_recv()


def summed_over(x, ones):
    total = None
    for piece in split(x, 2):
        term = dot(piece, ones, NN)
        total = term if total is None else total + term
    return total


def whole_stage(x, a, r, k, v, g, b, speed, reward):
    vmem = pl.BlockSpec(memory_space=pltpu.VMEM)
    channels = x.shape[1]
    full = jax.ShapeDtypeStruct((TOK, channels), BF16)
    wide = pltpu.VMEM((TOK, channels), F32)
    short = pltpu.VMEM((TOK, channels), BF16)
    half = pltpu.VMEM((HALF, channels), F32)
    low = pltpu.VMEM((HALF, channels), BF16)
    matrix = pltpu.VMEM((channels, 128), BF16)
    vector = pltpu.VMEM((channels,), F32)
    square = pltpu.VMEM((TOK, 128), F32)
    state = pltpu.VMEM((32, 40, 128), F32)
    states = pltpu.VMEM((2, 32, 40, 128), F32)
    message = pltpu.VMEM((32, 48, 128), F32)
    decay = pltpu.VMEM((GROUPS, 8, 128), F32)
    sums = pltpu.VMEM((CHUNKS, 48, 128), F32)
    sems = pltpu.SemaphoreType.DMA
    speed, reward = (pltpu.with_memory_space_constraint(t, pltpu.HBM) for t in (speed, reward))
    x, a, r, k, v, g, b = (
        pltpu.with_memory_space_constraint(t, pltpu.HBM) for t in (x, a, r, k, v, g, b)
    )
    return pl.pallas_call(
        whole_kernel,
        in_specs=[pl.BlockSpec(memory_space=pltpu.HBM)] * 9,
        out_specs=[vmem] * 6,
        out_shape=[full] * 5 + [jax.ShapeDtypeStruct((2, CHIPS, 48, 128), F32)],
        scratch_shapes=[short, matrix, short, short, short, short, matrix, vector, vector, sems((9,))]
        + [low] * 4
        + [square, pltpu.VMEM((TOK, 128), BF16)]
        + [wide] * 4
        + [short] * 2
        + [half, half, pltpu.VMEM((8, channels), F32)]
        + [wide] * 6
        + [square]
        + [states, decay, state, decay, decay, message, message, state, state, state, states]
        + [sums] * 5
        + [pltpu.VMEM((48, 128), F32)]
        + [sems(())] * 10
        + [sems((2 * GROUPS,)), sems((CHIPS,)), sems((GROUPS,)), sems((GROUPS,)), sems((CHUNKS,))],
        compiler_params=pltpu.CompilerParams(
            collective_id=0, has_side_effects=True, vmem_limit_bytes=50 * 1024 * 1024
        ),
        name="whole_stage",
    )(x, a, r, k, v, g, b, speed, reward)


def emit_kernel(*refs):
    sources, red_hbm = refs[:5], refs[5]
    targets, weights = refs[6:11], refs[11:13]
    time_ref, bonus_ref, red_ref, red_sem, sem = refs[13:]
    fetches = [
        pltpu.make_async_copy(red_hbm.at[i], red_ref.at[i], red_sem.at[i]) for i in range(2)
    ]
    copies = [
        pltpu.make_async_copy(source, target, sem.at[i])
        for i, (source, target) in enumerate(zip(sources, targets))
    ]
    for copy in fetches + copies:
        copy.start()
    for i, (fetch, target) in enumerate(zip(fetches, weights)):
        fetch.wait()
        copies.append(
            pltpu.make_async_copy(red_ref.at[i, :, pl.ds(0, 40)], target, sem.at[5 + i])
        )
        copies[-1].start()
    for i in range(10):
        time_ref[pl.ds(128 * i, 128)] = red_ref[0, i, 40:41, :].reshape(128)
        bonus_ref[pl.ds(128 * i, 128)] = red_ref[1, i, 40:41, :].reshape(128)
    for copy in copies:
        copy.wait()


def emit_stage(mixed, dr, dk, dv, dx, red):
    vmem = pl.BlockSpec(memory_space=pltpu.VMEM)
    hbm = pl.BlockSpec(memory_space=pltpu.HBM)
    full = jax.ShapeDtypeStruct(mixed.shape, BF16)
    red = pltpu.with_memory_space_constraint(red, pltpu.HBM)
    return pl.pallas_call(
        emit_kernel,
        in_specs=[vmem] * 5 + [hbm],
        out_specs=[hbm] * 7 + [vmem] * 2,
        out_shape=[full] * 5
        + [jax.ShapeDtypeStruct((CHIPS, 40, 128), F32)] * 2
        + [jax.ShapeDtypeStruct((1280,), F32)] * 2,
        scratch_shapes=[
            pltpu.VMEM(red.shape, F32),
            pltpu.SemaphoreType.DMA((2,)),
            pltpu.SemaphoreType.DMA((7,)),
        ],
        compiler_params=pltpu.CompilerParams(vmem_limit_bytes=8 * 1024 * 1024),
        name="emit_stage",
    )(mixed, dr, dk, dv, dx, red)


def per_device(r, k, v, x, g, lowering, raising, speed, reward):
    r, k, v, x, g = (t[0] for t in (r, k, v, x, g))
    outs = emit_stage(*whole_stage(x, lowering, r, k, v, g, raising, speed, reward))
    lora = tuple(t.reshape(1280, 128) for t in outs[5:7])
    return tuple(t[None] for t in outs[:5]) + lora + tuple(outs[7:])


def solution(mesh):
    tokens = P("dp", "seq", None)
    return jax.shard_map(
        per_device,
        mesh=mesh,
        in_specs=(tokens,) * 5 + (P(),) * 4,
        out_specs=(tokens,) * 5 + (P("dp", None),) * 2 + (P("dp"),) * 2,
        check_vma=False,
    )
```

```python
import jax
import jax.numpy as jnp
from jax import lax
from jax.experimental import pallas as pl
from jax.experimental.pallas import tpu as pltpu
from jax.sharding import PartitionSpec as P

F32 = jnp.float32
BF16 = jnp.bfloat16
TOK = 128
HALF = 64
GROUPS = 4
PAIRS = 5
WIDTH = PAIRS * 128
CHIPS = 32
CHUNKS = 2 * CHIPS
BATCH = CHUNKS // GROUPS
HOPS = (0, 1, 2, 1)
OFFSETS = sorted(
    ((y, x, z) for y in range(4) for x in range(2) for z in range(4) if y + x + z > 0),
    key=lambda step: -(HOPS[step[0]] + 2 * step[1] + HOPS[step[2]]),
)
NN = (((1,), (0,)), ((), ()))
NT = (((1,), (1,)), ((), ()))
TN = (((0,), (0,)), ((), ()))


def dot(a, b, dims):
    return lax.dot_general(a, b, dims, preferred_element_type=F32)


def split(x, parts):
    pieces = []
    for _ in range(parts - 1):
        head = x.astype(BF16)
        pieces.append(head)
        x = x - head.astype(F32)
    pieces.append(x.astype(BF16))
    return pieces


def summed_by(matrix, x, parts):
    total = None
    for piece in split(x, parts):
        term = dot(matrix, piece, NN)
        total = term if total is None else total + term
    return total


def grids():
    row = lax.broadcasted_iota(jnp.int32, (TOK, TOK), 0)
    col = lax.broadcasted_iota(jnp.int32, (TOK, TOK), 1)
    same = (row < HALF) == (col < HALF)
    return row, col, same


def as_matrix(condition):
    return jnp.where(condition, 1.0, 0.0).astype(BF16)


def decay_sums(gate, raising, speed, lower):
    rank = dot(gate, raising, NT)
    log_decay = -speed * jnp.exp(rank)
    inclusive = summed_by(lower, log_decay, 3)
    return (
        log_decay,
        inclusive,
        inclusive - log_decay,
        inclusive[HALF - 1 : HALF],
        inclusive[TOK - 1 : TOK],
    )


def both(lhs, first, last, dims):
    return jnp.concatenate([dot(lhs[:HALF], first, dims), dot(lhs[HALF:], last, dims)], axis=0)


def twofold(pieces, high, low):
    return dot(pieces[0], high, NN) + dot(pieces[1], high, NN) + dot(pieces[0], low, NN)


def packed(product, left):
    return jnp.where(left[:HALF], product[:HALF], product[HALF:])


def spread(state, left):
    zero = jnp.zeros_like(state)
    return jnp.concatenate(
        [jnp.where(left[:HALF], state, zero), jnp.where(left[:HALF], zero, state)], axis=0
    )


def whole_kernel(
    x_hbm, a_hbm, r_hbm, k_hbm, v_hbm, g_hbm, b_hbm, speed_hbm, reward_hbm,
    mixed_ref, dr_ref, dk_ref, dv_ref, dx_ref, red_ref,
    x_ref, a_ref, r_ref, k_ref, v_ref, g_ref, b_ref, speed_ref, reward_ref, fetch_sem,
    s0_ref, s1_ref, e0_ref, e1_ref,
    smooth_ref, gate_ref, log_ref, sum_ref, enter_ref, leave_ref, reached_ref, faded_ref,
    own_ref, pull_ref, ends_ref,
    mixed_near, dv_near, dr_near, dk_near, read_near, change_near, acc_ref,
    z_ref, d_ref, zx_ref, dx_decay, dc_ref, t_ref, rec_ref, q_ref, p_ref, y_ref, st_ref,
    wa_ref, wb_ref, wx_ref, wt_ref, wr_ref, ws_ref,
    swap_send, decay_send, out_send, back_send, end_send, give_send, cast_send, share_send,
    last_send, last_recv, swap_recv, back_recv, end_recv, give_recv, cast_recv,
):
    seq = lax.axis_index("seq")
    chip, core = seq // 2, seq % 2
    other = 1 - core
    half = lax.axis_index("dp") * CHIPS
    mine = half + chip
    partner = {"seq": chip * 2 + other}

    def peer(m):
        return {"seq": m * 2 + core}

    def turn(o):
        return lax.rem(chip + o, CHIPS)

    def wide_turn(o):
        return lax.rem(mine + o, CHUNKS)

    fetches = [
        pltpu.make_async_copy(source, target, fetch_sem.at[i])
        for i, (source, target) in enumerate(
            (
                (x_hbm, x_ref),
                (a_hbm, a_ref),
                (b_hbm, b_ref),
                (speed_hbm, speed_ref),
                (k_hbm, k_ref),
                (r_hbm, r_ref),
                (v_hbm, v_ref),
                (g_hbm, g_ref),
                (reward_hbm, reward_ref),
            )
        )
    ]
    for fetch in fetches:
        fetch.start()

    barrier = pltpu.get_barrier_semaphore()
    pl.semaphore_signal(barrier, inc=1, device_id=partner)

    depths = [lax.rem(chip // 8 + d, 4) for d in range(4)]
    sides = [lax.rem(chip // 4 + d, 2) for d in range(2)]
    levels = [lax.rem(chip + d, 4) for d in range(4)]
    far_first = [(depths[y], (depths[y] * 2 + sides[x]) * 4 + levels[z]) for y, x, z in OFFSETS]

    for replica in (1 - lax.axis_index("dp"), lax.axis_index("dp")):
        for _, m in far_first:
            pl.semaphore_signal(
                barrier, inc=1, device_id={"seq": m * 2 + core, "dp": replica}
            )
    pl.semaphore_signal(
        barrier, inc=1, device_id={"dp": 1 - lax.axis_index("dp")}
    )

    row, col, same = grids()
    lower = as_matrix(same & (row >= col))
    ones = as_matrix((row < HALF) == (col < HALF))
    left = col < HALF
    early = row < HALF
    around = jnp.where(
        same & ~early & (col < row), 1.0, jnp.where(same & early & (col >= row), -1.0, 0.0)
    ).astype(BF16)

    fetches[0].wait()
    fetches[1].wait()
    smooth = jnp.tanh(dot(x_ref[...], a_ref[...], NN))
    smooth_ref[...] = smooth
    gate_ref[...] = smooth.astype(BF16)
    acc_ref[...] = jnp.zeros_like(acc_ref)
    wa_ref[:, 40:, :] = jnp.zeros((CHUNKS, 8, 128), F32)
    wb_ref[:, 40:, :] = jnp.zeros((CHUNKS, 8, 128), F32)

    def lanes(group, pair):
        return pl.ds(pl.multiple_of(group * WIDTH + pair * 128, 128), 128)

    def vector(ref, group, pair):
        return ref[lanes(group, pair)].reshape(1, 128)

    def by_head(x):
        zero = jnp.zeros_like(x)
        return jnp.concatenate([jnp.where(left, x, zero), jnp.where(left, zero, x)], axis=0)

    def outputs_of(group):
        for pair in range(PAIRS):
            at = lanes(group, pair)
            s0, s1, e0, e1 = (
                spread(ref[:, at], left) for ref in (s0_ref, s1_ref, e0_ref, e1_ref)
            )
            mixed_ref[:, at] = (
                mixed_near[:, at] + both(reached_ref[:, at], s0, s1, NT)
            ).astype(BF16)
            dv_ref[:, at] = (dv_near[:, at] + both(faded_ref[:, at], e0, e1, NT)).astype(BF16)

    def group_lanes(group):
        return pl.ds(pl.multiple_of(group * WIDTH, 128), WIDTH)

    def pair_lanes(pair):
        return slice(pair * 128, pair * 128 + 128)

    def states_of(group):
        wide = group_lanes(group)
        early_wide = lax.broadcasted_iota(jnp.int32, (TOK, WIDTH), 0) < HALF
        log_decay, inclusive, exclusive, total0, total1 = decay_sums(
            gate_ref[...], b_ref[wide, :], speed_ref[wide].reshape(1, WIDTH), lower
        )
        log_ref[:, wide] = log_decay
        sum_ref[:, wide] = inclusive
        entering = jnp.exp(exclusive)
        leaving = jnp.exp(jnp.where(early_wide, total0, total1) - inclusive)
        enter_ref[:, wide] = entering
        leave_ref[:, wide] = leaving
        reached = (r_ref[:, wide].astype(F32) * entering).astype(BF16)
        faded = (k_ref[:, wide].astype(F32) * leaving).astype(BF16)
        reached_ref[:, wide] = reached
        faded_ref[:, wide] = faded
        end0, end1 = jnp.exp(total0), jnp.exp(total1)
        ends_ref[0:1, wide] = end0
        ends_ref[1:2, wide] = end1
        decay = jnp.exp(total0 + total1)
        chunks = pl.ds(group * 8, 8)
        for pair in range(PAIRS):
            at = pair_lanes(pair)
            here = lanes(group, pair)
            v16, g16 = v_ref[:, here], g_ref[:, here]
            own0 = packed(dot(v16[:HALF], faded[:HALF, at], TN), left)
            own1 = packed(dot(v16[HALF:], faded[HALF:, at], TN), left)
            pull0 = packed(dot(g16[:HALF], reached[:HALF, at], TN), left)
            pull1 = packed(dot(g16[HALF:], reached[HALF:, at], TN), left)
            own_ref[:, here] = own0
            pull_ref[:, here] = pull1
            rows = slice(pair * 8, pair * 8 + 8)
            z_ref[0, chunks, rows, :] = (end1[:, at] * own0 + own1).reshape(8, 8, 128)
            z_ref[1, chunks, rows, :] = (end0[:, at] * pull1 + pull0).reshape(8, 8, 128)
            d_ref[group, pair : pair + 1, :] = decay[:, at]
        d_ref[group, PAIRS:, :] = jnp.zeros((8 - PAIRS, 128), F32)

    def near_terms(group):
        wide_row = lax.broadcasted_iota(jnp.int32, (TOK, 2 * TOK), 0)
        wide_col = lax.broadcasted_iota(jnp.int32, (TOK, 2 * TOK), 1) % TOK
        wide_same = (wide_row < HALF) == (wide_col < HALF)
        beneath = wide_same & (wide_row > wide_col)
        above = wide_same & (wide_row < wide_col)
        zero = jnp.zeros((), F32)
        for pair in range(PAIRS):
            at = lanes(group, pair)
            inclusive = sum_ref[:, at]
            middle = jnp.where(
                early,
                inclusive[HALF // 2 - 1 : HALF // 2],
                inclusive[HALF + HALF // 2 - 1 : HALF + HALF // 2],
            )
            upward = jnp.exp(inclusive - log_ref[:, at] - middle)
            downward = jnp.exp(middle - inclusive)
            v16, g16 = v_ref[:, at], g_ref[:, at]
            r, k, v, g = (t[:, at].astype(F32) for t in (r_ref, k_ref, v_ref, g_ref))
            reward = vector(reward_ref, group, pair)
            up, up_low = split(r * upward, 2)
            down, down_low = split(k * downward, 2)
            v2, g2, up2, down2 = by_head(v16), by_head(g16), by_head(up), by_head(down)
            scores = jnp.where(beneath, dot(up, down2, NT), zero).astype(BF16)
            scores_t = jnp.where(above, dot(down, up2, NT), zero).astype(BF16)
            products = split(jnp.where(beneath, dot(g16, v2, NT), zero), 2)
            products_t = split(jnp.where(above, dot(v16, g2, NT), zero), 2)
            present = summed_over(r * reward * k, ones)
            agreement = summed_over(v * g, ones)
            mixed_near[:, at] = dot(scores, v2, NN) + present * v
            dv_near[:, at] = dot(scores_t, g2, NN) + present * g
            near_past = twofold(products, down2, by_head(down_low))
            near_later = twofold(products_t, up2, by_head(up_low))
            dr_near[:, at] = upward * near_past + reward * k * agreement
            dk_near[:, at] = downward * near_later + reward * r * agreement
            read = (up.astype(F32) + up_low.astype(F32)) * near_past
            read_near[:, at] = read
            change_near[:, at] = (
                down.astype(F32) + down_low.astype(F32)
            ) * near_later - read
            chunk = CHIPS * (group // 2) + PAIRS * (group % 2) + pair
            wb_ref[chunk, 40:41, :] = jnp.sum(r * k * agreement, axis=0, keepdims=True)

    def far_terms(group):
        wide = group_lanes(group)
        chunks = pl.ds(group * 8, 8)
        starts, ends = [], []
        for pair in range(PAIRS):
            rows = slice(pair * 8, pair * 8 + 8)
            starts.append(st_ref[0, chunks, rows, :].reshape(HALF, 128))
            ends.append(st_ref[1, chunks, rows, :].reshape(HALF, 128))
        start0, end1 = jnp.concatenate(starts, axis=1), jnp.concatenate(ends, axis=1)
        start1 = ends_ref[0:1, wide] * start0 + own_ref[:, wide]
        end0 = ends_ref[1:2, wide] * end1 + pull_ref[:, wide]
        lows = [t.astype(BF16) for t in (start0, start1, end0, end1)]
        for low_ref, low in zip((s0_ref, s1_ref, e0_ref, e1_ref), lows):
            low_ref[:, wide] = low
        pasts, laters = [], []
        for pair in range(PAIRS):
            at = pair_lanes(pair)
            here = lanes(group, pair)
            s0, s1, e0, e1 = (spread(t[:, at], left) for t in lows)
            pasts.append(both(g_ref[:, here], s0, s1, NN))
            laters.append(both(v_ref[:, here], e0, e1, NN))
        past, later = jnp.concatenate(pasts, axis=1), jnp.concatenate(laters, axis=1)
        far_read = reached_ref[:, wide].astype(F32) * past
        change = change_near[:, wide] + (faded_ref[:, wide].astype(F32) * later - far_read)
        total = summed_by(around, change, 2)
        dr_ref[:, wide] = (dr_near[:, wide] + enter_ref[:, wide] * past).astype(BF16)
        dk_ref[:, wide] = (dk_near[:, wide] + leave_ref[:, wide] * later).astype(BF16)
        coupling = jnp.where(
            lax.broadcasted_iota(jnp.int32, (TOK, WIDTH), 0) < HALF,
            jnp.sum(lows[2].astype(F32) * start1, axis=0, keepdims=True),
            jnp.sum(end0 * lows[1].astype(F32), axis=0, keepdims=True),
        )
        slope = (coupling + total - (read_near[:, wide] + far_read)) * log_ref[:, wide]
        slopes = slope.astype(BF16)
        acc_ref[...] += dot(slopes, b_ref[wide, :], NN)
        wb_ref[pl.ds(group * BATCH, BATCH), :40, :] = dot(slopes, gate_ref[...], TN).reshape(
            BATCH, 40, 128
        )
        slope_sum = jnp.sum(slope, axis=0, keepdims=True)
        chunk = CHIPS * (group // 2) + PAIRS * (group % 2)
        for pair in range(PAIRS):
            wa_ref[chunk + pair, 40:41, :] = slope_sum[:, pair_lanes(pair)]

    def swap(group):
        chunks = pl.ds(group * 8, 8)
        return pltpu.make_async_remote_copy(
            z_ref.at[other, chunks], zx_ref.at[chunks],
            swap_send, swap_recv.at[group], device_id=partner,
        )

    def swap_decay(group):
        return pltpu.make_async_remote_copy(
            d_ref.at[group], dx_decay.at[group],
            decay_send, swap_recv.at[GROUPS + group], device_id=partner,
        )

    for fetch in fetches[2:]:
        fetch.wait()

    @pl.loop(0, GROUPS)
    def _(group):
        states_of(group)

        @pl.when(group == 0)
        def _():
            pl.semaphore_wait(barrier, CHUNKS)

        swap_decay(group).start()
        swap(group).start()

    @pl.loop(0, GROUPS)
    def _(group):
        swap_decay(group).wait_recv()
        dc_ref[group] = d_ref[group] * dx_decay[group]
        swap(group).wait_recv()

    def out_copy(m, slot):
        return pltpu.make_async_remote_copy(
            t_ref.at[m], rec_ref.at[slot], out_send, cast_recv.at[half + slot], device_id=peer(m)
        )

    def back_copy(n, slot):
        return pltpu.make_async_remote_copy(
            q_ref.at[n], p_ref.at[slot], back_send, back_recv.at[slot], device_id=peer(n)
        )

    def end_copy(m):
        return pltpu.make_async_remote_copy(
            y_ref.at[m], st_ref.at[core, m], end_send, end_recv.at[m // 8], device_id=partner
        )

    def end_wait(group):
        chunks = pl.ds(group * 8, 8)
        pltpu.make_async_remote_copy(
            y_ref.at[chunks], st_ref.at[other, chunks], end_send, end_recv.at[group],
            device_id=partner,
        ).wait_recv()

    def chip_total(m, group, target):
        for j in range(PAIRS):
            rows = slice(8 * j, 8 * j + 8)
            target[rows, :] = (
                dx_decay[group, j : j + 1, :] * z_ref[core, m, rows, :] + zx_ref[m, rows, :]
            )
        target[40:48, :] = dc_ref[group]

    for depth, m in far_first:
        chip_total(m, depth, t_ref.at[m])
        out_copy(m, chip).start()

    chip_total(chip, depths[0], rec_ref.at[chip])

    @pl.loop(0, GROUPS // 2)
    def _(group):
        near_terms(group)

    def step(i, carry):
        n = core * (CHIPS - 1) + (1 - 2 * core) * i

        @pl.when(n != chip)
        def _():
            out_copy(n, n).wait_recv()

        after = []
        for j in range(PAIRS):
            rows = slice(8 * j, 8 * j + 8)
            q_ref[n, rows, :] = carry[j]
            after.append(rec_ref[n, 40 + j : 41 + j, :] * carry[j] + rec_ref[n, rows, :])

        @pl.when(n != chip)
        def _():
            back_copy(n, chip).start()

        return tuple(after)

    lax.fori_loop(0, CHIPS, step, tuple(jnp.zeros((8, 128), F32) for _ in range(PAIRS)))

    @pl.loop(GROUPS // 2, GROUPS)
    def _(group):
        near_terms(group)

    def finish(m, source):
        group = m // 8
        st_ref[core, m] = source[...]
        for j in range(PAIRS):
            rows = slice(8 * j, 8 * j + 8)
            y_ref[m, rows, :] = (
                d_ref[group, j : j + 1, :] * source[rows, :] + z_ref[core, m, rows, :]
            )
        end_copy(m).start()

    finish(chip, q_ref.at[chip])

    @pl.loop(1, CHIPS)
    def _(o):
        m = turn(o)
        back_copy(m, m).wait_recv()
        finish(m, p_ref.at[m])

    def give(w_ref, part):
        at = pl.ds(part * BATCH, BATCH)
        return pltpu.make_async_remote_copy(
            w_ref.at[at], wx_ref.at[at], give_send, give_recv.at[part], device_id=partner
        )

    def cast(c, slot, target):
        return pltpu.make_async_remote_copy(
            wt_ref.at[c], wr_ref.at[slot], cast_send, cast_recv.at[slot], device_id=target
        )

    def ship(w_ref, part):
        give(w_ref, part).wait_recv()
        batch = pl.ds(part * BATCH, BATCH)
        wt_ref[batch] = w_ref[batch] + wx_ref[batch]
        for i in range(BATCH):
            inner = lax.rem(mine + 1 + i, BATCH)
            target = {"seq": ((part % 2) * BATCH + inner) * 2 + core, "dp": part // 2}
            copy = cast(part * BATCH + inner, mine, target)
            if i < BATCH - 1:
                copy.start()
            else:
                pl.when(part != mine // BATCH)(copy.start)

    def rotated(i):
        return lax.rem(mine // BATCH + 1 + i, GROUPS)

    @pl.loop(0, GROUPS)
    def _(i):
        group = rotated(i)

        end_wait(group)
        far_terms(group)

        @pl.when(core == 0)
        def _():
            give(wb_ref, group).start()

        @pl.when((core == 1) & (i > 0))
        def _():
            ship(wb_ref, rotated(i - 1))

    smooth = smooth_ref[...]
    project = (acc_ref[...] * (1.0 - smooth * smooth)).astype(BF16)

    @pl.loop(0, GROUPS)
    def _(i):
        group = rotated(i)
        wide = pl.ds(pl.multiple_of(group * WIDTH, 128), WIDTH)
        wa_ref[pl.ds(group * BATCH, BATCH), :40, :] = dot(x_ref[:, wide], project, TN).reshape(
            BATCH, 40, 128
        )

        @pl.when(core == 1)
        def _():
            give(wa_ref, group).start()

    @pl.when(core == 1)
    def _():
        ship(wb_ref, rotated(GROUPS - 1))

    @pl.when(core == 0)
    def _():
        @pl.loop(0, GROUPS)
        def _(i):
            ship(wa_ref, rotated(i))

    @pl.loop(0, GROUPS)
    def _(group):
        wide = pl.ds(pl.multiple_of(group * WIDTH, 128), WIDTH)
        dx_ref[:, wide] = dot(project, a_ref[wide, :], NT).astype(BF16)
        outputs_of(group)

    def share(n):
        return pltpu.make_async_remote_copy(
            ws_ref, red_ref.at[core, chip], share_send, back_recv.at[chip], device_id=peer(n)
        )

    def share_wait(n):
        pltpu.make_async_remote_copy(
            ws_ref, red_ref.at[core, n], share_send, back_recv.at[n], device_id=peer(n)
        ).wait_recv()

    def last(n):
        return pltpu.make_async_remote_copy(
            red_ref.at[core, n], red_ref.at[core, n], last_send, last_recv, device_id=partner
        )

    def add(o, total):
        c = wide_turn(o)
        cast(c, c, partner).wait_recv()
        return total + wr_ref[c]

    ws_ref[...] = lax.fori_loop(1, CHUNKS, add, wt_ref[mine])

    for _, m in far_first:
        share(m).start()

    red_ref[core, chip] = ws_ref[...]
    last(chip).start()

    @pl.loop(1, CHIPS)
    def _(o):
        n = turn(o)
        share_wait(n)
        last(n).start()

    def sent(ref, sem):
        pltpu.make_async_remote_copy(ref, ref, sem, last_recv, device_id=partner).wait_send()

    sent(z_ref.at[other], swap_send)
    sent(d_ref, decay_send)
    sent(t_ref.at[pl.ds(0, CHIPS - 1)], out_send)
    sent(q_ref.at[pl.ds(0, CHIPS - 1)], back_send)
    sent(y_ref, end_send)
    sent(wb_ref, give_send)
    sent(wt_ref.at[pl.ds(0, CHUNKS - 1)], cast_send)
    sent(red_ref.at[core, pl.ds(0, CHIPS - 1)], share_send)
    sent(red_ref.at[core], last_send)
    pltpu.make_async_remote_copy(
        red_ref.at[other], red_ref.at[other], last_send, last_recv, device_id=partner
    ).wait_recv()


def summed_over(x, ones):
    total = None
    for piece in split(x, 2):
        term = dot(piece, ones, NN)
        total = term if total is None else total + term
    return total


def whole_stage(x, a, r, k, v, g, b, speed, reward):
    vmem = pl.BlockSpec(memory_space=pltpu.VMEM)
    channels = x.shape[1]
    full = jax.ShapeDtypeStruct((TOK, channels), BF16)
    wide = pltpu.VMEM((TOK, channels), F32)
    short = pltpu.VMEM((TOK, channels), BF16)
    half = pltpu.VMEM((HALF, channels), F32)
    low = pltpu.VMEM((HALF, channels), BF16)
    matrix = pltpu.VMEM((channels, 128), BF16)
    vector = pltpu.VMEM((channels,), F32)
    square = pltpu.VMEM((TOK, 128), F32)
    state = pltpu.VMEM((32, 40, 128), F32)
    states = pltpu.VMEM((2, 32, 40, 128), F32)
    message = pltpu.VMEM((32, 48, 128), F32)
    decay = pltpu.VMEM((GROUPS, 8, 128), F32)
    sums = pltpu.VMEM((CHUNKS, 48, 128), F32)
    sems = pltpu.SemaphoreType.DMA
    speed, reward = (pltpu.with_memory_space_constraint(t, pltpu.HBM) for t in (speed, reward))
    x, a, r, k, v, g, b = (
        pltpu.with_memory_space_constraint(t, pltpu.HBM) for t in (x, a, r, k, v, g, b)
    )
    return pl.pallas_call(
        whole_kernel,
        in_specs=[pl.BlockSpec(memory_space=pltpu.HBM)] * 9,
        out_specs=[vmem] * 6,
        out_shape=[full] * 5 + [jax.ShapeDtypeStruct((2, CHIPS, 48, 128), F32)],
        scratch_shapes=[short, matrix, short, short, short, short, matrix, vector, vector, sems((9,))]
        + [low] * 4
        + [square, pltpu.VMEM((TOK, 128), BF16)]
        + [wide] * 4
        + [short] * 2
        + [half, half, pltpu.VMEM((8, channels), F32)]
        + [wide] * 6
        + [square]
        + [states, decay, state, decay, decay, message, message, state, state, state, states]
        + [sums] * 5
        + [pltpu.VMEM((48, 128), F32)]
        + [sems(())] * 10
        + [sems((2 * GROUPS,)), sems((CHIPS,)), sems((GROUPS,)), sems((GROUPS,)), sems((CHUNKS,))],
        compiler_params=pltpu.CompilerParams(
            collective_id=0, has_side_effects=True, vmem_limit_bytes=50 * 1024 * 1024
        ),
        name="whole_stage",
    )(x, a, r, k, v, g, b, speed, reward)


def emit_kernel(*refs):
    sources, red_hbm = refs[:5], refs[5]
    targets, weights = refs[6:11], refs[11:13]
    time_ref, bonus_ref, red_ref, red_sem, sem = refs[13:]
    fetches = [
        pltpu.make_async_copy(red_hbm.at[i], red_ref.at[i], red_sem.at[i]) for i in range(2)
    ]
    copies = [
        pltpu.make_async_copy(source, target, sem.at[i])
        for i, (source, target) in enumerate(zip(sources, targets))
    ]
    for copy in fetches + copies:
        copy.start()
    for i, (fetch, target) in enumerate(zip(fetches, weights)):
        fetch.wait()
        copies.append(
            pltpu.make_async_copy(red_ref.at[i, :, pl.ds(0, 40)], target, sem.at[5 + i])
        )
        copies[-1].start()
    for i in range(10):
        time_ref[pl.ds(128 * i, 128)] = red_ref[0, i, 40:41, :].reshape(128)
        bonus_ref[pl.ds(128 * i, 128)] = red_ref[1, i, 40:41, :].reshape(128)
    for copy in copies:
        copy.wait()


def emit_stage(mixed, dr, dk, dv, dx, red):
    vmem = pl.BlockSpec(memory_space=pltpu.VMEM)
    hbm = pl.BlockSpec(memory_space=pltpu.HBM)
    full = jax.ShapeDtypeStruct(mixed.shape, BF16)
    red = pltpu.with_memory_space_constraint(red, pltpu.HBM)
    return pl.pallas_call(
        emit_kernel,
        in_specs=[vmem] * 5 + [hbm],
        out_specs=[hbm] * 7 + [vmem] * 2,
        out_shape=[full] * 5
        + [jax.ShapeDtypeStruct((CHIPS, 40, 128), F32)] * 2
        + [jax.ShapeDtypeStruct((1280,), F32)] * 2,
        scratch_shapes=[
            pltpu.VMEM(red.shape, F32),
            pltpu.SemaphoreType.DMA((2,)),
            pltpu.SemaphoreType.DMA((7,)),
        ],
        compiler_params=pltpu.CompilerParams(vmem_limit_bytes=8 * 1024 * 1024),
        name="emit_stage",
    )(mixed, dr, dk, dv, dx, red)


def per_device(r, k, v, x, g, lowering, raising, speed, reward):
    r, k, v, x, g = (t[0] for t in (r, k, v, x, g))
    outs = emit_stage(*whole_stage(x, lowering, r, k, v, g, raising, speed, reward))
    lora = tuple(t.reshape(1280, 128) for t in outs[5:7])
    return tuple(t[None] for t in outs[:5]) + lora + tuple(outs[7:])


def solution(mesh):
    tokens = P("dp", "seq", None)
    return jax.shard_map(
        per_device,
        mesh=mesh,
        in_specs=(tokens,) * 5 + (P(),) * 4,
        out_specs=(tokens,) * 5 + (P("dp", None),) * 2 + (P("dp"),) * 2,
        check_vma=False,
    )
```

```python
import jax
import jax.numpy as jnp
from jax import lax
from jax.experimental import pallas as pl
from jax.experimental.pallas import tpu as pltpu
from jax.sharding import PartitionSpec as P

F32 = jnp.float32
BF16 = jnp.bfloat16
TOK = 128
HALF = 64
GROUPS = 4
PAIRS = 5
WIDTH = PAIRS * 128
CHIPS = 32
CHUNKS = 2 * CHIPS
BATCH = CHUNKS // GROUPS
HOPS = (0, 1, 2, 1)
OFFSETS = sorted(
    ((y, x, z) for y in range(4) for x in range(2) for z in range(4) if y + x + z > 0),
    key=lambda step: -(HOPS[step[0]] + 2 * step[1] + HOPS[step[2]]),
)
NN = (((1,), (0,)), ((), ()))
NT = (((1,), (1,)), ((), ()))
TN = (((0,), (0,)), ((), ()))


def dot(a, b, dims):
    return lax.dot_general(a, b, dims, preferred_element_type=F32)


def split(x, parts):
    pieces = []
    for _ in range(parts - 1):
        head = x.astype(BF16)
        pieces.append(head)
        x = x - head.astype(F32)
    pieces.append(x.astype(BF16))
    return pieces


def summed_by(matrix, x, parts):
    total = None
    for piece in split(x, parts):
        term = dot(matrix, piece, NN)
        total = term if total is None else total + term
    return total


def grids():
    row = lax.broadcasted_iota(jnp.int32, (TOK, TOK), 0)
    col = lax.broadcasted_iota(jnp.int32, (TOK, TOK), 1)
    same = (row < HALF) == (col < HALF)
    return row, col, same


def as_matrix(condition):
    return jnp.where(condition, 1.0, 0.0).astype(BF16)


def decay_sums(gate, raising, speed, lower):
    rank = dot(gate, raising, NT)
    log_decay = -speed * jnp.exp(rank)
    inclusive = summed_by(lower, log_decay, 3)
    return (
        log_decay,
        inclusive,
        inclusive - log_decay,
        inclusive[HALF - 1 : HALF],
        inclusive[TOK - 1 : TOK],
    )


def both(lhs, first, last, dims):
    return jnp.concatenate([dot(lhs[:HALF], first, dims), dot(lhs[HALF:], last, dims)], axis=0)


def twofold(pieces, high, low):
    return dot(pieces[0], high, NN) + dot(pieces[1], high, NN) + dot(pieces[0], low, NN)


def packed(product, left):
    return jnp.where(left[:HALF], product[:HALF], product[HALF:])


def spread(state, left):
    zero = jnp.zeros_like(state)
    return jnp.concatenate(
        [jnp.where(left[:HALF], state, zero), jnp.where(left[:HALF], zero, state)], axis=0
    )


def whole_kernel(
    x_hbm, a_hbm, r_hbm, k_hbm, v_hbm, g_hbm, b_hbm, speed_hbm, reward_hbm,
    mixed_ref, dr_ref, dk_ref, dv_ref, dx_ref, red_ref,
    x_ref, a_ref, r_ref, k_ref, v_ref, g_ref, b_ref, speed_ref, reward_ref, fetch_sem,
    s0_ref, s1_ref, e0_ref, e1_ref,
    smooth_ref, gate_ref, log_ref, sum_ref, enter_ref, leave_ref, reached_ref, faded_ref,
    own_ref, pull_ref, ends_ref,
    mixed_near, dv_near, dr_near, dk_near, read_near, change_near, acc_ref,
    z_ref, d_ref, zx_ref, dx_decay, dc_ref, t_ref, rec_ref, q_ref, p_ref, y_ref, st_ref,
    wa_ref, wb_ref, wx_ref, wt_ref, wr_ref, ws_ref,
    swap_send, decay_send, out_send, back_send, end_send, give_send, cast_send, share_send,
    last_send, last_recv, swap_recv, back_recv, end_recv, give_recv, cast_recv,
):
    seq = lax.axis_index("seq")
    chip, core = seq // 2, seq % 2
    other = 1 - core
    half = lax.axis_index("dp") * CHIPS
    mine = half + chip
    partner = {"seq": chip * 2 + other}

    def peer(m):
        return {"seq": m * 2 + core}

    def turn(o):
        return lax.rem(chip + o, CHIPS)

    def wide_turn(o):
        return lax.rem(mine + o, CHUNKS)

    fetches = [
        pltpu.make_async_copy(source, target, fetch_sem.at[i])
        for i, (source, target) in enumerate(
            (
                (x_hbm, x_ref),
                (a_hbm, a_ref),
                (b_hbm, b_ref),
                (speed_hbm, speed_ref),
                (k_hbm, k_ref),
                (r_hbm, r_ref),
                (v_hbm, v_ref),
                (g_hbm, g_ref),
                (reward_hbm, reward_ref),
            )
        )
    ]
    for fetch in fetches:
        fetch.start()

    barrier = pltpu.get_barrier_semaphore()
    pl.semaphore_signal(barrier, inc=1, device_id=partner)

    depths = [lax.rem(chip // 8 + d, 4) for d in range(4)]
    sides = [lax.rem(chip // 4 + d, 2) for d in range(2)]
    levels = [lax.rem(chip + d, 4) for d in range(4)]
    far_first = [(depths[y], (depths[y] * 2 + sides[x]) * 4 + levels[z]) for y, x, z in OFFSETS]

    for replica in (1 - lax.axis_index("dp"), lax.axis_index("dp")):
        for _, m in far_first:
            pl.semaphore_signal(
                barrier, inc=1, device_id={"seq": m * 2 + core, "dp": replica}
            )
    pl.semaphore_signal(
        barrier, inc=1, device_id={"dp": 1 - lax.axis_index("dp")}
    )

    row, col, same = grids()
    lower = as_matrix(same & (row >= col))
    ones = as_matrix((row < HALF) == (col < HALF))
    left = col < HALF
    early = row < HALF
    around = jnp.where(
        same & ~early & (col < row), 1.0, jnp.where(same & early & (col >= row), -1.0, 0.0)
    ).astype(BF16)

    fetches[0].wait()
    fetches[1].wait()
    smooth = jnp.tanh(dot(x_ref[...], a_ref[...], NN))
    smooth_ref[...] = smooth
    gate_ref[...] = smooth.astype(BF16)
    acc_ref[...] = jnp.zeros_like(acc_ref)
    wa_ref[:, 40:, :] = jnp.zeros((CHUNKS, 8, 128), F32)
    wb_ref[:, 40:, :] = jnp.zeros((CHUNKS, 8, 128), F32)

    def lanes(group, pair):
        return pl.ds(pl.multiple_of(group * WIDTH + pair * 128, 128), 128)

    def vector(ref, group, pair):
        return ref[lanes(group, pair)].reshape(1, 128)

    def by_head(x):
        zero = jnp.zeros_like(x)
        return jnp.concatenate([jnp.where(left, x, zero), jnp.where(left, zero, x)], axis=0)

    def outputs_of(group):
        for pair in range(PAIRS):
            at = lanes(group, pair)
            s0, s1, e0, e1 = (
                spread(ref[:, at], left) for ref in (s0_ref, s1_ref, e0_ref, e1_ref)
            )
            mixed_ref[:, at] = (
                mixed_near[:, at] + both(reached_ref[:, at], s0, s1, NT)
            ).astype(BF16)
            dv_ref[:, at] = (dv_near[:, at] + both(faded_ref[:, at], e0, e1, NT)).astype(BF16)

    def group_lanes(group):
        return pl.ds(pl.multiple_of(group * WIDTH, 128), WIDTH)

    def pair_lanes(pair):
        return slice(pair * 128, pair * 128 + 128)

    def states_of(group):
        wide = group_lanes(group)
        early_wide = lax.broadcasted_iota(jnp.int32, (TOK, WIDTH), 0) < HALF
        log_decay, inclusive, exclusive, total0, total1 = decay_sums(
            gate_ref[...], b_ref[wide, :], speed_ref[wide].reshape(1, WIDTH), lower
        )
        log_ref[:, wide] = log_decay
        sum_ref[:, wide] = inclusive
        entering = jnp.exp(exclusive)
        leaving = jnp.exp(jnp.where(early_wide, total0, total1) - inclusive)
        enter_ref[:, wide] = entering
        leave_ref[:, wide] = leaving
        reached = (r_ref[:, wide].astype(F32) * entering).astype(BF16)
        faded = (k_ref[:, wide].astype(F32) * leaving).astype(BF16)
        reached_ref[:, wide] = reached
        faded_ref[:, wide] = faded
        end0, end1 = jnp.exp(total0), jnp.exp(total1)
        ends_ref[0:1, wide] = end0
        ends_ref[1:2, wide] = end1
        decay = jnp.exp(total0 + total1)
        chunks = pl.ds(group * 8, 8)
        for pair in range(PAIRS):
            at = pair_lanes(pair)
            here = lanes(group, pair)
            v16, g16 = v_ref[:, here], g_ref[:, here]
            own0 = packed(dot(v16[:HALF], faded[:HALF, at], TN), left)
            own1 = packed(dot(v16[HALF:], faded[HALF:, at], TN), left)
            pull0 = packed(dot(g16[:HALF], reached[:HALF, at], TN), left)
            pull1 = packed(dot(g16[HALF:], reached[HALF:, at], TN), left)
            own_ref[:, here] = own0
            pull_ref[:, here] = pull1
            rows = slice(pair * 8, pair * 8 + 8)
            z_ref[0, chunks, rows, :] = (end1[:, at] * own0 + own1).reshape(8, 8, 128)
            z_ref[1, chunks, rows, :] = (end0[:, at] * pull1 + pull0).reshape(8, 8, 128)
            d_ref[group, pair : pair + 1, :] = decay[:, at]
        d_ref[group, PAIRS:, :] = jnp.zeros((8 - PAIRS, 128), F32)

    def near_terms(group):
        wide_row = lax.broadcasted_iota(jnp.int32, (TOK, 2 * TOK), 0)
        wide_col = lax.broadcasted_iota(jnp.int32, (TOK, 2 * TOK), 1) % TOK
        wide_same = (wide_row < HALF) == (wide_col < HALF)
        beneath = wide_same & (wide_row > wide_col)
        above = wide_same & (wide_row < wide_col)
        zero = jnp.zeros((), F32)
        for pair in range(PAIRS):
            at = lanes(group, pair)
            inclusive = sum_ref[:, at]
            middle = jnp.where(
                early,
                inclusive[HALF // 2 - 1 : HALF // 2],
                inclusive[HALF + HALF // 2 - 1 : HALF + HALF // 2],
            )
            upward = jnp.exp(inclusive - log_ref[:, at] - middle)
            downward = jnp.exp(middle - inclusive)
            v16, g16 = v_ref[:, at], g_ref[:, at]
            r, k, v, g = (t[:, at].astype(F32) for t in (r_ref, k_ref, v_ref, g_ref))
            reward = vector(reward_ref, group, pair)
            up, up_low = split(r * upward, 2)
            down, down_low = split(k * downward, 2)
            v2, g2, up2, down2 = by_head(v16), by_head(g16), by_head(up), by_head(down)
            scores = jnp.where(beneath, dot(up, down2, NT), zero).astype(BF16)
            scores_t = jnp.where(above, dot(down, up2, NT), zero).astype(BF16)
            products = split(jnp.where(beneath, dot(g16, v2, NT), zero), 2)
            products_t = split(jnp.where(above, dot(v16, g2, NT), zero), 2)
            present = summed_over(r * reward * k, ones)
            agreement = summed_over(v * g, ones)
            mixed_near[:, at] = dot(scores, v2, NN) + present * v
            dv_near[:, at] = dot(scores_t, g2, NN) + present * g
            near_past = twofold(products, down2, by_head(down_low))
            near_later = twofold(products_t, up2, by_head(up_low))
            dr_near[:, at] = upward * near_past + reward * k * agreement
            dk_near[:, at] = downward * near_later + reward * r * agreement
            read = (up.astype(F32) + up_low.astype(F32)) * near_past
            read_near[:, at] = read
            change_near[:, at] = (
                down.astype(F32) + down_low.astype(F32)
            ) * near_later - read
            chunk = CHIPS * (group // 2) + PAIRS * (group % 2) + pair
            wb_ref[chunk, 40:41, :] = jnp.sum(r * k * agreement, axis=0, keepdims=True)

    def far_terms(group):
        wide = group_lanes(group)
        chunks = pl.ds(group * 8, 8)
        starts, ends = [], []
        for pair in range(PAIRS):
            rows = slice(pair * 8, pair * 8 + 8)
            starts.append(st_ref[0, chunks, rows, :].reshape(HALF, 128))
            ends.append(st_ref[1, chunks, rows, :].reshape(HALF, 128))
        start0, end1 = jnp.concatenate(starts, axis=1), jnp.concatenate(ends, axis=1)
        start1 = ends_ref[0:1, wide] * start0 + own_ref[:, wide]
        end0 = ends_ref[1:2, wide] * end1 + pull_ref[:, wide]
        lows = [t.astype(BF16) for t in (start0, start1, end0, end1)]
        for low_ref, low in zip((s0_ref, s1_ref, e0_ref, e1_ref), lows):
            low_ref[:, wide] = low
        pasts, laters = [], []
        for pair in range(PAIRS):
            at = pair_lanes(pair)
            here = lanes(group, pair)
            s0, s1, e0, e1 = (spread(t[:, at], left) for t in lows)
            pasts.append(both(g_ref[:, here], s0, s1, NN))
            laters.append(both(v_ref[:, here], e0, e1, NN))
        past, later = jnp.concatenate(pasts, axis=1), jnp.concatenate(laters, axis=1)
        far_read = reached_ref[:, wide].astype(F32) * past
        change = change_near[:, wide] + (faded_ref[:, wide].astype(F32) * later - far_read)
        total = summed_by(around, change, 2)
        dr_ref[:, wide] = (dr_near[:, wide] + enter_ref[:, wide] * past).astype(BF16)
        dk_ref[:, wide] = (dk_near[:, wide] + leave_ref[:, wide] * later).astype(BF16)
        coupling = jnp.where(
            lax.broadcasted_iota(jnp.int32, (TOK, WIDTH), 0) < HALF,
            jnp.sum(lows[2].astype(F32) * start1, axis=0, keepdims=True),
            jnp.sum(end0 * lows[1].astype(F32), axis=0, keepdims=True),
        )
        slope = (coupling + total - (read_near[:, wide] + far_read)) * log_ref[:, wide]
        slopes = slope.astype(BF16)
        acc_ref[...] += dot(slopes, b_ref[wide, :], NN)
        wb_ref[pl.ds(group * BATCH, BATCH), :40, :] = dot(slopes, gate_ref[...], TN).reshape(
            BATCH, 40, 128
        )
        slope_sum = jnp.sum(slope, axis=0, keepdims=True)
        chunk = CHIPS * (group // 2) + PAIRS * (group % 2)
        for pair in range(PAIRS):
            wa_ref[chunk + pair, 40:41, :] = slope_sum[:, pair_lanes(pair)]

    def swap(group):
        chunks = pl.ds(group * 8, 8)
        return pltpu.make_async_remote_copy(
            z_ref.at[other, chunks], zx_ref.at[chunks],
            swap_send, swap_recv.at[group], device_id=partner,
        )

    def swap_decay(group):
        return pltpu.make_async_remote_copy(
            d_ref.at[group], dx_decay.at[group],
            decay_send, swap_recv.at[GROUPS + group], device_id=partner,
        )

    for fetch in fetches[2:]:
        fetch.wait()

    @pl.loop(0, GROUPS)
    def _(group):
        states_of(group)

        @pl.when(group == 2)
        def _():
            pl.semaphore_wait(barrier, CHUNKS)
            for earlier in range(2):
                swap_decay(earlier).start()
                swap(earlier).start()

        @pl.when(group >= 2)
        def _():
            swap_decay(group).start()
            swap(group).start()

    @pl.loop(0, GROUPS)
    def _(group):
        swap_decay(group).wait_recv()
        dc_ref[group] = d_ref[group] * dx_decay[group]
        swap(group).wait_recv()

    def out_copy(m, slot):
        return pltpu.make_async_remote_copy(
            t_ref.at[m], rec_ref.at[slot], out_send, cast_recv.at[half + slot], device_id=peer(m)
        )

    def back_copy(n, slot):
        return pltpu.make_async_remote_copy(
            q_ref.at[n], p_ref.at[slot], back_send, back_recv.at[slot], device_id=peer(n)
        )

    def end_copy(m):
        return pltpu.make_async_remote_copy(
            y_ref.at[m], st_ref.at[core, m], end_send, end_recv.at[m // 8], device_id=partner
        )

    def end_wait(group):
        chunks = pl.ds(group * 8, 8)
        pltpu.make_async_remote_copy(
            y_ref.at[chunks], st_ref.at[other, chunks], end_send, end_recv.at[group],
            device_id=partner,
        ).wait_recv()

    def chip_total(m, group, target):
        for j in range(PAIRS):
            rows = slice(8 * j, 8 * j + 8)
            target[rows, :] = (
                dx_decay[group, j : j + 1, :] * z_ref[core, m, rows, :] + zx_ref[m, rows, :]
            )
        target[40:48, :] = dc_ref[group]

    for depth, m in far_first:
        chip_total(m, depth, t_ref.at[m])
        out_copy(m, chip).start()

    chip_total(chip, depths[0], rec_ref.at[chip])

    @pl.loop(0, GROUPS // 2)
    def _(group):
        near_terms(group)

    def step(i, carry):
        n = core * (CHIPS - 1) + (1 - 2 * core) * i

        @pl.when(n != chip)
        def _():
            out_copy(n, n).wait_recv()

        after = []
        for j in range(PAIRS):
            rows = slice(8 * j, 8 * j + 8)
            q_ref[n, rows, :] = carry[j]
            after.append(rec_ref[n, 40 + j : 41 + j, :] * carry[j] + rec_ref[n, rows, :])

        @pl.when(n != chip)
        def _():
            back_copy(n, chip).start()

        return tuple(after)

    lax.fori_loop(0, CHIPS, step, tuple(jnp.zeros((8, 128), F32) for _ in range(PAIRS)))

    @pl.loop(GROUPS // 2, GROUPS)
    def _(group):
        near_terms(group)

    def finish(m, source):
        group = m // 8
        st_ref[core, m] = source[...]
        for j in range(PAIRS):
            rows = slice(8 * j, 8 * j + 8)
            y_ref[m, rows, :] = (
                d_ref[group, j : j + 1, :] * source[rows, :] + z_ref[core, m, rows, :]
            )
        end_copy(m).start()

    finish(chip, q_ref.at[chip])

    @pl.loop(1, CHIPS)
    def _(o):
        m = turn(o)
        back_copy(m, m).wait_recv()
        finish(m, p_ref.at[m])

    def give(w_ref, part):
        at = pl.ds(part * BATCH, BATCH)
        return pltpu.make_async_remote_copy(
            w_ref.at[at], wx_ref.at[at], give_send, give_recv.at[part], device_id=partner
        )

    def cast(c, slot, target):
        return pltpu.make_async_remote_copy(
            wt_ref.at[c], wr_ref.at[slot], cast_send, cast_recv.at[slot], device_id=target
        )

    def ship(w_ref, part):
        give(w_ref, part).wait_recv()
        batch = pl.ds(part * BATCH, BATCH)
        wt_ref[batch] = w_ref[batch] + wx_ref[batch]
        for i in range(BATCH):
            inner = lax.rem(mine + 1 + i, BATCH)
            target = {"seq": ((part % 2) * BATCH + inner) * 2 + core, "dp": part // 2}
            copy = cast(part * BATCH + inner, mine, target)
            if i < BATCH - 1:
                copy.start()
            else:
                pl.when(part != mine // BATCH)(copy.start)

    def rotated(i):
        return lax.rem(mine // BATCH + 1 + i, GROUPS)

    @pl.loop(0, GROUPS)
    def _(i):
        group = rotated(i)

        end_wait(group)
        far_terms(group)

        @pl.when(core == 0)
        def _():
            give(wb_ref, group).start()

        @pl.when((core == 1) & (i > 0))
        def _():
            ship(wb_ref, rotated(i - 1))

    smooth = smooth_ref[...]
    project = (acc_ref[...] * (1.0 - smooth * smooth)).astype(BF16)

    @pl.loop(0, GROUPS)
    def _(i):
        group = rotated(i)
        wide = pl.ds(pl.multiple_of(group * WIDTH, 128), WIDTH)
        wa_ref[pl.ds(group * BATCH, BATCH), :40, :] = dot(x_ref[:, wide], project, TN).reshape(
            BATCH, 40, 128
        )

        @pl.when(core == 1)
        def _():
            give(wa_ref, group).start()

    @pl.when(core == 1)
    def _():
        ship(wb_ref, rotated(GROUPS - 1))

    @pl.when(core == 0)
    def _():
        @pl.loop(0, GROUPS)
        def _(i):
            ship(wa_ref, rotated(i))

    @pl.loop(0, GROUPS)
    def _(group):
        wide = pl.ds(pl.multiple_of(group * WIDTH, 128), WIDTH)
        dx_ref[:, wide] = dot(project, a_ref[wide, :], NT).astype(BF16)
        outputs_of(group)

    def share(n):
        return pltpu.make_async_remote_copy(
            ws_ref, red_ref.at[core, chip], share_send, back_recv.at[chip], device_id=peer(n)
        )

    def share_wait(n):
        pltpu.make_async_remote_copy(
            ws_ref, red_ref.at[core, n], share_send, back_recv.at[n], device_id=peer(n)
        ).wait_recv()

    def last(n):
        return pltpu.make_async_remote_copy(
            red_ref.at[core, n], red_ref.at[core, n], last_send, last_recv, device_id=partner
        )

    def add(o, total):
        c = wide_turn(o)
        cast(c, c, partner).wait_recv()
        return total + wr_ref[c]

    ws_ref[...] = lax.fori_loop(1, CHUNKS, add, wt_ref[mine])

    for _, m in far_first:
        share(m).start()

    red_ref[core, chip] = ws_ref[...]
    last(chip).start()

    @pl.loop(1, CHIPS)
    def _(o):
        n = turn(o)
        share_wait(n)
        last(n).start()

    def sent(ref, sem):
        pltpu.make_async_remote_copy(ref, ref, sem, last_recv, device_id=partner).wait_send()

    sent(z_ref.at[other], swap_send)
    sent(d_ref, decay_send)
    sent(t_ref.at[pl.ds(0, CHIPS - 1)], out_send)
    sent(q_ref.at[pl.ds(0, CHIPS - 1)], back_send)
    sent(y_ref, end_send)
    sent(wb_ref, give_send)
    sent(wt_ref.at[pl.ds(0, CHUNKS - 1)], cast_send)
    sent(red_ref.at[core, pl.ds(0, CHIPS - 1)], share_send)
    sent(red_ref.at[core], last_send)
    pltpu.make_async_remote_copy(
        red_ref.at[other], red_ref.at[other], last_send, last_recv, device_id=partner
    ).wait_recv()


def summed_over(x, ones):
    total = None
    for piece in split(x, 2):
        term = dot(piece, ones, NN)
        total = term if total is None else total + term
    return total


def whole_stage(x, a, r, k, v, g, b, speed, reward):
    vmem = pl.BlockSpec(memory_space=pltpu.VMEM)
    channels = x.shape[1]
    full = jax.ShapeDtypeStruct((TOK, channels), BF16)
    wide = pltpu.VMEM((TOK, channels), F32)
    short = pltpu.VMEM((TOK, channels), BF16)
    half = pltpu.VMEM((HALF, channels), F32)
    low = pltpu.VMEM((HALF, channels), BF16)
    matrix = pltpu.VMEM((channels, 128), BF16)
    vector = pltpu.VMEM((channels,), F32)
    square = pltpu.VMEM((TOK, 128), F32)
    state = pltpu.VMEM((32, 40, 128), F32)
    states = pltpu.VMEM((2, 32, 40, 128), F32)
    message = pltpu.VMEM((32, 48, 128), F32)
    decay = pltpu.VMEM((GROUPS, 8, 128), F32)
    sums = pltpu.VMEM((CHUNKS, 48, 128), F32)
    sems = pltpu.SemaphoreType.DMA
    speed, reward = (pltpu.with_memory_space_constraint(t, pltpu.HBM) for t in (speed, reward))
    x, a, r, k, v, g, b = (
        pltpu.with_memory_space_constraint(t, pltpu.HBM) for t in (x, a, r, k, v, g, b)
    )
    return pl.pallas_call(
        whole_kernel,
        in_specs=[pl.BlockSpec(memory_space=pltpu.HBM)] * 9,
        out_specs=[vmem] * 6,
        out_shape=[full] * 5 + [jax.ShapeDtypeStruct((2, CHIPS, 48, 128), F32)],
        scratch_shapes=[short, matrix, short, short, short, short, matrix, vector, vector, sems((9,))]
        + [low] * 4
        + [square, pltpu.VMEM((TOK, 128), BF16)]
        + [wide] * 4
        + [short] * 2
        + [half, half, pltpu.VMEM((8, channels), F32)]
        + [wide] * 6
        + [square]
        + [states, decay, state, decay, decay, message, message, state, state, state, states]
        + [sums] * 5
        + [pltpu.VMEM((48, 128), F32)]
        + [sems(())] * 10
        + [sems((2 * GROUPS,)), sems((CHIPS,)), sems((GROUPS,)), sems((GROUPS,)), sems((CHUNKS,))],
        compiler_params=pltpu.CompilerParams(
            collective_id=0, has_side_effects=True, vmem_limit_bytes=50 * 1024 * 1024
        ),
        name="whole_stage",
    )(x, a, r, k, v, g, b, speed, reward)


def emit_kernel(*refs):
    sources, red_hbm = refs[:5], refs[5]
    targets, weights = refs[6:11], refs[11:13]
    time_ref, bonus_ref, red_ref, red_sem, sem = refs[13:]
    fetches = [
        pltpu.make_async_copy(red_hbm.at[i], red_ref.at[i], red_sem.at[i]) for i in range(2)
    ]
    copies = [
        pltpu.make_async_copy(source, target, sem.at[i])
        for i, (source, target) in enumerate(zip(sources, targets))
    ]
    for copy in fetches + copies:
        copy.start()
    for i, (fetch, target) in enumerate(zip(fetches, weights)):
        fetch.wait()
        copies.append(
            pltpu.make_async_copy(red_ref.at[i, :, pl.ds(0, 40)], target, sem.at[5 + i])
        )
        copies[-1].start()
    for i in range(10):
        time_ref[pl.ds(128 * i, 128)] = red_ref[0, i, 40:41, :].reshape(128)
        bonus_ref[pl.ds(128 * i, 128)] = red_ref[1, i, 40:41, :].reshape(128)
    for copy in copies:
        copy.wait()


def emit_stage(mixed, dr, dk, dv, dx, red):
    vmem = pl.BlockSpec(memory_space=pltpu.VMEM)
    hbm = pl.BlockSpec(memory_space=pltpu.HBM)
    full = jax.ShapeDtypeStruct(mixed.shape, BF16)
    red = pltpu.with_memory_space_constraint(red, pltpu.HBM)
    return pl.pallas_call(
        emit_kernel,
        in_specs=[vmem] * 5 + [hbm],
        out_specs=[hbm] * 7 + [vmem] * 2,
        out_shape=[full] * 5
        + [jax.ShapeDtypeStruct((CHIPS, 40, 128), F32)] * 2
        + [jax.ShapeDtypeStruct((1280,), F32)] * 2,
        scratch_shapes=[
            pltpu.VMEM(red.shape, F32),
            pltpu.SemaphoreType.DMA((2,)),
            pltpu.SemaphoreType.DMA((7,)),
        ],
        compiler_params=pltpu.CompilerParams(vmem_limit_bytes=8 * 1024 * 1024),
        name="emit_stage",
    )(mixed, dr, dk, dv, dx, red)


def per_device(r, k, v, x, g, lowering, raising, speed, reward):
    r, k, v, x, g = (t[0] for t in (r, k, v, x, g))
    outs = emit_stage(*whole_stage(x, lowering, r, k, v, g, raising, speed, reward))
    lora = tuple(t.reshape(1280, 128) for t in outs[5:7])
    return tuple(t[None] for t in outs[:5]) + lora + tuple(outs[7:])


def solution(mesh):
    tokens = P("dp", "seq", None)
    return jax.shard_map(
        per_device,
        mesh=mesh,
        in_specs=(tokens,) * 5 + (P(),) * 4,
        out_specs=(tokens,) * 5 + (P("dp", None),) * 2 + (P("dp"),) * 2,
        check_vma=False,
    )
```
